32 devices in a mesh: band: 2 (over core), page: 16 (over z, y, x).
Axes of the slice: x: 2, y: 2, z: 4, core: 2. Of those that a mesh axis runs over, the one named last changes fastest.
Arguments:
- hidden: bfloat16 [48, 576, 768], P('page', 'band'), may hold values from -6 to 6
- cotangent: bfloat16 [48, 576, 768], P('page', 'band'), may hold values from -6 to 6
- page_lengths: int32 [48], P('page'), may hold values from 263 to 527, as said below
- x_coord: int32 [48, 576], P('page'), may hold values from 0 to 999
- line_ids: int32 [48, 576], P('page'), may hold values from 0 to 63, never falling along the last dimension, each value on 1 to 24 neighbouring positions
- qkv_w: bfloat16 [768, 2304], replicated, may hold values from -0.21875 to 0.21875
- q_bias: bfloat16 [768], replicated, may hold values from -3 to 3
- v_bias: bfloat16 [768], replicated, may hold values from -3 to 3
- rel_table: bfloat16 [32, 12], replicated, may hold values from -4 to 4
- x_table: bfloat16 [64, 12], replicated, may hold values from -4 to 4
- y_table: bfloat16 [64, 12], replicated, may hold values from -4 to 4
- out_w: bfloat16 [768, 768], replicated, may hold values from -0.875 to 0.875
- out_b: bfloat16 [768], replicated, may hold values from -1.75 to 1.75
- ln1_gain: bfloat16 [768], replicated, may hold values from 0.5 to 1.5
- ln1_bias: bfloat16 [768], replicated, may hold values from -1.75 to 1.75
- ffn_in_w: bfloat16 [768, 3072], replicated, may hold values from -0.21875 to 0.21875
- ffn_in_b: bfloat16 [3072], replicated, may hold values from -1.75 to 1.75
- ffn_out_w: bfloat16 [3072, 768], replicated, may hold values from -0.109375 to 0.109375
- ffn_out_b: bfloat16 [768], replicated, may hold values from -1.75 to 1.75
- ln2_gain: bfloat16 [768], replicated, may hold values from 0.5 to 1.5
- ln2_bias: bfloat16 [768], replicated, may hold values from -1.75 to 1.75
Outputs:
- output: bfloat16 [48, 576, 768], P('page', 'band')
- grad_hidden: float32 [48, 576, 768], P('page', 'band')
- grad_qkv_w: float32 [768, 2304], replicated
- grad_q_bias: float32 [768], replicated
- grad_v_bias: float32 [768], replicated
- grad_rel_table: float32 [32, 12], replicated
- grad_x_table: float32 [64, 12], replicated
- grad_y_table: float32 [64, 12], replicated
- grad_out_w: float32 [768, 768], replicated
- grad_out_b: float32 [768], replicated
- grad_ln1_gain: float32 [768], replicated
- grad_ln1_bias: float32 [768], replicated
- grad_ffn_in_w: float32 [768, 3072], P(None, ('band', 'page'))
- grad_ffn_in_b: float32 [3072], replicated
- grad_ffn_out_w: float32 [3072, 768], P(('band', 'page'))
- grad_ffn_out_b: float32 [768], replicated
- grad_ln2_gain: float32 [768], replicated
- grad_ln2_bias: float32 [768], replicated
The draws below stay inside these ranges and needn't reach their ends.
Inputs may be any that keep to these rules, and one draw needn't show every extreme that they name: `page_lengths`: positions from 49 plus a page's length on are padding. Of the 3 pages held by each position of the `page` axis, one holds 527 text tokens. `line_ids`: along a page the line numbers never fall; a line holds 1 to 24 positions.
All inputs are finite; a program needn't handle non-finite values.
Results may differ from the reference program's by a relative error of at most 0.014.
Values may be sent and summed in bfloat16 or wider, within the bound.
No kernel may reach another device: no remote copies, remote signals or barrier semaphores. Data moves between devices by JAX's collectives and lax.ppermute only.
A program may use at most 256 MiB of HBM per device.

```python
import math
import jax
import jax.numpy as jnp
import numpy as np
from jax import lax

D = 768
HEADS = 12
HEAD_DIM = 64
FF = 3072
REL_BUCKETS = 32
REL_REACH = 128
XY_BUCKETS = 64
XY_REACH = 256
VIS_SIDE = 7
VIS = 49
SEQ = 576
TEXT = 527
HALF = 64
LINES = 64
LINE_MOST = 24
PAGES_DEV = 3
PAGES = 48


def draw_page_lengths(key, part):
    key_lengths, key_full, key_short = jax.random.split(key, 3)
    group_count = PAGES // PAGES_DEV
    lengths = jax.random.randint(key_lengths, (PAGES,), TEXT // 2, TEXT + 1, dtype=jnp.int32)
    chosen = jax.random.randint(key_full, (group_count,), 0, PAGES_DEV, dtype=jnp.int32)
    page_index = jnp.arange(PAGES, dtype=jnp.int32)
    is_full = page_index % PAGES_DEV == jnp.repeat(chosen, PAGES_DEV)
    shortest = jax.random.randint(key_short, (), 0, PAGES, dtype=jnp.int32)
    lengths = jnp.where((page_index == shortest) & jnp.logical_not(is_full), TEXT // 2, lengths)
    return jnp.where(is_full, TEXT, lengths).astype(jnp.int32)


def place_ends(array, stream_key, least, high):
    extent = array.shape
    spot = [jax.random.randint(jax.random.fold_in(stream_key, axis), (), 0, extent[axis]) for axis in range(len(extent))]
    array = array.at[tuple(spot)].set(least)
    longest = extent.index(max(extent))
    spot[longest] = (spot[longest] + 1) % extent[longest]
    return array.at[tuple(spot)].set(high)


def level_of(own_key, dims, cuts, least, largest):
    def one(dim, parts):
        heights = jax.random.uniform(jax.random.fold_in(jax.random.fold_in(own_key, 6), dim), (parts,), jnp.float32, least / len(cuts), largest / len(cuts))
        return jnp.repeat(jnp.exp(heights), dims[dim] // parts).reshape((-1,) + (1,) * (len(dims) - dim - 1))

    gain = one(*cuts[0])
    for cut in cuts[1:]:
        gain = gain * one(*cut)
    return gain


def profile(number_of, total, reach, lean):
    loads = [(1 << 20) // math.isqrt(standing ** lean) + 1 for standing in range(2, number_of + 1)]
    surplus, counts = total - reach - (number_of - 1), [1] * (number_of - 1)
    while surplus > 0:
        candidates = [i for i in range(number_of - 1) if counts[i] < reach]
        pool, remaining = sum([loads[i] for i in candidates]), surplus
        for i in candidates:
            addition = min(reach - counts[i], max(1, remaining * loads[i] // pool), surplus)
            counts[i] = counts[i] + addition
            surplus = surplus - addition
    return np.array([reach] + counts)


def ragged_sizes(own_key, number_of, total, bound, skew):
    if number_of == 2:
        one = jax.random.randint(own_key, (), max(1, total - bound), min(bound, total - 1) + 1)
        return jnp.stack([one, total - one])
    sizes = jnp.asarray(profile(number_of, total, bound, skew), jnp.int32)
    pairs = (number_of - 1) // 2
    donor, taker = sizes[1:1 + 2 * pairs:2], sizes[2:2 + 2 * pairs:2]
    slack = jnp.minimum(donor - 1, bound - taker)
    moved = jax.random.randint(jax.random.fold_in(own_key, 1), (pairs,), 0, 1 << 20) % (slack + 1)
    sizes = sizes.at[1:1 + 2 * pairs:2].set(donor - moved).at[2:2 + 2 * pairs:2].set(taker + moved)
    return sizes[jax.random.permutation(jax.random.fold_in(own_key, 2), number_of)]


def gaussian(key, shape, scale, most, cuts=(), held_as=jnp.bfloat16):
    array = scale * jax.random.normal(key, shape, jnp.float32)
    if cuts:
        array = array * level_of(key, shape, cuts, -0.22, 0.18)
    return jnp.clip(array, -most, most).astype(held_as)


def setup_inputs(seed: int = 0) -> dict:
    streams_of = jax.random.split(jax.random.key(seed), 22)
    hidden = gaussian(streams_of[0], (PAGES, SEQ, D), 1.0, 6.0, ((0, 16), (1, 2)))
    cotangent = gaussian(streams_of[1], (PAGES, SEQ, D), 1.0, 6.0, ((0, 16), (1, 2)))
    page_lengths = draw_page_lengths(jax.random.fold_in(streams_of[21], 71), 0)
    x_coord = place_ends(jax.random.randint(streams_of[3], (PAGES, SEQ), 0, 1000), jax.random.fold_in(streams_of[3], 1), 0, 999).astype(jnp.int32)
    line_ids = jax.vmap(lambda own: jnp.searchsorted(jnp.cumsum(ragged_sizes(own, LINES, SEQ, LINE_MOST, 2)), jnp.arange(SEQ), side="right"))(jax.random.split(streams_of[4], PAGES)).reshape((PAGES, SEQ)).astype(jnp.int32)
    qkv_w = gaussian(streams_of[5], (D, 3 * D), D ** -0.5, 0.21875)
    q_bias = gaussian(streams_of[6], (D,), 0.5, 3.0)
    v_bias = gaussian(streams_of[7], (D,), 0.5, 3.0)
    rel_table = gaussian(streams_of[8], (REL_BUCKETS, HEADS), 0.7, 4.0)
    x_table = gaussian(streams_of[9], (XY_BUCKETS, HEADS), 0.7, 4.0)
    y_table = gaussian(streams_of[10], (XY_BUCKETS, HEADS), 0.7, 4.0)
    out_w = gaussian(streams_of[11], (D, D), (D // 16) ** -0.5, 0.875)
    out_b = gaussian(streams_of[12], (D,), 0.3, 1.75)
    ln1_gain = jnp.clip(1.0 + 0.1 * jax.random.normal(streams_of[13], (D,), jnp.float32), 0.5, 1.5).astype(jnp.bfloat16)
    ln1_bias = gaussian(streams_of[14], (D,), 0.3, 1.75)
    ffn_in_w = gaussian(streams_of[15], (D, FF), D ** -0.5, 0.21875)
    ffn_in_b = gaussian(streams_of[16], (FF,), 0.3, 1.75)
    ffn_out_w = gaussian(streams_of[17], (FF, D), FF ** -0.5, 0.109375)
    ffn_out_b = gaussian(streams_of[18], (D,), 0.3, 1.75)
    ln2_gain = jnp.clip(1.0 + 0.1 * jax.random.normal(streams_of[19], (D,), jnp.float32), 0.5, 1.5).astype(jnp.bfloat16)
    ln2_bias = gaussian(streams_of[20], (D,), 0.3, 1.75)
    return {"hidden": hidden, "cotangent": cotangent, "page_lengths": page_lengths, "x_coord": x_coord, "line_ids": line_ids, "qkv_w": qkv_w, "q_bias": q_bias, "v_bias": v_bias, "rel_table": rel_table, "x_table": x_table, "y_table": y_table, "out_w": out_w, "out_b": out_b, "ln1_gain": ln1_gain, "ln1_bias": ln1_bias, "ffn_in_w": ffn_in_w, "ffn_in_b": ffn_in_b, "ffn_out_w": ffn_out_w, "ffn_out_b": ffn_out_b, "ln2_gain": ln2_gain, "ln2_bias": ln2_bias}


epsilon = 1e-05
line_gap = 15
masked_value = -1e+30

@jax.custom_vjp
def low(v):
    return lax.optimization_barrier(v.astype(jnp.bfloat16)).astype(jnp.float32)

@jax.custom_vjp
def low_back(v):
    return v

def low_keep(v):
    return (low(v), None)

def low_pass(kept, grad):
    return (grad,)

def back_keep(v):
    return (v, None)

def back_low(kept, grad):
    return (low(grad),)
low.defvjp(low_keep, low_pass)
low_back.defvjp(back_keep, back_low)

def bucket_edges(buckets, reach_max):
    half_count = buckets // 2
    exact_count = half_count // 2
    spread = half_count - exact_count
    thresholds = []
    for step_level in range(1, spread):
        bound_value = exact_count * (reach_max / exact_count) ** (step_level / spread)
        thresholds.append(int(np.ceil(bound_value - 1e-09)))
    return thresholds

def bucketize(offsets, buckets, reach_max):
    half_count = buckets // 2
    distance = jnp.abs(offsets)
    result = jnp.minimum(distance, half_count // 2)
    for threshold in bucket_edges(buckets, reach_max):
        result = result + (distance >= threshold).astype(jnp.int32)
    return (result + half_count * (offsets > 0).astype(jnp.int32)).astype(jnp.int32)

def page_coords(x_coord, line_ids):
    position = jnp.arange(x_coord.shape[-1], dtype=jnp.int32)
    cell_size = 1000 // VIS_SIDE
    grid_x = position % VIS_SIDE * cell_size + cell_size // 2
    grid_y = position // VIS_SIDE * cell_size + cell_size // 2
    visual = position < VIS
    return (jnp.where(visual, grid_x, x_coord), jnp.where(visual, grid_y, line_ids * line_gap))

def allowed(query_pos, key_pos, lengths):
    keys_row = key_pos[None, :]
    queries_col = query_pos[:, None]
    in_reach = (keys_row < VIS) | (queries_col >= VIS) & (jnp.abs(queries_col - keys_row) <= HALF)
    key_live = (key_pos[None, None, :] >= 0) & (key_pos[None, None, :] < VIS + lengths[:, None, None])
    return key_live & in_reach[None]

def layer_norm(running, norm_gain, norm_shift):
    row_mean = lax.optimization_barrier(jnp.mean(running, axis=-1, keepdims=True))
    centred = running - row_mean
    variance = lax.optimization_barrier(jnp.mean(centred * centred, axis=-1, keepdims=True))
    return centred * lax.rsqrt(variance + epsilon) * norm_gain + norm_shift

def layer_page(params, page_rows, length, coord_x, coord_y):
    qkv_w, q_bias, v_bias, rel_table, x_table, y_table, out_w, out_b, ln1_gain, ln1_bias, ffn_in_w, ffn_in_b, ffn_out_w, ffn_out_b, ln2_gain, ln2_bias = params
    highest = lax.Precision.HIGHEST
    seq_len = page_rows.shape[0]
    position = jnp.arange(seq_len, dtype=jnp.int32)
    mixed_bias = jnp.concatenate([q_bias, jnp.zeros_like(q_bias), v_bias])
    mixed_rows = low_back(low(jnp.dot(page_rows, qkv_w, precision=highest) + mixed_bias))
    queries = mixed_rows[:, :D].reshape(seq_len, HEADS, HEAD_DIM)
    key_heads = mixed_rows[:, D:2 * D].reshape(seq_len, HEADS, HEAD_DIM)
    value_heads = mixed_rows[:, 2 * D:].reshape(seq_len, HEADS, HEAD_DIM)
    rel_ids = bucketize(position[None, :] - position[:, None], REL_BUCKETS, REL_REACH)
    x_ids = bucketize(coord_x[None, :] - coord_x[:, None], XY_BUCKETS, XY_REACH)
    y_ids = bucketize(coord_y[None, :] - coord_y[:, None], XY_BUCKETS, XY_REACH)
    bias_sum = rel_table[rel_ids] + x_table[x_ids] + y_table[y_ids]
    scores = jnp.einsum('qhd,khd->hqk', queries, key_heads, precision=highest) * HEAD_DIM ** (-0.5)
    scores = low_back(scores + jnp.transpose(bias_sum, (2, 0, 1)))
    key_mask = allowed(position, position, length[None])[0]
    scores = jnp.where(key_mask[None], scores, masked_value)
    row_peak = lax.optimization_barrier(jnp.max(scores, axis=-1, keepdims=True))
    raised = jnp.exp(scores - row_peak)
    weights = low(raised / lax.optimization_barrier(jnp.sum(raised, axis=-1, keepdims=True)))
    context = jnp.einsum('hqk,khd->qhd', weights, value_heads, precision=highest).reshape(seq_len, D)
    context = low_back(low(context))
    attended = low_back(jnp.dot(context, out_w, precision=highest) + out_b)
    first_out = low(layer_norm(page_rows + attended, ln1_gain, ln1_bias))
    inner_pre = low_back(jnp.dot(first_out, ffn_in_w, precision=highest) + ffn_in_b)
    activated = low(jax.nn.gelu(inner_pre, approximate=False))
    second = low_back(jnp.dot(activated, ffn_out_w, precision=highest) + ffn_out_b)
    return layer_norm(first_out + second, ln2_gain, ln2_bias)

def reference(hidden, cotangent, page_lengths, x_coord, line_ids, qkv_w, q_bias, v_bias, rel_table, x_table, y_table, out_w, out_b, ln1_gain, ln1_bias, ffn_in_w, ffn_in_b, ffn_out_w, ffn_out_b, ln2_gain, ln2_bias):
    params = tuple((weight.astype(jnp.float32) for weight in (qkv_w, q_bias, v_bias, rel_table, x_table, y_table, out_w, out_b, ln1_gain, ln1_bias, ffn_in_w, ffn_in_b, ffn_out_w, ffn_out_b, ln2_gain, ln2_bias)))
    all_rows = hidden.astype(jnp.float32)
    coord_x, coord_y = page_coords(x_coord, line_ids)
    one_page = jax.checkpoint(layer_page)

    def forward(weight_set, page_stack):
        return lax.map(lambda bundle: one_page(weight_set, bundle[0], bundle[1], bundle[2], bundle[3]), (page_stack, page_lengths, coord_x, coord_y))
    final_out, pullback = jax.vjp(forward, params, all_rows)
    grad_list, grad_hidden = pullback(cotangent.astype(jnp.float32))
    return (final_out.astype(jnp.bfloat16), grad_hidden, grad_list[0], grad_list[1], grad_list[2], grad_list[3], grad_list[4], grad_list[5], grad_list[6], grad_list[7], grad_list[8], grad_list[9], grad_list[10], grad_list[11], grad_list[12], grad_list[13], grad_list[14], grad_list[15])
```

```python
import functools
import math

import jax
import jax.numpy as jnp
import numpy as np
from jax import lax
from jax.experimental import pallas as pl
from jax.experimental.pallas import tpu as pltpu
from jax.sharding import PartitionSpec as P

F32 = jnp.float32
BF16 = jnp.bfloat16
I32 = jnp.int32

HEADS = 12
WIDTH = 768
FF = 3072
REL_BUCKETS = 32
REL_REACH = 128
XY_BUCKETS = 64
XY_REACH = 256
VIS = 49
HALF = 64
ROWS = 64
KEYS = 256
CLASSES = 128
HIDE = 127
EPSILON = 1e-05
MASKED = -1e30
NT = (((1,), (1,)), ((), ()))
TN = (((0,), (0,)), ((), ()))
NN = (((1,), (0,)), ((), ()))


def dot(a, b, dims=NN):
    return lax.dot_general(a, b, dims, preferred_element_type=F32)


def bucket_edges(buckets, reach):
    exact = buckets // 4
    spread = buckets // 2 - exact
    return [
        int(np.ceil(exact * (reach / exact) ** (level / spread) - 1e-09))
        for level in range(1, spread)
    ]


def bucket(offsets, buckets, reach):
    distance = jnp.abs(offsets)
    result = jnp.minimum(distance, float(buckets // 4))
    for edge in bucket_edges(buckets, reach):
        result = result + jnp.where(distance >= float(edge), 1.0, 0.0)
    return result + jnp.where(offsets > 0.0, float(buckets // 2), 0.0)


def iota(shape, axis):
    return lax.broadcasted_iota(I32, shape, axis)


def seventh(index):
    return lax.shift_right_logical(index * 37, 8)


def column_of(row):
    size = row.shape[1]
    shape = (size, size)
    spread = jnp.broadcast_to(row, shape)
    return jnp.sum(jnp.where(iota(shape, 0) == iota(shape, 1), spread, 0.0), axis=1, keepdims=True)


def stage_geometry(first_pos, band, x_own, line_own, kx_ref, kc_ref, blocks):
    extent = ROWS * blocks + 2 * HALF
    seq = x_own.shape[-1]
    half_seq = seq // 2

    def window(row):
        left = jnp.concatenate([jnp.zeros((1, HALF), I32), row[:, : extent - HALF]], axis=1)
        start = half_seq - HALF
        right = jnp.concatenate(
            [row[:, start:], jnp.zeros((1, extent - (seq - start)), I32)], axis=1
        )
        return jnp.where(band == 0, left, right)

    pos = first_pos - HALF + iota((1, extent), 1)
    visual = (pos >= 0) & (pos < VIS)
    seventh_pos = seventh(pos)
    x_row = jnp.where(visual, (pos - 7 * seventh_pos) * 142 + 71, window(x_own))
    c_row = jnp.where(visual, 64 + seventh_pos, window(line_own))
    lane = iota((1, HALF), 1)
    x_vis = (lane - 7 * seventh(lane)) * 142 + 71
    c_vis = 64 + seventh(lane)
    for i in range(blocks):
        cut = slice(ROWS * i, ROWS * i + 3 * HALF)
        kx_ref[i : i + 1, :] = jnp.concatenate([x_vis, x_row[:, cut]], axis=1).astype(F32)
        kc_ref[i : i + 1, :] = jnp.concatenate([c_vis, c_row[:, cut]], axis=1).astype(F32)


def key_positions(first_pos, i, shape):
    lane = iota(shape, 1)
    return jnp.where(
        lane < HALF,
        jnp.where(lane < VIS, lane, -1),
        first_pos + ROWS * i - 2 * HALF + lane,
    )


def allowed(first_pos, i, length):
    shape = (ROWS, KEYS)
    lane = iota(shape, 1)
    key = key_positions(first_pos, i, shape)
    query = first_pos + ROWS * i + iota(shape, 0)
    near = (key >= VIS) & (query >= VIS) & (jnp.abs(query - key) <= HALF)
    return (key >= 0) & (key < VIS + length) & ((lane < HALF) | near)


def rel_buckets(first_pos, i):
    shape = (ROWS, KEYS)
    key = key_positions(first_pos, i, shape)
    query = first_pos + ROWS * i + iota(shape, 0)
    return bucket((key - query).astype(F32), REL_BUCKETS, REL_REACH)


def class_y(index):
    return jnp.where(index < 64, 15 * index, 142 * (index - 64) + 71).astype(F32)


def lookup(table_row, index):
    shape = index.shape
    row = jnp.broadcast_to(table_row, (shape[0], 128))
    cuts = [
        jnp.take_along_axis(row, index[:, s : s + 128], axis=1) for s in range(0, shape[1], 128)
    ]
    return cuts[0] if len(cuts) == 1 else jnp.concatenate(cuts, axis=1)


def head_split(tile):
    low = iota(tile.shape, 1) < 64
    zero = jnp.zeros_like(tile)
    return jnp.concatenate([jnp.where(low, tile, zero), jnp.where(low, zero, tile)], axis=0)


def head_join(stack):
    rows = stack.shape[0] // 2
    low = iota((rows, stack.shape[1]), 1) < 64
    return jnp.where(low, stack[:rows], stack[rows:])


def key_tile(kv_ref, i, column):
    return jnp.concatenate(
        [
            kv_ref[0, 0:HALF, column : column + 128],
            kv_ref[0, pl.ds(pl.multiple_of(HALF + ROWS * i, ROWS), 3 * HALF), column : column + 128],
        ],
        axis=0,
    )


def attention_kernel(
    band_ref, len_ref, hid_ref, got_ref, x_ref, line_ref, w_ref, qb_ref, vb_ref,
    rel_ref, xt_ref, yt_ref,
    ctx_ref, p_ref, q_ref, kv_ref, ext_ref,
    kx_ref, kc_ref, rb_ref, yb_ref, ctx_s, tab_ref,
):
    page = pl.program_id(0)
    band = band_ref[0]
    rows = hid_ref.shape[1]
    blocks = q_ref.shape[1] // ROWS
    first_pos = band * rows

    @pl.when(page == 0)
    def _():
        for slot, table in enumerate((rel_ref, xt_ref, yt_ref)):
            count = table.shape[0]
            eye = jnp.where(iota((count, 128), 0) == iota((count, 128), 1), 1.0, 0.0).astype(BF16)
            turned = dot(table[...], eye, TN)
            if slot == 1:
                turned = jnp.where(iota((HEADS, 128), 1) == HIDE, MASKED, turned)
            tab_ref[:HEADS, 128 * slot : 128 * slot + 128] = turned
        for i in range(blocks):
            index = rel_buckets(first_pos, i).astype(I32)
            for h in range(HEADS):
                rb_ref[i, ROWS * h : ROWS * h + ROWS, :] = lookup(tab_ref[h : h + 1, 0:128], index)
        square = (CLASSES, CLASSES)
        gap = class_y(iota(square, 1)) - class_y(iota(square, 0))
        index = jnp.minimum(bucket(gap, XY_BUCKETS, XY_REACH), 63.0).astype(I32)
        for h in range(HEADS):
            yb_ref[:, CLASSES * h : CLASSES * h + CLASSES] = lookup(
                tab_ref[h : h + 1, 256:384], index
            ).astype(BF16)

    own = pl.ds(page, 1)
    stage_geometry(first_pos, band, x_ref[own, :], line_ref[own, :], kx_ref, kc_ref, blocks)
    ext_ref[0, :HALF] = jnp.where(band == 0, hid_ref[0, :HALF], got_ref[0, :HALF])
    ext_ref[0, HALF : 2 * HALF] = got_ref[0, HALF:]
    ext_ref[0, 2 * HALF :] = hid_ref[0]
    q_ref[0, 0:rows] = (
        (dot(hid_ref[0], w_ref[:, :WIDTH]) + qb_ref[...].astype(F32)).astype(BF16).astype(F32)
        * 0.125
    ).astype(BF16)
    q_ref[0, rows:] = jnp.zeros((q_ref.shape[1] - rows, WIDTH), BF16)
    kv_ref[0, : 2 * HALF + rows, :WIDTH] = dot(ext_ref[0], w_ref[:, WIDTH : 2 * WIDTH]).astype(BF16)
    kv_ref[0, : 2 * HALF + rows, WIDTH:] = (
        dot(ext_ref[0], w_ref[:, 2 * WIDTH :]) + vb_ref[...].astype(F32)
    ).astype(BF16)
    kv_ref[0, 2 * HALF + rows : 3 * HALF + rows] = kv_ref[0, HALF : 2 * HALF]
    tail = kv_ref.shape[1] - (3 * HALF + rows)
    kv_ref[0, 3 * HALF + rows :] = jnp.zeros((tail, 2 * WIDTH), BF16)

    def block(i, _):
        start = pl.multiple_of(ROWS * i, ROWS)
        kx = kx_ref[pl.ds(i, 1), :]
        kc = kc_ref[pl.ds(i, 1), :]
        gap = kx - column_of(kx[:, 2 * HALF : 3 * HALF])
        index = jnp.where(
            allowed(first_pos, i, len_ref[page]), bucket(gap, XY_BUCKETS, XY_REACH), float(HIDE)
        ).astype(I32)
        pick_q = jnp.where(
            iota((ROWS, CLASSES), 1).astype(F32) == column_of(kc[:, 2 * HALF : 3 * HALF]), 1.0, 0.0
        ).astype(BF16)
        pick_k = jnp.where(
            iota((KEYS, CLASSES), 1).astype(F32) == column_of(kc), 1.0, 0.0
        ).astype(BF16)
        pairs = range(HEADS // 2)
        scores = []
        for j in pairs:
            column = 128 * j
            queries = head_split(q_ref[0, pl.ds(start, ROWS), column : column + 128])
            picked = dot(pick_q, yb_ref[:, 2 * column : 2 * column + 256]).astype(BF16)
            picked = jnp.concatenate([picked[:, :128], picked[:, 128:]], axis=0)
            scores.append(
                dot(
                    jnp.concatenate([queries, picked], axis=1),
                    jnp.concatenate([key_tile(kv_ref, i, column), pick_k], axis=1),
                    NT,
                )
            )
        weights = []
        for j in pairs:
            x_bias = jnp.concatenate(
                [lookup(tab_ref[2 * j + e : 2 * j + e + 1, 128:256], index) for e in (0, 1)], axis=0
            )
            biased = scores[j] + rb_ref[i, 128 * j : 128 * j + 128, :] + x_bias
            peak = jnp.max(biased, axis=1, keepdims=True)
            raised = jnp.exp(biased - peak)
            weights.append(
                (raised * (1.0 / jnp.sum(raised, axis=1, keepdims=True))).astype(BF16)
            )
        contexts = [
            dot(weights[j], key_tile(kv_ref, i, WIDTH + 128 * j)) for j in pairs
        ]
        for j in pairs:
            p_ref[0, i, 128 * j : 128 * j + 128, :] = weights[j]
        ctx_s[pl.ds(start, ROWS), :] = jnp.concatenate(
            [head_join(c).astype(BF16) for c in contexts], axis=1
        )
        return 0

    lax.fori_loop(0, blocks, block, 0)
    ctx_ref[0] = ctx_s[:rows]


def page_block(*shape):
    return pl.BlockSpec((1,) + shape, lambda p, *_: (p,) + (0,) * len(shape))


def whole(*shape):
    return pl.BlockSpec(shape, lambda *_: (0,) * len(shape))


def attention_forward(
    band, lengths, hidden, got, x_coord, line_ids, qkv_w, q_bias, v_bias, tables
):
    pages, rows, width = hidden.shape
    blocks = -(-rows // ROWS)
    padded = blocks * ROWS
    ext = padded + 3 * HALF
    shape = jax.ShapeDtypeStruct
    return pl.pallas_call(
        attention_kernel,
        out_shape=(
            shape((pages, rows, width), BF16),
            shape((pages, blocks, HEADS * ROWS, KEYS), BF16),
            shape((pages, padded, width), BF16),
            shape((pages, ext, 2 * width), BF16),
            shape((pages, rows + 2 * HALF, width), BF16),
        ),
        grid_spec=pltpu.PrefetchScalarGridSpec(
            num_scalar_prefetch=2,
            grid=(pages,),
            in_specs=[
                page_block(rows, width),
                page_block(2 * HALF, width),
                whole(*x_coord.shape),
                whole(*line_ids.shape),
                whole(width, 3 * width),
                whole(1, width),
                whole(1, width),
            ]
            + [whole(*table.shape) for table in tables],
            out_specs=[
                page_block(rows, width),
                page_block(blocks, HEADS * ROWS, KEYS),
                page_block(padded, width),
                page_block(ext, 2 * width),
                page_block(rows + 2 * HALF, width),
            ],
            scratch_shapes=[
                pltpu.VMEM((8, KEYS), F32),
                pltpu.VMEM((8, KEYS), F32),
                pltpu.VMEM((blocks, HEADS * ROWS, KEYS), F32),
                pltpu.VMEM((CLASSES, HEADS * CLASSES), BF16),
                pltpu.VMEM((padded, width), BF16),
                pltpu.VMEM((16, 384), F32),
            ],
        ),
        compiler_params=pltpu.CompilerParams(vmem_limit_bytes=56 << 20),
        cost_estimate=pl.CostEstimate(
            flops=2 * pages * (rows + 2 * HALF) * width * 3 * width
            + 8 * pages * padded * HEADS * KEYS * 128,
            bytes_accessed=30 << 20,
            transcendentals=pages * padded * HEADS * KEYS,
        ),
        name="attention_forward",
    )(
        band, lengths, hidden, got, x_coord, line_ids, qkv_w,
        q_bias.reshape(1, width), v_bias.reshape(1, width), *tables,
    )


def layer_norm(total):
    centred = total - jnp.mean(total, axis=1, keepdims=True)
    inverse = lax.rsqrt(jnp.mean(centred * centred, axis=1, keepdims=True) + EPSILON)
    return centred * inverse, inverse


def norm_back(grad, normed, inverse, gain):
    scaled = grad * gain
    return inverse * (
        scaled
        - jnp.mean(scaled, axis=1, keepdims=True)
        - normed * jnp.mean(scaled * normed, axis=1, keepdims=True)
    )


def gelu_parts(inner):
    size = jnp.abs(inner)
    falling = jnp.exp(inner * inner * -0.5)
    t = 1.0 / (1.0 + (0.3275911 * math.sqrt(0.5)) * size)
    poly = 1.061405429 * t - 1.453152027
    poly = poly * t + 1.421413741
    poly = poly * t - 0.284496736
    poly = poly * t + 0.254829592
    tail = (0.5 * poly) * (t * falling)
    share = jnp.where(inner >= 0.0, 1.0 - tail, tail)
    return inner * share, share + inner * falling * (2.0 * math.pi) ** (-0.5)


def column_sum(values):
    return jnp.sum(values, axis=0, keepdims=True)


def accumulate(ref, row, value):
    first = pl.program_id(0) == 0

    @pl.when(first)
    def _():
        ref[row : row + 1, :] = value

    @pl.when(jnp.logical_not(first))
    def _():
        ref[row : row + 1, :] = ref[row : row + 1, :] + value


def ffn_forward_kernel(
    ctx_ref, hid_ref, cot_ref, ob_ref, g1_ref, b1_ref, fb_ref, g2_ref, b2_ref, bin_ref,
    wo_ref, w1_ref, w2_ref,
    out_ref, first_ref, norm_ref, inv_ref, act_ref, slope_ref, dh_ref, ds_ref, sums_ref,
):
    out_b, gain1, bias1, ffn_b, gain2, bias2 = (
        r[...].astype(F32) for r in (ob_ref, g1_ref, b1_ref, fb_ref, g2_ref, b2_ref)
    )
    attended = dot(ctx_ref[0], wo_ref[...]) + out_b
    normed, inverse = layer_norm(hid_ref[0].astype(F32) + attended)
    first = (normed * gain1 + bias1).astype(BF16)
    first_ref[0] = first
    norm_ref[0] = normed
    inv_ref[0] = jnp.broadcast_to(inverse, inv_ref.shape[1:])
    chunk = 768
    count = FF // chunk
    second = first.astype(F32) + ffn_b

    def inner_of(c):
        cut = slice(chunk * c, chunk * c + chunk)
        return dot(first, w1_ref[:, cut]) + bin_ref[:, cut].astype(F32)

    ahead = inner_of(0)
    for c in range(count):
        cut = slice(chunk * c, chunk * c + chunk)
        inner = ahead
        if c + 1 < count:
            ahead = inner_of(c + 1)
        act, slope = gelu_parts(inner)
        act = act.astype(BF16)
        act_ref[0, :, cut] = act
        slope_ref[0, :, cut] = slope.astype(BF16)
        second = second + dot(act, w2_ref[cut, :])
    normed2, inverse2 = layer_norm(second)
    out_ref[0] = (normed2 * gain2 + bias2).astype(BF16)
    grad = cot_ref[0].astype(F32)
    back = norm_back(grad, normed2, inverse2, gain2)
    low = back.astype(BF16)
    dh_ref[0] = back
    ds_ref[0] = low
    accumulate(sums_ref, 0, column_sum(grad * normed2))
    accumulate(sums_ref, 1, column_sum(grad))
    accumulate(sums_ref, 2, column_sum(low.astype(F32)))


def ffn_forward(context, hidden, cotangent, vectors, ffn_in_b, out_w, ffn_in_w, ffn_out_w):
    pages, rows, width = context.shape
    shape = jax.ShapeDtypeStruct
    return pl.pallas_call(
        ffn_forward_kernel,
        out_shape=(
            shape((pages, rows, width), BF16),
            shape((pages, rows, width), BF16),
            shape((pages, rows, width), F32),
            shape((pages, rows, 128), F32),
            shape((pages, rows, FF), BF16),
            shape((pages, rows, FF), BF16),
            shape((pages, rows, width), F32),
            shape((pages, rows, width), BF16),
            shape((8, width), F32),
        ),
        grid=(pages,),
        in_specs=[
            page_block(rows, width),
            page_block(rows, width),
            page_block(rows, width),
        ]
        + [whole(1, width)] * 6
        + [
            whole(1, FF),
            whole(width, width),
            whole(width, FF),
            whole(FF, width),
        ],
        out_specs=[
            page_block(rows, width),
            page_block(rows, width),
            page_block(rows, width),
            page_block(rows, 128),
            page_block(rows, FF),
            page_block(rows, FF),
            page_block(rows, width),
            page_block(rows, width),
            whole(8, width),
        ],
        compiler_params=pltpu.CompilerParams(vmem_limit_bytes=60 << 20),
        cost_estimate=pl.CostEstimate(
            flops=2 * pages * rows * width * (2 * FF + width),
            bytes_accessed=40 << 20,
            transcendentals=pages * rows * FF,
        ),
        name="ffn_forward",
    )(
        context, hidden, cotangent, *[v.reshape(1, width) for v in vectors],
        ffn_in_b.reshape(1, FF), out_w, ffn_in_w, ffn_out_w,
    )


def ffn_backward_kernel(
    ds_ref, slope_ref, dh_ref, norm_ref, inv_ref, g1_ref, wo_ref, w1_ref, w2_ref,
    di_ref, dh1_ref, da_ref, dc_ref, sums_ref, bsum_ref,
):
    low = ds_ref[0]
    chunk = 768
    count = FF // chunk
    total = dh_ref[0]

    def act_of(c):
        return dot(low, w2_ref[chunk * c : chunk * c + chunk, :], NT)

    ahead = act_of(0)
    for c in range(count):
        cut = slice(chunk * c, chunk * c + chunk)
        grad = ahead
        if c + 1 < count:
            ahead = act_of(c + 1)
        inner = (grad * slope_ref[0, :, cut].astype(F32)).astype(BF16)
        di_ref[0, :, cut] = inner
        accumulate(bsum_ref.at[:, cut], 0, column_sum(inner.astype(F32)))
        total = total + dot(inner, w1_ref[:, cut], NT)
    normed = norm_ref[0]
    back = norm_back(total, normed, inv_ref[0, :, 0:1], g1_ref[...].astype(F32))
    low = back.astype(BF16)
    dh1_ref[0] = back
    da_ref[0] = low
    dc_ref[0] = dot(low, wo_ref[...], NT).astype(BF16)
    accumulate(sums_ref, 0, column_sum(total * normed))
    accumulate(sums_ref, 1, column_sum(total))
    accumulate(sums_ref, 2, column_sum(low.astype(F32)))


def ffn_backward(second_low, slope, grad_total, normed, inverse, gain, out_w, ffn_in_w, ffn_out_w):
    pages, rows, width = second_low.shape
    shape = jax.ShapeDtypeStruct
    return pl.pallas_call(
        ffn_backward_kernel,
        out_shape=(
            shape((pages, rows, FF), BF16),
            shape((pages, rows, width), F32),
            shape((pages, rows, width), BF16),
            shape((pages, rows, width), BF16),
            shape((8, width), F32),
            shape((8, FF), F32),
        ),
        grid=(pages,),
        in_specs=[
            page_block(rows, width),
            page_block(rows, FF),
            page_block(rows, width),
            page_block(rows, width),
            page_block(rows, 128),
            whole(1, width),
            whole(width, width),
            whole(width, FF),
            whole(FF, width),
        ],
        out_specs=[
            page_block(rows, FF),
            page_block(rows, width),
            page_block(rows, width),
            page_block(rows, width),
            whole(8, width),
            whole(8, FF),
        ],
        compiler_params=pltpu.CompilerParams(vmem_limit_bytes=60 << 20),
        cost_estimate=pl.CostEstimate(
            flops=2 * pages * rows * width * (2 * FF + width),
            bytes_accessed=40 << 20,
            transcendentals=0,
        ),
        name="ffn_backward",
    )(
        second_low, slope, grad_total, normed, inverse, gain.reshape(1, width),
        out_w, ffn_in_w, ffn_out_w,
    )


def attention_back_kernel(
    p_ref, q_ref, kv_ref, dc_ref,
    dm_ref, ds_ref,
    dkv_ref, dc_s, dq_s,
):
    rows = dc_ref.shape[1]
    blocks = q_ref.shape[1] // ROWS
    dkv_ref[...] = jnp.zeros_like(dkv_ref)
    dc_s[:rows] = dc_ref[0]
    dc_s[rows:] = jnp.zeros((dc_s.shape[0] - rows, WIDTH), BF16)
    def block(i, _):
        start = pl.multiple_of(ROWS * i, ROWS)
        window = pl.ds(pl.multiple_of(HALF + ROWS * i, ROWS), 3 * HALF)
        pairs = range(HEADS // 2)
        grads = []
        for j in pairs:
            column = 128 * j
            grads.append(head_split(dc_s[pl.ds(start, ROWS), column : column + 128]))
        dprobs = [dot(grads[j], key_tile(kv_ref, i, WIDTH + 128 * j), NT) for j in pairs]
        for j in pairs:
            dv = dot(p_ref[0, i, 128 * j : 128 * j + 128, :], grads[j], TN)
            column = WIDTH + 128 * j
            cut = slice(column, column + 128)
            dkv_ref[0:HALF, cut] = dkv_ref[0:HALF, cut] + dv[:HALF]
            dkv_ref[window, cut] = dkv_ref[window, cut] + dv[HALF:]
        lows = []
        for j in pairs:
            probs = p_ref[0, i, 128 * j : 128 * j + 128, :].astype(F32)
            grad = probs * (
                dprobs[j] - jnp.sum(probs * dprobs[j], axis=1, keepdims=True)
            )
            lows.append(grad.astype(BF16))
        dq = [head_join(dot(lows[j], key_tile(kv_ref, i, 128 * j))) for j in pairs]
        dq_s[pl.ds(start, ROWS), :] = (jnp.concatenate(dq, axis=1) * 0.125).astype(BF16)
        for j in pairs:
            cut = slice(128 * j, 128 * j + 128)
            dk = dot(lows[j], head_split(q_ref[0, pl.ds(start, ROWS), cut]), TN)
            dkv_ref[0:HALF, cut] = dkv_ref[0:HALF, cut] + dk[:HALF]
            dkv_ref[window, cut] = dkv_ref[window, cut] + dk[HALF:]

        for j in pairs:
            ds_ref[0, i, 128 * j : 128 * j + 128, :] = lows[j]
        return 0

    lax.fori_loop(0, blocks, block, 0)
    dm_ref[0, : 2 * HALF, :WIDTH] = jnp.zeros((2 * HALF, WIDTH), BF16)
    dm_ref[0, 2 * HALF :, :WIDTH] = dq_s[:rows]
    dm_ref[0, :HALF, WIDTH:] = dkv_ref[:HALF].astype(BF16)
    dm_ref[0, HALF : 2 * HALF, WIDTH:] = (
        dkv_ref[HALF : 2 * HALF] + dkv_ref[2 * HALF + rows : 3 * HALF + rows]
    ).astype(BF16)
    dm_ref[0, 2 * HALF :, WIDTH:] = dkv_ref[2 * HALF : 2 * HALF + rows].astype(BF16)


def attention_backward(probs, queries, pairs, grad_context):
    pages, rows, width = grad_context.shape
    padded = queries.shape[1]
    blocks = padded // ROWS
    ext = pairs.shape[1]
    shape = jax.ShapeDtypeStruct
    return pl.pallas_call(
        attention_back_kernel,
        out_shape=(
            shape((pages, rows + 2 * HALF, 3 * width), BF16),
            shape(probs.shape, BF16),
        ),
        grid=(pages,),
        in_specs=[
            page_block(blocks, HEADS * ROWS, KEYS),
            page_block(padded, width),
            page_block(ext, 2 * width),
            page_block(rows, width),
        ],
        out_specs=[page_block(rows + 2 * HALF, 3 * width), page_block(blocks, HEADS * ROWS, KEYS)],
        scratch_shapes=[
            pltpu.VMEM((ext, 2 * width), F32),
            pltpu.VMEM((padded, width), BF16),
            pltpu.VMEM((padded, width), BF16),
        ],
        compiler_params=pltpu.CompilerParams(vmem_limit_bytes=56 << 20),
        cost_estimate=pl.CostEstimate(
            flops=10 * pages * padded * HEADS * KEYS * 128, bytes_accessed=30 << 20, transcendentals=0
        ),
        name="attention_backward",
    )(probs, queries, pairs, grad_context)


def table_kernel(
    band_ref, ds_ref, x_ref, line_ref, tab_ref, kx_ref, kc_ref, left_ref, right_ref, index_ref
):
    page = pl.program_id(0)
    band = band_ref[0]
    blocks = ds_ref.shape[1]
    first_pos = band * (x_ref.shape[-1] // 2)
    own_page = pl.ds(page, 1)
    stage_geometry(first_pos, band, x_ref[own_page, :], line_ref[own_page, :], kx_ref, kc_ref, blocks)
    slots = iota((REL_BUCKETS + 2 * XY_BUCKETS, KEYS), 0).astype(F32).astype(BF16)
    one = jnp.ones((), BF16)
    zero = jnp.zeros((), BF16)

    def block(i, table_sum):
        left_ref[...] = ds_ref[0, i, :, :128].astype(F32)
        right_ref[...] = ds_ref[0, i, :, 128:].astype(F32)
        kx = kx_ref[pl.ds(i, 1), :]
        ky = class_y(kc_ref[pl.ds(i, 1), :].astype(I32))
        index_ref[0:ROWS] = bucket(kx - column_of(kx[:, 2 * HALF : 3 * HALF]), XY_BUCKETS, XY_REACH)
        index_ref[ROWS : 2 * ROWS] = 64.0 + bucket(
            ky - column_of(ky[:, 2 * HALF : 3 * HALF]), XY_BUCKETS, XY_REACH
        )
        index_ref[2 * ROWS : 3 * ROWS] = 128.0 + rel_buckets(first_pos, i)

        def table_row(q, acc):
            own = jnp.concatenate(
                [
                    jnp.broadcast_to(index_ref[pl.ds(q, 1), :], (XY_BUCKETS, KEYS)),
                    jnp.broadcast_to(index_ref[pl.ds(ROWS + q, 1), :], (XY_BUCKETS, KEYS)),
                    jnp.broadcast_to(index_ref[pl.ds(2 * ROWS + q, 1), :], (REL_BUCKETS, KEYS)),
                ],
                axis=0,
            ).astype(BF16)
            heads = jnp.concatenate(
                [
                    left_ref[pl.ds(q, HEADS, stride=ROWS), :],
                    right_ref[pl.ds(q, HEADS, stride=ROWS), :],
                ],
                axis=1,
            ).astype(BF16)
            return acc + dot(heads, jnp.where(slots == own, one, zero), NT)

        return lax.fori_loop(0, ROWS, table_row, table_sum, unroll=8)

    table_sum = lax.fori_loop(
        0, blocks, block, jnp.zeros((HEADS, REL_BUCKETS + 2 * XY_BUCKETS), F32)
    )

    @pl.when(page == 0)
    def _():
        tab_ref[...] = table_sum

    @pl.when(page > 0)
    def _():
        tab_ref[...] = tab_ref[...] + table_sum


def table_sums(band, grad_scores, x_coord, line_ids):
    pages, blocks, height, keys = grad_scores.shape
    buckets = REL_BUCKETS + 2 * XY_BUCKETS
    return pl.pallas_call(
        table_kernel,
        out_shape=jax.ShapeDtypeStruct((HEADS, buckets), F32),
        grid_spec=pltpu.PrefetchScalarGridSpec(
            num_scalar_prefetch=1,
            grid=(pages,),
            in_specs=[
                page_block(blocks, height, keys),
                whole(*x_coord.shape),
                whole(*line_ids.shape),
            ],
            out_specs=whole(HEADS, buckets),
            scratch_shapes=[
                pltpu.VMEM((8, KEYS), F32),
                pltpu.VMEM((8, KEYS), F32),
                pltpu.VMEM((height, 128), F32),
                pltpu.VMEM((height, 128), F32),
                pltpu.VMEM((3 * ROWS, KEYS), F32),
            ],
        ),
        compiler_params=pltpu.CompilerParams(vmem_limit_bytes=24 << 20),
        cost_estimate=pl.CostEstimate(
            flops=60 * pages * blocks * height * keys * 32, bytes_accessed=6 << 20, transcendentals=0
        ),
        name="table_sums",
    )(band, grad_scores, x_coord, line_ids)


def hidden_back_kernel(dm_ref, dh_ref, w_ref, own_ref, far_ref, sums_ref):
    accumulate(sums_ref, 0, column_sum(dm_ref[0].astype(F32)))
    own_ref[0] = dh_ref[0] + dot(dm_ref[0, 2 * HALF :], w_ref[...], NT)
    far_ref[0] = dot(dm_ref[0, : 2 * HALF, WIDTH:], w_ref[:, WIDTH:], NT).astype(BF16)


def hidden_backward(grad_mixed, grad_total, qkv_w):
    pages, rows, width = grad_total.shape
    shape = jax.ShapeDtypeStruct
    return pl.pallas_call(
        hidden_back_kernel,
        out_shape=(
            shape((pages, rows, width), F32),
            shape((pages, 2 * HALF, width), BF16),
            shape((8, 3 * width), F32),
        ),
        grid=(pages,),
        in_specs=[
            page_block(rows + 2 * HALF, 3 * width),
            page_block(rows, width),
            whole(width, 3 * width),
        ],
        out_specs=[page_block(rows, width), page_block(2 * HALF, width), whole(8, 3 * width)],
        compiler_params=pltpu.CompilerParams(vmem_limit_bytes=40 << 20),
        cost_estimate=pl.CostEstimate(
            flops=2 * pages * rows * width * 3 * width, bytes_accessed=15 << 20, transcendentals=0
        ),
        name="hidden_backward",
    )(grad_mixed, grad_total, qkv_w)


def edge_kernel(band_ref, grad_ref, far_ref, got_ref, out_ref):
    side = pl.program_id(1)
    band = band_ref[0]
    far = far_ref[0].astype(F32)
    got = got_ref[0].astype(F32)
    low = jnp.where(band == 0, far[:HALF] + got[:HALF], got[HALF:])
    high = jnp.where(band == 0, got[HALF:], 0.0)
    add = jnp.where(side < 2, low, high)
    half = HALF // 2
    out_ref[0] = grad_ref[0] + jnp.where(side % 2 == 0, add[:half], add[half:])


def edge_add(band, grad, far, got):
    pages, rows, width = grad.shape
    half = HALF // 2
    last = rows // half - 2

    def edge(p, s, *_):
        return (p, jnp.where(s < 2, s, last + s - 2), 0)

    return pl.pallas_call(
        edge_kernel,
        out_shape=jax.ShapeDtypeStruct(grad.shape, F32),
        grid_spec=pltpu.PrefetchScalarGridSpec(
            num_scalar_prefetch=1,
            grid=(pages, 4),
            in_specs=[
                pl.BlockSpec((1, half, width), edge),
                page_block(2 * HALF, width),
                page_block(2 * HALF, width),
            ],
            out_specs=pl.BlockSpec((1, half, width), edge),
        ),
        input_output_aliases={1: 0},
        name="edge_add",
    )(band, grad, far, got)


def split_orders(count):
    total = count.bit_length() - 1
    side = total // 3
    x, y, z = (range(side), range(side, 2 * side), range(2 * side, total))
    near, far = list(z)[:-1], list(z)[-1:]
    return list(x) + list(y) + near + far, list(y) + near + list(x) + far


def place(chunk, order):
    spot = 0
    for level, bit in enumerate(order):
        spot = spot + (((chunk >> bit) & 1) << (len(order) - 1 - level))
    return spot


def product_parts(band, left, right, chunks):
    tokens, height = left.shape
    width = right.shape[1]
    size = height // chunks
    step = 384
    each = step // size
    half = chunks // 2
    orders = split_orders(half)

    def kernel(band_ref, l_ref, r_ref, send_ref, keep_ref):
        i = pl.program_id(0)
        result = dot(l_ref[...], r_ref[...], TN).astype(BF16)
        owner = (i >= pl.num_programs(0) // 2).astype(I32)

        def write(ref):
            for c in range(each):
                chunk = i * each + c - owner * half
                spot = jnp.where(owner == 0, place(chunk, orders[0]), place(chunk, orders[1]))
                ref[spot] = result[size * c : size * c + size]

        pl.when(owner == band_ref[0])(lambda: write(keep_ref))
        pl.when(owner != band_ref[0])(lambda: write(send_ref))

    out = jax.ShapeDtypeStruct((half, size, width), BF16)
    return pl.pallas_call(
        kernel,
        out_shape=(out, out),
        grid_spec=pltpu.PrefetchScalarGridSpec(
            num_scalar_prefetch=1,
            grid=(height // step,),
            in_specs=[pl.BlockSpec((tokens, step), lambda i, *_: (0, i)), whole(tokens, width)],
            out_specs=[whole(half, size, width), whole(half, size, width)],
        ),
        compiler_params=pltpu.CompilerParams(vmem_limit_bytes=40 << 20),
        cost_estimate=pl.CostEstimate(
            flops=2 * tokens * height * width, bytes_accessed=16 << 20, transcendentals=0
        ),
        name="product_parts",
    )(band, left, right)


def product_halves(band, left, right):
    tokens, height = left.shape
    width = right.shape[1]
    step = height // 2

    def kernel(band_ref, l_ref, r_ref, send_ref, keep_ref):
        result = dot(l_ref[...], r_ref[...], TN).astype(BF16)

        @pl.when(pl.program_id(0) == 0)
        def _():
            send_ref[...] = result

        @pl.when(pl.program_id(0) == 1)
        def _():
            keep_ref[...] = result

    out = jax.ShapeDtypeStruct((step, width), BF16)
    return pl.pallas_call(
        kernel,
        out_shape=(out, out),
        grid_spec=pltpu.PrefetchScalarGridSpec(
            num_scalar_prefetch=1,
            grid=(2,),
            in_specs=[
                pl.BlockSpec(
                    (tokens, step), lambda i, b: (0, jnp.where(i == 0, 1 - b[0], b[0]))
                ),
                whole(tokens, width),
            ],
            out_specs=[whole(step, width), whole(step, width)],
        ),
        compiler_params=pltpu.CompilerParams(vmem_limit_bytes=40 << 20),
        cost_estimate=pl.CostEstimate(
            flops=2 * tokens * height * width, bytes_accessed=16 << 20, transcendentals=0
        ),
        name="product_halves",
    )(band, left, right)


def swap_bands(block):
    return lax.ppermute(block, "band", [(0, 1), (1, 0)])


def swap_pages(block, level, orders):
    count = lax.axis_size("page")
    route = [
        (b * count + p, b * count + (p ^ (1 << orders[b][level])))
        for b in range(2)
        for p in range(count)
    ]
    return lax.ppermute(block, ("band", "page"), route)


def sides(orders):
    band, page = lax.axis_index("band"), lax.axis_index("page")
    return [
        jnp.where(band == 0, (page >> first) & 1, (page >> second) & 1)
        for first, second in zip(*orders)
    ]


def half_of(block, side):
    size = block.shape[0] // 2
    return lax.dynamic_slice_in_dim(block, side * size, size, 0)


def add_low(a, b):
    return (a.astype(F32) + b.astype(F32)).astype(BF16)


def scatter_sum(send, keep):
    orders = split_orders(lax.axis_size("page"))
    got = swap_bands(send)
    for level, side in enumerate(sides(orders)):
        sent = add_low(half_of(keep, 1 - side), half_of(got, 1 - side))
        keep = add_low(half_of(keep, side), half_of(got, side))
        got = swap_pages(sent, level, orders)
    return (keep.astype(F32) + got.astype(F32))[0]


def join(mine, other, side):
    return jnp.where(
        side == 0,
        jnp.concatenate([mine, other], axis=0),
        jnp.concatenate([other, mine], axis=0),
    )


def all_sum(send, keep):
    orders = split_orders(lax.axis_size("page"))
    got = swap_bands(send)
    places = sides(orders)
    for level, side in enumerate(places[:-1]):
        sent = add_low(half_of(keep, 1 - side), half_of(got, 1 - side))
        keep = add_low(half_of(keep, side), half_of(got, side))
        got = swap_pages(sent, level, orders)
    keep = add_low(keep, got)
    keep = add_low(keep, swap_pages(keep, len(places) - 1, orders))
    for level in reversed(range(len(places) - 1)):
        keep = join(keep, swap_pages(keep, level, orders), places[level])
    return join(keep, swap_bands(keep), lax.axis_index("band")).astype(F32)


def all_sum_small(block):
    orders = split_orders(lax.axis_size("page"))
    block = block + swap_bands(block)
    for level in range(len(orders[0])):
        block = block + swap_pages(block, level, orders)
    return block


def flat(block):
    return block.reshape(-1, block.shape[-1])


def local(
    hidden, cotangent, page_lengths, x_coord, line_ids, qkv_w, q_bias, v_bias,
    rel_table, x_table, y_table, out_w, out_b, ln1_gain, ln1_bias,
    ffn_in_w, ffn_in_b, ffn_out_w, ffn_out_b, ln2_gain, ln2_bias,
):
    pages, rows, width = hidden.shape
    band = lax.axis_index("band")
    chunks = 2 * lax.axis_size("page")
    band_arr = band.reshape(1).astype(I32)
    own_edge = jnp.where(band == 0, hidden[:, rows - HALF :], hidden[:, :HALF])
    got = swap_bands(jnp.concatenate([hidden[:, :HALF], own_edge], axis=1))
    context, probs, queries, pairs, extended = attention_forward(
        band_arr, page_lengths, hidden, got, x_coord, line_ids, qkv_w, q_bias, v_bias,
        (rel_table, x_table, y_table),
    )
    output, first, normed, inverse, act, slope, grad_total2, second_low, sums2 = ffn_forward(
        context, hidden, cotangent, (out_b, ln1_gain, ln1_bias, ffn_out_b, ln2_gain, ln2_bias),
        ffn_in_b, out_w, ffn_in_w, ffn_out_w,
    )
    grad_ffn_out = scatter_sum(*product_parts(band_arr, flat(act), flat(second_low), chunks))
    grad_inner, grad_total1, attn_low, grad_context, sums1, inner_sums = ffn_backward(
        second_low, slope, grad_total2, normed, inverse, ln1_gain, out_w, ffn_in_w, ffn_out_w
    )
    grad_ffn_in = scatter_sum(*product_parts(band_arr, flat(grad_inner), flat(first), chunks))
    grad_out = all_sum(*product_halves(band_arr, flat(context), flat(attn_low)))
    grad_mixed, grad_scores = attention_backward(probs, queries, pairs, grad_context)
    grad_qkv = all_sum(*product_halves(band_arr, flat(extended), flat(grad_mixed)))
    grad_hidden, far, mixed_sums = hidden_backward(grad_mixed, grad_total1, qkv_w)
    grad_hidden = edge_add(band_arr, grad_hidden, far, swap_bands(far))
    tables = table_sums(band_arr, grad_scores, x_coord, line_ids)
    small = jnp.concatenate(
        [
            mixed_sums[0].reshape(3, width),
            sums1[:3],
            sums2[:3],
            inner_sums[0].reshape(FF // width, width),
            jnp.pad(tables, ((0, 3), (0, width - tables.shape[1]))),
        ],
        axis=0,
    )
    small = all_sum_small(small)
    tables = small[13 : 13 + HEADS]
    return (
        output,
        grad_hidden,
        grad_qkv,
        small[0],
        small[2],
        tables[:, 128:160].T,
        tables[:, :64].T,
        tables[:, 64:128].T,
        grad_out,
        small[5],
        small[3],
        small[4],
        grad_ffn_in.T,
        small[9:13].reshape(FF),
        grad_ffn_out,
        small[8],
        small[6],
        small[7],
    )


def solution(mesh):
    in_specs = (
        P("page", "band", None),
        P("page", "band", None),
        P("page"),
        P("page", None),
        P("page", None),
        P(),
        P(),
        P(),
        P(),
        P(),
        P(),
        P(),
        P(),
        P(),
        P(),
        P(),
        P(),
        P(),
        P(),
        P(),
        P(),
    )
    out_specs = (
        P("page", "band", None),
        P("page", "band", None),
        P(),
        P(),
        P(),
        P(),
        P(),
        P(),
        P(),
        P(),
        P(),
        P(),
        P(None, ("band", "page")),
        P(),
        P(("band", "page"), None),
        P(),
        P(),
        P(),
    )
    return jax.shard_map(local, mesh=mesh, in_specs=in_specs, out_specs=out_specs, check_vma=False)
```

```python
import functools
import math

import jax
import jax.numpy as jnp
import numpy as np
from jax import lax
from jax.experimental import pallas as pl
from jax.experimental.pallas import tpu as pltpu
from jax.sharding import PartitionSpec as P

F32 = jnp.float32
BF16 = jnp.bfloat16
I32 = jnp.int32

HEADS = 12
WIDTH = 768
FF = 3072
REL_BUCKETS = 32
REL_REACH = 128
XY_BUCKETS = 64
XY_REACH = 256
VIS = 49
HALF = 64
ROWS = 64
KEYS = 256
CLASSES = 128
HIDE = 127
EPSILON = 1e-05
MASKED = -1e30
OUT_B, LN1_G, LN1_B, FFN_OUT_B, LN2_G, LN2_B, Q_B, V_B = range(8)
NT = (((1,), (1,)), ((), ()))
TN = (((0,), (0,)), ((), ()))
NN = (((1,), (0,)), ((), ()))


def far_away(*arrays):
    return [pltpu.with_memory_space_constraint(a, pltpu.HBM) for a in arrays]


def dot(a, b, dims=NN):
    return lax.dot_general(a, b, dims, preferred_element_type=F32)


def bucket_edges(buckets, reach):
    exact = buckets // 4
    spread = buckets // 2 - exact
    return [
        int(np.ceil(exact * (reach / exact) ** (level / spread) - 1e-09))
        for level in range(1, spread)
    ]


def bucket(offsets, buckets, reach):
    distance = jnp.abs(offsets)
    result = jnp.minimum(distance, float(buckets // 4))
    for edge in bucket_edges(buckets, reach):
        result = result + jnp.where(distance >= float(edge), 1.0, 0.0)
    return result + jnp.where(offsets > 0.0, float(buckets // 2), 0.0)


def iota(shape, axis):
    return lax.broadcasted_iota(I32, shape, axis)


def seventh(index):
    return lax.shift_right_logical(index * 37, 8)


def column_of(row):
    size = row.shape[1]
    shape = (size, size)
    spread = jnp.broadcast_to(row, shape)
    return jnp.sum(jnp.where(iota(shape, 0) == iota(shape, 1), spread, 0.0), axis=1, keepdims=True)


def stage_geometry(first_pos, band, x_own, line_own, kx_ref, kc_ref, blocks):
    extent = ROWS * blocks + 2 * HALF
    seq = x_own.shape[-1]
    half_seq = seq // 2

    def window(row):
        left = jnp.concatenate([jnp.zeros((1, HALF), I32), row[:, : extent - HALF]], axis=1)
        start = half_seq - HALF
        right = jnp.concatenate(
            [row[:, start:], jnp.zeros((1, extent - (seq - start)), I32)], axis=1
        )
        return jnp.where(band == 0, left, right)

    pos = first_pos - HALF + iota((1, extent), 1)
    visual = (pos >= 0) & (pos < VIS)
    seventh_pos = seventh(pos)
    x_row = jnp.where(visual, (pos - 7 * seventh_pos) * 142 + 71, window(x_own))
    c_row = jnp.where(visual, 64 + seventh_pos, window(line_own))
    lane = iota((1, HALF), 1)
    x_vis = (lane - 7 * seventh(lane)) * 142 + 71
    c_vis = 64 + seventh(lane)
    for i in range(blocks):
        cut = slice(ROWS * i, ROWS * i + 3 * HALF)
        kx_ref[i : i + 1, :] = jnp.concatenate([x_vis, x_row[:, cut]], axis=1).astype(F32)
        kc_ref[i : i + 1, :] = jnp.concatenate([c_vis, c_row[:, cut]], axis=1).astype(F32)


def key_positions(first_pos, i, shape):
    lane = iota(shape, 1)
    return jnp.where(
        lane < HALF,
        jnp.where(lane < VIS, lane, -1),
        first_pos + ROWS * i - 2 * HALF + lane,
    )


def allowed(first_pos, i, length):
    shape = (ROWS, KEYS)
    lane = iota(shape, 1)
    key = key_positions(first_pos, i, shape)
    query = first_pos + ROWS * i + iota(shape, 0)
    near = (key >= VIS) & (query >= VIS) & (jnp.abs(query - key) <= HALF)
    return (key >= 0) & (key < VIS + length) & ((lane < HALF) | near)


def rel_buckets(first_pos, i):
    shape = (ROWS, KEYS)
    key = key_positions(first_pos, i, shape)
    query = first_pos + ROWS * i + iota(shape, 0)
    return bucket((key - query).astype(F32), REL_BUCKETS, REL_REACH)


def class_y(index):
    return jnp.where(index < 64, 15 * index, 142 * (index - 64) + 71).astype(F32)


def lookup(table_row, index):
    shape = index.shape
    row = jnp.broadcast_to(table_row, (shape[0], 128))
    cuts = [
        jnp.take_along_axis(row, index[:, s : s + 128], axis=1) for s in range(0, shape[1], 128)
    ]
    return cuts[0] if len(cuts) == 1 else jnp.concatenate(cuts, axis=1)


def head_split(tile):
    low = iota(tile.shape, 1) < 64
    zero = jnp.zeros_like(tile)
    return jnp.concatenate([jnp.where(low, tile, zero), jnp.where(low, zero, tile)], axis=0)


def head_join(stack):
    rows = stack.shape[0] // 2
    low = iota((rows, stack.shape[1]), 1) < 64
    return jnp.where(low, stack[:rows], stack[rows:])


def key_tile(kv_ref, i, column):
    return jnp.concatenate(
        [
            kv_ref[0, 0:HALF, column : column + 128],
            kv_ref[0, pl.ds(pl.multiple_of(HALF + ROWS * i, ROWS), 3 * HALF), column : column + 128],
        ],
        axis=0,
    )


def attention_kernel(
    band_ref, len_ref, hid_ref, got_ref, x_ref, line_ref, w_ref, vec_ref, table_ref,
    ctx_ref, p_ref, q_ref, kv_ref, ext_ref,
    kx_ref, kc_ref, rb_ref, yb_ref, ctx_s, tab_ref,
):
    page = pl.program_id(0)
    band = band_ref[0]
    rows = hid_ref.shape[1]
    blocks = q_ref.shape[1] // ROWS
    first_pos = band * rows

    @pl.when(page == 0)
    def _():
        start = 0
        for slot, count in enumerate((REL_BUCKETS, XY_BUCKETS, XY_BUCKETS)):
            eye = jnp.where(iota((count, 128), 0) == iota((count, 128), 1), 1.0, 0.0).astype(BF16)
            turned = dot(table_ref[start : start + count, :], eye, TN)
            if slot == 1:
                turned = jnp.where(iota((HEADS, 128), 1) == HIDE, MASKED, turned)
            tab_ref[:HEADS, 128 * slot : 128 * slot + 128] = turned
            start += count
        for i in range(blocks):
            index = rel_buckets(first_pos, i).astype(I32)
            for h in range(HEADS):
                rb_ref[i, ROWS * h : ROWS * h + ROWS, :] = lookup(tab_ref[h : h + 1, 0:128], index)
        square = (CLASSES, CLASSES)
        gap = class_y(iota(square, 1)) - class_y(iota(square, 0))
        index = jnp.minimum(bucket(gap, XY_BUCKETS, XY_REACH), 63.0).astype(I32)
        for h in range(HEADS):
            yb_ref[:, CLASSES * h : CLASSES * h + CLASSES] = lookup(
                tab_ref[h : h + 1, 256:384], index
            ).astype(BF16)

    own = pl.ds(page, 1)
    stage_geometry(first_pos, band, x_ref[own, :], line_ref[own, :], kx_ref, kc_ref, blocks)
    ext_ref[0, :HALF] = jnp.where(band == 0, hid_ref[0, :HALF], got_ref[0, :HALF])
    ext_ref[0, HALF : 2 * HALF] = got_ref[0, HALF:]
    ext_ref[0, 2 * HALF :] = hid_ref[0]
    q_ref[0, 0:rows] = (
        (dot(hid_ref[0], w_ref[:, :WIDTH]) + vec_ref[Q_B : Q_B + 1, :].astype(F32)).astype(BF16).astype(F32)
        * 0.125
    ).astype(BF16)
    q_ref[0, rows:] = jnp.zeros((q_ref.shape[1] - rows, WIDTH), BF16)
    kv_ref[0, : 2 * HALF + rows, :WIDTH] = dot(ext_ref[0], w_ref[:, WIDTH : 2 * WIDTH]).astype(BF16)
    kv_ref[0, : 2 * HALF + rows, WIDTH:] = (
        dot(ext_ref[0], w_ref[:, 2 * WIDTH :]) + vec_ref[V_B : V_B + 1, :].astype(F32)
    ).astype(BF16)
    kv_ref[0, 2 * HALF + rows : 3 * HALF + rows] = kv_ref[0, HALF : 2 * HALF]
    tail = kv_ref.shape[1] - (3 * HALF + rows)
    kv_ref[0, 3 * HALF + rows :] = jnp.zeros((tail, 2 * WIDTH), BF16)

    def block(i, _):
        start = pl.multiple_of(ROWS * i, ROWS)
        kx = kx_ref[pl.ds(i, 1), :]
        kc = kc_ref[pl.ds(i, 1), :]
        gap = kx - column_of(kx[:, 2 * HALF : 3 * HALF])
        index = jnp.where(
            allowed(first_pos, i, len_ref[page]), bucket(gap, XY_BUCKETS, XY_REACH), float(HIDE)
        ).astype(I32)
        pick_q = jnp.where(
            iota((ROWS, CLASSES), 1).astype(F32) == column_of(kc[:, 2 * HALF : 3 * HALF]), 1.0, 0.0
        ).astype(BF16)
        pick_k = jnp.where(
            iota((KEYS, CLASSES), 1).astype(F32) == column_of(kc), 1.0, 0.0
        ).astype(BF16)
        pairs = range(HEADS // 2)
        scores = []
        for j in pairs:
            column = 128 * j
            queries = head_split(q_ref[0, pl.ds(start, ROWS), column : column + 128])
            picked = dot(pick_q, yb_ref[:, 2 * column : 2 * column + 256]).astype(BF16)
            picked = jnp.concatenate([picked[:, :128], picked[:, 128:]], axis=0)
            scores.append(
                dot(
                    jnp.concatenate([queries, picked], axis=1),
                    jnp.concatenate([key_tile(kv_ref, i, column), pick_k], axis=1),
                    NT,
                )
            )
        weights = []
        for j in pairs:
            x_bias = jnp.concatenate(
                [lookup(tab_ref[2 * j + e : 2 * j + e + 1, 128:256], index) for e in (0, 1)], axis=0
            )
            biased = scores[j] + rb_ref[i, 128 * j : 128 * j + 128, :] + x_bias
            peak = jnp.max(biased, axis=1, keepdims=True)
            raised = jnp.exp(biased - peak)
            weights.append(
                (raised * (1.0 / jnp.sum(raised, axis=1, keepdims=True))).astype(BF16)
            )
        contexts = [
            dot(weights[j], key_tile(kv_ref, i, WIDTH + 128 * j)) for j in pairs
        ]
        for j in pairs:
            p_ref[0, i, 128 * j : 128 * j + 128, :] = weights[j]
        ctx_s[pl.ds(start, ROWS), :] = jnp.concatenate(
            [head_join(c).astype(BF16) for c in contexts], axis=1
        )
        return 0

    lax.fori_loop(0, blocks, block, 0)
    ctx_ref[0] = ctx_s[:rows]


def page_block(*shape):
    return pl.BlockSpec((1,) + shape, lambda p, *_: (p,) + (0,) * len(shape))


def whole(*shape):
    return pl.BlockSpec(shape, lambda *_: (0,) * len(shape))


def attention_forward(
    band, lengths, hidden, got, x_coord, line_ids, qkv_w, vectors, tables
):
    pages, rows, width = hidden.shape
    blocks = -(-rows // ROWS)
    padded = blocks * ROWS
    ext = padded + 3 * HALF
    shape = jax.ShapeDtypeStruct
    return pl.pallas_call(
        attention_kernel,
        out_shape=(
            pltpu.HBM((pages, rows, width), BF16),
            pltpu.HBM((pages, blocks, HEADS * ROWS, KEYS), BF16),
            pltpu.HBM((pages, padded, width), BF16),
            pltpu.HBM((pages, ext, 2 * width), BF16),
            pltpu.HBM((pages, rows + 2 * HALF, width), BF16),
        ),
        grid_spec=pltpu.PrefetchScalarGridSpec(
            num_scalar_prefetch=2,
            grid=(pages,),
            in_specs=[
                page_block(rows, width),
                page_block(2 * HALF, width),
                whole(*x_coord.shape),
                whole(*line_ids.shape),
                whole(width, 3 * width),
                whole(*vectors.shape),
                whole(*tables.shape),
            ],
            out_specs=[
                page_block(rows, width),
                page_block(blocks, HEADS * ROWS, KEYS),
                page_block(padded, width),
                page_block(ext, 2 * width),
                page_block(rows + 2 * HALF, width),
            ],
            scratch_shapes=[
                pltpu.VMEM((8, KEYS), F32),
                pltpu.VMEM((8, KEYS), F32),
                pltpu.VMEM((blocks, HEADS * ROWS, KEYS), F32),
                pltpu.VMEM((CLASSES, HEADS * CLASSES), BF16),
                pltpu.VMEM((padded, width), BF16),
                pltpu.VMEM((16, 384), F32),
            ],
        ),
        compiler_params=pltpu.CompilerParams(vmem_limit_bytes=56 << 20),
        cost_estimate=pl.CostEstimate(
            flops=2 * pages * (rows + 2 * HALF) * width * 3 * width
            + 8 * pages * padded * HEADS * KEYS * 128,
            bytes_accessed=30 << 20,
            transcendentals=pages * padded * HEADS * KEYS,
        ),
        name="attention_forward",
    )(
        band, lengths, *far_away(hidden), got, x_coord, line_ids, *far_away(qkv_w), vectors, tables,
    )


def layer_norm(total):
    centred = total - jnp.mean(total, axis=1, keepdims=True)
    inverse = lax.rsqrt(jnp.mean(centred * centred, axis=1, keepdims=True) + EPSILON)
    return centred * inverse, inverse


def norm_back(grad, normed, inverse, gain):
    scaled = grad * gain
    return inverse * (
        scaled
        - jnp.mean(scaled, axis=1, keepdims=True)
        - normed * jnp.mean(scaled * normed, axis=1, keepdims=True)
    )


def gelu_parts(inner):
    size = jnp.abs(inner)
    falling = jnp.exp(inner * inner * -0.5)
    t = 1.0 / (1.0 + (0.3275911 * math.sqrt(0.5)) * size)
    poly = 1.061405429 * t - 1.453152027
    poly = poly * t + 1.421413741
    poly = poly * t - 0.284496736
    poly = poly * t + 0.254829592
    tail = (0.5 * poly) * (t * falling)
    share = jnp.where(inner >= 0.0, 1.0 - tail, tail)
    return inner * share, share + inner * falling * (2.0 * math.pi) ** (-0.5)


def column_sum(values):
    return jnp.sum(values, axis=0, keepdims=True)


def accumulate(ref, row, value):
    first = pl.program_id(0) == 0

    @pl.when(first)
    def _():
        ref[row : row + 1, :] = value

    @pl.when(jnp.logical_not(first))
    def _():
        ref[row : row + 1, :] = ref[row : row + 1, :] + value


def fixed(*shape):
    return pl.BlockSpec(shape, lambda *_: (0,) * len(shape), pipeline_mode=pl.Buffered(1))


def resident():
    return pl.BlockSpec(memory_space=pltpu.VMEM)


FORWARD_CUT = 768
CUT = 768
PART = 384


def ffn_forward_kernel(
    ctx_ref, hid_ref, cot_ref, vec_ref, bin_ref, wo_ref, w1_ref, w2_ref,
    out_ref, first_ref, norm_ref, inv_ref, act_ref, slope_ref, dh_ref, ds_ref, sums_ref,
    second_s,
):
    step = pl.program_id(0)

    def vector(row):
        return vec_ref[row : row + 1, :].astype(F32)

    @pl.when(step == 0)
    def _():
        attended = dot(ctx_ref[...], wo_ref[...]) + vector(OUT_B)
        normed, inverse = layer_norm(hid_ref[...].astype(F32) + attended)
        first = (normed * vector(LN1_G) + vector(LN1_B)).astype(BF16)
        first_ref[...] = first
        norm_ref[...] = normed
        inv_ref[...] = jnp.broadcast_to(inverse, inv_ref.shape)
        second_s[...] = first.astype(F32) + vector(FFN_OUT_B)

    first = first_ref[...]
    count = FORWARD_CUT // PART

    def inner_of(c):
        part = slice(PART * c, PART * c + PART)
        return dot(first, w1_ref[:, part]) + bin_ref[:, part].astype(F32)

    ahead = inner_of(0)
    for c in range(count):
        part = slice(PART * c, PART * c + PART)
        inner = ahead
        if c + 1 < count:
            ahead = inner_of(c + 1)
        act, slope = gelu_parts(inner)
        act_ref[:, part] = act.astype(BF16)
        slope_ref[:, part] = slope.astype(BF16)
    second_s[...] = second_s[...] + dot(act_ref[...], w2_ref[...])

    @pl.when(step == pl.num_programs(0) - 1)
    def _():
        normed2, inverse2 = layer_norm(second_s[...])
        out_ref[...] = (normed2 * vector(LN2_G) + vector(LN2_B)).astype(BF16)
        grad = cot_ref[...].astype(F32)
        back = norm_back(grad, normed2, inverse2, vector(LN2_G))
        low = back.astype(BF16)
        dh_ref[...] = back
        ds_ref[...] = low
        sums_ref[0:1, :] = column_sum(grad * normed2)
        sums_ref[1:2, :] = column_sum(grad)
        sums_ref[2:3, :] = column_sum(low.astype(F32))


def ffn_forward(context, hidden, cotangent, vectors, ffn_in_b, out_w, ffn_in_w, ffn_out_w):
    tokens, width = context.shape
    shape = jax.ShapeDtypeStruct
    rows = fixed(tokens, width)
    step = FORWARD_CUT
    wide = pl.BlockSpec((tokens, step), lambda i: (0, i))
    return pl.pallas_call(
        ffn_forward_kernel,
        out_shape=(
            pltpu.HBM((tokens, width), BF16),
            shape((tokens, width), BF16),
            shape((tokens, width), F32),
            shape((tokens, 128), F32),
            pltpu.HBM((tokens, FF), BF16),
            pltpu.HBM((tokens, FF), BF16),
            shape((tokens, width), F32),
            shape((tokens, width), BF16),
            shape((8, width), F32),
        ),
        grid=(FF // step,),
        in_specs=[
            rows, rows, rows,
            whole(*vectors.shape),
            pl.BlockSpec((1, step), lambda i: (0, i)),
            fixed(width, width),
            pl.BlockSpec((width, step), lambda i: (0, i)),
            pl.BlockSpec((step, width), lambda i: (i, 0)),
        ],
        out_specs=[
            rows, resident(), resident(), resident(),
            wide, wide, resident(), resident(),
            whole(8, width),
        ],
        scratch_shapes=[pltpu.VMEM((tokens, width), F32)],
        compiler_params=pltpu.CompilerParams(vmem_limit_bytes=36 << 20),
        cost_estimate=pl.CostEstimate(
            flops=2 * tokens * width * (2 * FF + width),
            bytes_accessed=40 << 20,
            transcendentals=tokens * FF,
        ),
        name="ffn_forward",
    )(
        *far_away(context, hidden, cotangent), vectors, ffn_in_b,
        *far_away(out_w, ffn_in_w, ffn_out_w),
    )


def ffn_parts(owner, ds_ref, first_ref, act_ref, slope_ref, w1_ref, w2_ref, parts_ref, bsum_ref):
    step = pl.program_id(0)
    chunks, size, _ = parts_ref.shape
    orders = split_orders(chunks)
    low = ds_ref[...]
    grad = dot(low, w2_ref[...], NT)
    inner = (grad * slope_ref[...].astype(F32)).astype(BF16)
    out_part = dot(act_ref[...], low, TN).astype(BF16)
    in_part = dot(inner, first_ref[...], TN).astype(BF16)
    bsum_ref[...] = column_sum(inner.astype(F32))
    for c in range(CUT // size):
        chunk = step * (CUT // size) + c
        spot = jnp.where(owner == 0, place(chunk, orders[0]), place(chunk, orders[1]))
        part = slice(size * c, size * c + size)
        parts_ref[spot] = jnp.concatenate([in_part[part], out_part[part]], axis=1)
    return dot(inner, w1_ref[...], NT)


def ffn_back_far_kernel(
    band_ref, ds_ref, first_ref, act_ref, slope_ref, w1_ref, w2_ref, dh_ref,
    parts_ref, bsum_ref, total_ref,
):
    added = ffn_parts(
        1 - band_ref[0], ds_ref, first_ref, act_ref, slope_ref, w1_ref, w2_ref, parts_ref, bsum_ref
    )

    @pl.when(pl.program_id(0) == 0)
    def _():
        total_ref[...] = dh_ref[...] + added

    @pl.when(pl.program_id(0) > 0)
    def _():
        total_ref[...] = total_ref[...] + added


def ffn_back_own_kernel(
    band_ref, ds_ref, first_ref, act_ref, slope_ref, w1_ref, w2_ref, part_ref, norm_ref, inv_ref,
    vec_ref, wo_ref,
    parts_ref, bsum_ref, dh1_ref, da_ref, dc_ref, sums_ref,
    total_s,
):
    added = ffn_parts(
        band_ref[0], ds_ref, first_ref, act_ref, slope_ref, w1_ref, w2_ref, parts_ref, bsum_ref
    )

    @pl.when(pl.program_id(0) == 0)
    def _():
        total_s[...] = part_ref[...] + added

    @pl.when(pl.program_id(0) > 0)
    def _():
        total_s[...] = total_s[...] + added

    @pl.when(pl.program_id(0) == pl.num_programs(0) - 1)
    def _():
        total = total_s[...]
        normed = norm_ref[...]
        gain = vec_ref[LN1_G : LN1_G + 1, :].astype(F32)
        back = norm_back(total, normed, inv_ref[:, 0:1], gain)
        low = back.astype(BF16)
        dh1_ref[...] = back
        da_ref[...] = low
        dc_ref[...] = dot(low, wo_ref[...], NT).astype(BF16)
        sums_ref[0:1, :] = column_sum(total * normed)
        sums_ref[1:2, :] = column_sum(total)
        sums_ref[2:3, :] = column_sum(low.astype(F32))


def ffn_back_call(own, band, second_low, first, act, slope, ffn_in_w, ffn_out_w, extra, chunks):
    tokens, width = second_low.shape
    half = FF // 2
    steps = half // CUT
    shape = jax.ShapeDtypeStruct
    rows = fixed(tokens, width)

    def at(i, b):
        return (b[0] if own else 1 - b[0]) * steps + i

    in_specs = [
        resident(), resident(),
        pl.BlockSpec((tokens, CUT), lambda i, b: (0, at(i, b))),
        pl.BlockSpec((tokens, CUT), lambda i, b: (0, at(i, b))),
        pl.BlockSpec((width, CUT), lambda i, b: (0, at(i, b))),
        pl.BlockSpec((CUT, width), lambda i, b: (at(i, b), 0)),
    ] + ([resident()] * 3 + [fixed(*e.shape) for e in extra[3:]] if own else [resident()])
    out_shape = [
        pltpu.HBM((chunks // 2, FF // chunks, 2 * width), BF16),
        shape((1, half), F32),
    ]
    out_specs = [
        fixed(chunks // 2, FF // chunks, 2 * width),
        pl.BlockSpec((1, CUT), lambda i, b: (0, i)),
    ]
    if own:
        out_shape += [
            pltpu.HBM((tokens, width), F32), pltpu.HBM((tokens, width), BF16),
            pltpu.HBM((tokens, width), BF16), shape((8, width), F32),
        ]
        out_specs += [rows, rows, rows, whole(8, width)]
    else:
        out_shape += [shape((tokens, width), F32)]
        out_specs += [resident()]
    return pl.pallas_call(
        ffn_back_own_kernel if own else ffn_back_far_kernel,
        out_shape=out_shape,
        grid_spec=pltpu.PrefetchScalarGridSpec(
            num_scalar_prefetch=1,
            grid=(steps,),
            in_specs=in_specs,
            out_specs=out_specs,
            scratch_shapes=[pltpu.VMEM((tokens, width), F32)] if own else [],
        ),
        compiler_params=pltpu.CompilerParams(vmem_limit_bytes=34 << 20),
        cost_estimate=pl.CostEstimate(
            flops=8 * tokens * width * half, bytes_accessed=30 << 20, transcendentals=0
        ),
        name="ffn_back_own" if own else "ffn_back_far",
    )(
        band, second_low, first, *far_away(act, slope, ffn_in_w, ffn_out_w),
        *(extra[:-1] + tuple(far_away(extra[-1])) if own else extra),
    )


def attention_back_kernel(
    p_ref, q_ref, kv_ref, dc_ref,
    dm_ref, ds_ref,
    dkv_ref, dc_s, dq_s,
):
    rows = dc_ref.shape[1]
    blocks = q_ref.shape[1] // ROWS
    dkv_ref[...] = jnp.zeros_like(dkv_ref)
    dc_s[:rows] = dc_ref[0]
    dc_s[rows:] = jnp.zeros((dc_s.shape[0] - rows, WIDTH), BF16)
    def block(i, _):
        start = pl.multiple_of(ROWS * i, ROWS)
        window = pl.ds(pl.multiple_of(HALF + ROWS * i, ROWS), 3 * HALF)
        pairs = range(HEADS // 2)
        grads = []
        for j in pairs:
            column = 128 * j
            grads.append(head_split(dc_s[pl.ds(start, ROWS), column : column + 128]))
        dprobs = [dot(grads[j], key_tile(kv_ref, i, WIDTH + 128 * j), NT) for j in pairs]
        for j in pairs:
            dv = dot(p_ref[0, i, 128 * j : 128 * j + 128, :], grads[j], TN)
            column = WIDTH + 128 * j
            cut = slice(column, column + 128)
            dkv_ref[0:HALF, cut] = dkv_ref[0:HALF, cut] + dv[:HALF]
            dkv_ref[window, cut] = dkv_ref[window, cut] + dv[HALF:]
        lows = []
        for j in pairs:
            probs = p_ref[0, i, 128 * j : 128 * j + 128, :].astype(F32)
            grad = probs * (
                dprobs[j] - jnp.sum(probs * dprobs[j], axis=1, keepdims=True)
            )
            lows.append(grad.astype(BF16))
        dq = [head_join(dot(lows[j], key_tile(kv_ref, i, 128 * j))) for j in pairs]
        dq_s[pl.ds(start, ROWS), :] = (jnp.concatenate(dq, axis=1) * 0.125).astype(BF16)
        for j in pairs:
            cut = slice(128 * j, 128 * j + 128)
            dk = dot(lows[j], head_split(q_ref[0, pl.ds(start, ROWS), cut]), TN)
            dkv_ref[0:HALF, cut] = dkv_ref[0:HALF, cut] + dk[:HALF]
            dkv_ref[window, cut] = dkv_ref[window, cut] + dk[HALF:]

        for j in pairs:
            ds_ref[0, i, 128 * j : 128 * j + 128, :] = lows[j]
        return 0

    lax.fori_loop(0, blocks, block, 0)
    dm_ref[0, : 2 * HALF, :WIDTH] = jnp.zeros((2 * HALF, WIDTH), BF16)
    dm_ref[0, 2 * HALF :, :WIDTH] = dq_s[:rows]
    dm_ref[0, :HALF, WIDTH:] = dkv_ref[:HALF].astype(BF16)
    dm_ref[0, HALF : 2 * HALF, WIDTH:] = (
        dkv_ref[HALF : 2 * HALF] + dkv_ref[2 * HALF + rows : 3 * HALF + rows]
    ).astype(BF16)
    dm_ref[0, 2 * HALF :, WIDTH:] = dkv_ref[2 * HALF : 2 * HALF + rows].astype(BF16)


def attention_backward(probs, queries, pairs, grad_context):
    pages, rows, width = grad_context.shape
    padded = queries.shape[1]
    blocks = padded // ROWS
    ext = pairs.shape[1]
    shape = jax.ShapeDtypeStruct
    return pl.pallas_call(
        attention_back_kernel,
        out_shape=(
            pltpu.HBM((pages, rows + 2 * HALF, 3 * width), BF16),
            pltpu.HBM(probs.shape, BF16),
        ),
        grid=(pages,),
        in_specs=[
            page_block(blocks, HEADS * ROWS, KEYS),
            page_block(padded, width),
            page_block(ext, 2 * width),
            page_block(rows, width),
        ],
        out_specs=[page_block(rows + 2 * HALF, 3 * width), page_block(blocks, HEADS * ROWS, KEYS)],
        scratch_shapes=[
            pltpu.VMEM((ext, 2 * width), F32),
            pltpu.VMEM((padded, width), BF16),
            pltpu.VMEM((padded, width), BF16),
        ],
        compiler_params=pltpu.CompilerParams(vmem_limit_bytes=56 << 20),
        cost_estimate=pl.CostEstimate(
            flops=10 * pages * padded * HEADS * KEYS * 128, bytes_accessed=30 << 20, transcendentals=0
        ),
        name="attention_backward",
    )(*far_away(probs, queries, pairs, grad_context))


def table_kernel(
    band_ref, page_ref, ds_ref, x_ref, line_ref, tab_ref, kx_ref, kc_ref, left_ref, right_ref,
    index_ref,
):
    page = page_ref[0]
    band = band_ref[0]
    blocks = ds_ref.shape[1]
    first_pos = band * (x_ref.shape[-1] // 2)
    own_page = pl.ds(page, 1)
    stage_geometry(first_pos, band, x_ref[own_page, :], line_ref[own_page, :], kx_ref, kc_ref, blocks)
    slots = iota((REL_BUCKETS + 2 * XY_BUCKETS, KEYS), 0).astype(F32).astype(BF16)
    one = jnp.ones((), BF16)
    zero = jnp.zeros((), BF16)

    def block(i, table_sum):
        left_ref[...] = ds_ref[0, i, :, :128].astype(F32)
        right_ref[...] = ds_ref[0, i, :, 128:].astype(F32)
        kx = kx_ref[pl.ds(i, 1), :]
        ky = class_y(kc_ref[pl.ds(i, 1), :].astype(I32))
        index_ref[0:ROWS] = bucket(kx - column_of(kx[:, 2 * HALF : 3 * HALF]), XY_BUCKETS, XY_REACH)
        index_ref[ROWS : 2 * ROWS] = 64.0 + bucket(
            ky - column_of(ky[:, 2 * HALF : 3 * HALF]), XY_BUCKETS, XY_REACH
        )
        index_ref[2 * ROWS : 3 * ROWS] = 128.0 + rel_buckets(first_pos, i)

        def table_row(q, acc):
            own = jnp.concatenate(
                [
                    jnp.broadcast_to(index_ref[pl.ds(q, 1), :], (XY_BUCKETS, KEYS)),
                    jnp.broadcast_to(index_ref[pl.ds(ROWS + q, 1), :], (XY_BUCKETS, KEYS)),
                    jnp.broadcast_to(index_ref[pl.ds(2 * ROWS + q, 1), :], (REL_BUCKETS, KEYS)),
                ],
                axis=0,
            ).astype(BF16)
            heads = jnp.concatenate(
                [
                    left_ref[pl.ds(q, HEADS, stride=ROWS), :],
                    right_ref[pl.ds(q, HEADS, stride=ROWS), :],
                ],
                axis=1,
            ).astype(BF16)
            return acc + dot(heads, jnp.where(slots == own, one, zero), NT)

        return lax.fori_loop(0, ROWS, table_row, table_sum, unroll=ROWS)

    table_sum = lax.fori_loop(
        0, blocks, block, jnp.zeros((HEADS, REL_BUCKETS + 2 * XY_BUCKETS), F32)
    )

    tab_ref[...] = table_sum


def table_sums(band, page, grad_scores, x_coord, line_ids):
    pages, blocks, height, keys = grad_scores.shape
    buckets = REL_BUCKETS + 2 * XY_BUCKETS
    return pl.pallas_call(
        table_kernel,
        out_shape=jax.ShapeDtypeStruct((HEADS, buckets), F32),
        grid_spec=pltpu.PrefetchScalarGridSpec(
            num_scalar_prefetch=2,
            grid=(1,),
            in_specs=[
                pl.BlockSpec((1, blocks, height, keys), lambda i, *_: (page, 0, 0, 0)),
                whole(*x_coord.shape),
                whole(*line_ids.shape),
            ],
            out_specs=whole(HEADS, buckets),
            scratch_shapes=[
                pltpu.VMEM((8, KEYS), F32),
                pltpu.VMEM((8, KEYS), F32),
                pltpu.VMEM((height, 128), F32),
                pltpu.VMEM((height, 128), F32),
                pltpu.VMEM((3 * ROWS, KEYS), F32),
            ],
        ),
        compiler_params=pltpu.CompilerParams(vmem_limit_bytes=60 << 20),
        cost_estimate=pl.CostEstimate(
            flops=60 * blocks * height * keys * 32, bytes_accessed=2 << 20, transcendentals=0
        ),
        name="table_sums",
    )(band, jnp.full((1,), page, I32), *far_away(grad_scores), x_coord, line_ids)


def hidden_back_kernel(dm_ref, dh_ref, w_ref, own_ref, far_ref, sums_ref):
    accumulate(sums_ref, 0, column_sum(dm_ref[0].astype(F32)))
    own_ref[0] = dh_ref[0] + dot(dm_ref[0, 2 * HALF :], w_ref[...], NT)
    far_ref[0] = dot(dm_ref[0, : 2 * HALF, WIDTH:], w_ref[:, WIDTH:], NT).astype(BF16)


def hidden_backward(grad_mixed, grad_total, qkv_w):
    pages, rows, width = grad_total.shape
    shape = jax.ShapeDtypeStruct
    return pl.pallas_call(
        hidden_back_kernel,
        out_shape=(
            pltpu.HBM((pages, rows, width), F32),
            pltpu.HBM((pages, 2 * HALF, width), BF16),
            shape((8, 3 * width), F32),
        ),
        grid=(pages,),
        in_specs=[
            page_block(rows + 2 * HALF, 3 * width),
            page_block(rows, width),
            whole(width, 3 * width),
        ],
        out_specs=[page_block(rows, width), page_block(2 * HALF, width), whole(8, 3 * width)],
        compiler_params=pltpu.CompilerParams(vmem_limit_bytes=60 << 20),
        cost_estimate=pl.CostEstimate(
            flops=2 * pages * rows * width * 3 * width, bytes_accessed=15 << 20, transcendentals=0
        ),
        name="hidden_backward",
    )(*far_away(grad_mixed, grad_total, qkv_w))


def edge_kernel(band_ref, grad_ref, far_ref, got_ref, out_ref):
    band = band_ref[0]
    side = pl.program_id(0)
    edge = HALF // 2
    for s in range(4):

        @pl.when(side == s)
        def _():
            part = slice(edge * (s % 2), edge * (s % 2) + edge)
            rim = slice(HALF + part.start, HALF + part.stop)
            if s < 2:
                own = far_ref[:, part].astype(F32) + got_ref[:, part].astype(F32)
                added = jnp.where(band == 0, own, got_ref[:, rim].astype(F32))
            else:
                added = jnp.where(band == 0, got_ref[:, rim].astype(F32), 0.0)
            out_ref[...] = grad_ref[...] + added


def edge_add(band, grad, far, got):
    pages, rows, width = grad.shape
    half = HALF // 2
    last = rows // half - 2

    def edge(s, *_):
        return (0, jnp.where(s < 2, s, last + s - 2), 0)

    return pl.pallas_call(
        edge_kernel,
        out_shape=jax.ShapeDtypeStruct(grad.shape, F32),
        grid_spec=pltpu.PrefetchScalarGridSpec(
            num_scalar_prefetch=1,
            grid=(4,),
            in_specs=[
                pl.BlockSpec((pages, half, width), edge),
                whole(*far.shape),
                whole(*got.shape),
            ],
            out_specs=pl.BlockSpec((pages, half, width), edge),
        ),
        input_output_aliases={1: 0},
        name="edge_add",
    )(band, grad, far, got)


def split_orders(count):
    total = count.bit_length() - 1
    side = total // 3
    x, y, z = (range(side), range(side, 2 * side), range(2 * side, total))
    near, far = list(z)[:-1], list(z)[-1:]
    return list(x) + list(y) + near + far, list(y) + near + list(x) + far


def place(chunk, order):
    spot = 0
    for level, bit in enumerate(order):
        spot = spot + (((chunk >> bit) & 1) << (len(order) - 1 - level))
    return spot


def product_halves(band, tokens_ext, grad_mixed, context, grad_attn):
    tokens, height = tokens_ext.shape
    width = grad_mixed.shape[1]
    step = height // 2

    def kernel(band_ref, l_ref, r_ref, l2_ref, r2_ref, send_ref, keep_ref):
        def write(ref):
            ref[:, :width] = dot(l_ref[...], r_ref[...], TN).astype(BF16)
            ref[:, width:] = dot(l2_ref[...], r2_ref[...], TN).astype(BF16)

        pl.when(pl.program_id(0) == 0)(lambda: write(send_ref))
        pl.when(pl.program_id(0) == 1)(lambda: write(keep_ref))

    def at(i, b):
        return (0, jnp.where(i == 0, 1 - b[0], b[0]))

    out = pltpu.HBM((step, width + height), BF16)
    return pl.pallas_call(
        kernel,
        out_shape=(out, out),
        grid_spec=pltpu.PrefetchScalarGridSpec(
            num_scalar_prefetch=1,
            grid=(2,),
            in_specs=[
                pl.BlockSpec((tokens, step), at),
                fixed(*grad_mixed.shape),
                pl.BlockSpec((context.shape[0], step), at),
                fixed(*grad_attn.shape),
            ],
            out_specs=[fixed(step, width + height), fixed(step, width + height)],
        ),
        compiler_params=pltpu.CompilerParams(vmem_limit_bytes=60 << 20),
        cost_estimate=pl.CostEstimate(
            flops=2 * tokens * height * (width + height), bytes_accessed=16 << 20, transcendentals=0
        ),
        name="product_halves",
    )(band, *far_away(tokens_ext, grad_mixed, context, grad_attn))


def swap_bands(block):
    return lax.ppermute(block, "band", [(0, 1), (1, 0)])


def swap_pages(block, level, orders):
    count = lax.axis_size("page")
    route = [
        (b * count + p, b * count + (p ^ (1 << orders[b][level])))
        for b in range(2)
        for p in range(count)
    ]
    return lax.ppermute(block, ("band", "page"), route)


def sides(orders):
    band, page = lax.axis_index("band"), lax.axis_index("page")
    return [
        jnp.where(band == 0, (page >> first) & 1, (page >> second) & 1)
        for first, second in zip(*orders)
    ]


def widen(band, block, own, outs, shapes):
    half, width = block.shape
    steps = 4
    step = half // steps
    edges = [sum(shape[1] for shape in shapes[:i]) for i in range(len(shapes) + 1)]

    def kernel(band_ref, block_ref, *refs):
        for out, start, stop in zip(refs[-len(shapes) :], edges, edges[1:]):
            out[...] = block_ref[:, start:stop].astype(F32)

    def at(i, b):
        return ((b[0] if own else 1 - b[0]) * steps + i, 0)

    return pl.pallas_call(
        kernel,
        out_shape=[pltpu.HBM(shape, F32) for shape in shapes],
        grid_spec=pltpu.PrefetchScalarGridSpec(
            num_scalar_prefetch=1,
            grid=(steps,),
            in_specs=[pl.BlockSpec((step, width), lambda i, *_: (i, 0))]
            + [pl.BlockSpec(memory_space=pl.ANY)] * len(outs),
            out_specs=[pl.BlockSpec((step, shape[1]), at) for shape in shapes],
        ),
        input_output_aliases={2 + i: i for i in range(len(outs))},
        compiler_params=pltpu.CompilerParams(vmem_limit_bytes=40 << 20),
        name="widen",
    )(band, *far_away(block), *outs)


class Order:
    def __init__(self):
        self.mark = None

    def __call__(self, part, *args):
        if self.mark is not None:
            leaves, tree = jax.tree.flatten(args)
            leaves = lax.optimization_barrier((*leaves, self.mark))[:-1]
            args = jax.tree.unflatten(tree, leaves)
        out = part(*args)
        self.mark = jax.tree.leaves(out)[0]
        return out


def halving_plan(size):
    starts, spots = [], [[0, 0]]
    for side in sides(split_orders(lax.axis_size("page"))):
        size = size // 2
        starts.append([at + (1 - side) * size for at in spots[-1]])
        spots.append([at + side * size for at in spots[-1]] + [0])
    return starts, spots


class Halving:
    def __init__(self, order, send, keep, plan):
        self.order = order
        self.orders = split_orders(lax.axis_size("page"))
        self.starts, self.spots, self.sides = plan
        self.level = 0
        self.held = [keep]
        self.size = keep.shape[0]
        self.flight = swap_bands(send)

    def land(self):
        self.held.append(self.flight)
        self.flight = None

    def total(self, size):
        def add(spots, *held):
            parts = [
                lax.dynamic_slice_in_dim(block, at, size, 0, allow_negative_indices=False)
                for block, at in zip(held, spots)
            ]
            return sum([part.astype(F32) for part in parts[1:]], parts[0].astype(F32))

        return add

    def step(self):
        self.land()
        self.size //= 2
        add = self.total(self.size)
        sent = self.order(
            lambda *a: add(*a).astype(BF16), self.starts[self.level], *self.held
        )
        self.flight = swap_pages(sent, self.level, self.orders)
        self.level += 1

    def finish(self, wrap):
        self.land()
        add = self.total(self.size)
        return self.order(lambda *a: wrap(add(*a)), self.spots[self.level], *self.held)

    def meet(self):
        self.land()
        add = self.total(self.size)
        mine = self.order(lambda *a: add(*a).astype(BF16), self.spots[self.level], *self.held)
        self.flight = swap_pages(mine, self.level, self.orders)
        self.mine = mine

    def met(self):
        self.mine = self.order(
            lambda a, b: (a.astype(F32) + b.astype(F32)).astype(BF16), self.mine, self.flight
        )
        self.level -= 1
        self.flight = swap_pages(self.mine, self.level, self.orders)

    def grow(self):
        self.mine = self.order(join, self.mine, self.flight, self.sides[self.level])
        self.level -= 1
        if self.level >= 0:
            self.flight = swap_pages(self.mine, self.level, self.orders)
        else:
            self.flight = swap_bands(self.mine)


def join(mine, other, side):
    return jnp.where(
        side == 0,
        jnp.concatenate([mine, other], axis=0),
        jnp.concatenate([other, mine], axis=0),
    )


def flat(block):
    return block.reshape(-1, block.shape[-1])


def local(
    hidden, cotangent, page_lengths, x_coord, line_ids, qkv_w, q_bias, v_bias,
    rel_table, x_table, y_table, out_w, out_b, ln1_gain, ln1_bias,
    ffn_in_w, ffn_in_b, ffn_out_w, ffn_out_b, ln2_gain, ln2_bias,
):
    pages, rows, width = hidden.shape
    band = lax.axis_index("band")
    chunks = 2 * lax.axis_size("page")
    band_arr = band.reshape(1).astype(I32)
    own_edge = jnp.where(band == 0, hidden[:, rows - HALF :], hidden[:, :HALF])
    got = swap_bands(jnp.concatenate([hidden[:, :HALF], own_edge], axis=1))
    half = chunks // 2
    places = sides(split_orders(half))
    plans = [(*halving_plan(size), places) for size in (half, width // 2)]
    got, plans = lax.optimization_barrier((got, plans))
    ffn_plan, attn_plan = plans
    vectors = jnp.concatenate(
        [out_b, ln1_gain, ln1_bias, ffn_out_b, ln2_gain, ln2_bias, q_bias, v_bias]
    ).reshape(8, width)
    tables = jnp.concatenate([rel_table, x_table, y_table], axis=0)
    context, probs, queries, pairs, extended = attention_forward(
        band_arr, page_lengths, hidden, got, x_coord, line_ids, qkv_w, vectors, tables
    )
    output, first, normed, inverse, act, slope, grad_total2, second_low, sums2 = ffn_forward(
        flat(context), flat(hidden), flat(cotangent), vectors,
        ffn_in_b.reshape(1, FF), out_w, ffn_in_w, ffn_out_w,
    )
    order = Order()
    send, bsum_far, part = order(
        lambda *a: ffn_back_call(False, band_arr, *a, chunks),
        second_low, first, act, slope, ffn_in_w, ffn_out_w, (grad_total2,),
    )
    keep, bsum_own, grad_total1, attn_low, grad_context, sums1 = order(
        lambda *a: ffn_back_call(True, band_arr, *a, chunks),
        second_low, first, act, slope, ffn_in_w, ffn_out_w,
        (part, normed, inverse, vectors, out_w),
    )
    ffn = Halving(order, send, keep, ffn_plan)
    ffn.step()
    grad_mixed, grad_scores = order(
        attention_backward, probs, queries, pairs, grad_context.reshape(pages, rows, width)
    )
    send, keep = order(
        product_halves, band_arr, flat(extended), flat(grad_mixed), flat(context), attn_low
    )
    attn = Halving(order, send, keep, attn_plan)
    ffn.step()
    attn.step()
    grad_hidden, far, mixed_sums = order(
        hidden_backward, grad_mixed, grad_total1.reshape(pages, rows, width), qkv_w
    )
    far_got = swap_bands(far)

    def tables_of(page):
        return order(lambda *a: table_sums(band_arr, page, *a), grad_scores, x_coord, line_ids)

    tables = [tables_of(0)]
    attn.step()
    ffn.step()
    tables.append(tables_of(1))
    attn.step()
    ffn.step()
    grad_hidden = order(edge_add, band_arr, grad_hidden, far, far_got)
    attn.meet()
    tables.append(tables_of(2))
    inner_sums = jnp.where(
        band == 0,
        jnp.concatenate([bsum_own, bsum_far], axis=1),
        jnp.concatenate([bsum_far, bsum_own], axis=1),
    )
    small = order(
        lambda m, a, b, c, *t: jnp.concatenate(
            [
                m[0].reshape(3, width), a[:3], b[:3], c.reshape(FF // width, width),
                jnp.pad(sum(t[1:], t[0]), ((0, 3), (0, width - t[0].shape[1]))),
            ],
            axis=0,
        ),
        mixed_sums, sums1, sums2, inner_sums, *tables,
    )
    small_got = swap_bands(small)
    attn.met()
    ffn_in_share, ffn_out_share = ffn.finish(
        lambda total: (total[0, :, :width].T, total[0, :, width:])
    )
    orders = split_orders(lax.axis_size("page"))
    for level in range(len(orders[0])):
        small = order(lambda a, b: a + b, small, small_got)
        small_got = swap_pages(small, level, orders)
        if attn.level > 0:
            attn.grow()
    while attn.level >= 0:
        attn.grow()
    shapes = ((width, 3 * width), (width, width))
    halves = order(lambda mine: widen(band_arr, mine, True, (), shapes), attn.mine)
    small = order(lambda a, b: a + b, small, small_got)
    grad_qkv, grad_out = order(
        lambda other, *outs: widen(band_arr, other, False, outs, shapes), attn.flight, *halves
    )
    tables = small[13 : 13 + HEADS]
    return (
        output.reshape(hidden.shape),
        grad_hidden,
        grad_qkv,
        small[0],
        small[2],
        tables[:, 128:160].T,
        tables[:, :64].T,
        tables[:, 64:128].T,
        grad_out,
        small[5],
        small[3],
        small[4],
        ffn_in_share,
        small[9:13].reshape(FF),
        ffn_out_share,
        small[8],
        small[6],
        small[7],
    )


def solution(mesh):
    in_specs = (
        P("page", "band", None),
        P("page", "band", None),
        P("page"),
        P("page", None),
        P("page", None),
        P(),
        P(),
        P(),
        P(),
        P(),
        P(),
        P(),
        P(),
        P(),
        P(),
        P(),
        P(),
        P(),
        P(),
        P(),
        P(),
    )
    out_specs = (
        P("page", "band", None),
        P("page", "band", None),
        P(),
        P(),
        P(),
        P(),
        P(),
        P(),
        P(),
        P(),
        P(),
        P(),
        P(None, ("band", "page")),
        P(),
        P(("band", "page"), None),
        P(),
        P(),
        P(),
    )
    return jax.shard_map(local, mesh=mesh, in_specs=in_specs, out_specs=out_specs, check_vma=False)
```

```python
import functools
import math

import jax
import jax.numpy as jnp
import numpy as np
from jax import lax
from jax.experimental import pallas as pl
from jax.experimental.pallas import tpu as pltpu
from jax.sharding import PartitionSpec as P

F32 = jnp.float32
BF16 = jnp.bfloat16
I32 = jnp.int32

HEADS = 12
WIDTH = 768
FF = 3072
REL_BUCKETS = 32
REL_REACH = 128
XY_BUCKETS = 64
XY_REACH = 256
VIS = 49
HALF = 64
ROWS = 64
KEYS = 256
CLASSES = 128
HIDE = 127
EPSILON = 1e-05
MASKED = -1e30
OUT_B, LN1_G, LN1_B, FFN_OUT_B, LN2_G, LN2_B, Q_B, V_B = range(8)
BRIEF = pl.CostEstimate(flops=1, bytes_accessed=1, transcendentals=0)
NT = (((1,), (1,)), ((), ()))
TN = (((0,), (0,)), ((), ()))
NN = (((1,), (0,)), ((), ()))


def far_away(*arrays):
    return [pltpu.with_memory_space_constraint(a, pltpu.HBM) for a in arrays]


def dot(a, b, dims=NN):
    return lax.dot_general(a, b, dims, preferred_element_type=F32)


def bucket_edges(buckets, reach):
    exact = buckets // 4
    spread = buckets // 2 - exact
    return [
        int(np.ceil(exact * (reach / exact) ** (level / spread) - 1e-09))
        for level in range(1, spread)
    ]


def bucket(offsets, buckets, reach):
    distance = jnp.abs(offsets)
    result = jnp.minimum(distance, float(buckets // 4))
    for edge in bucket_edges(buckets, reach):
        result = result + jnp.where(distance >= float(edge), 1.0, 0.0)
    return result + jnp.where(offsets > 0.0, float(buckets // 2), 0.0)


def iota(shape, axis):
    return lax.broadcasted_iota(I32, shape, axis)


def seventh(index):
    return lax.shift_right_logical(index * 37, 8)


def column_of(row):
    size = row.shape[1]
    shape = (size, size)
    spread = jnp.broadcast_to(row, shape)
    return jnp.sum(jnp.where(iota(shape, 0) == iota(shape, 1), spread, 0.0), axis=1, keepdims=True)


def stage_geometry(first_pos, band, x_own, line_own, kx_ref, kc_ref, blocks):
    extent = ROWS * blocks + 2 * HALF
    seq = x_own.shape[-1]
    half_seq = seq // 2

    def window(row):
        left = jnp.concatenate([jnp.zeros((1, HALF), I32), row[:, : extent - HALF]], axis=1)
        start = half_seq - HALF
        right = jnp.concatenate(
            [row[:, start:], jnp.zeros((1, extent - (seq - start)), I32)], axis=1
        )
        return jnp.where(band == 0, left, right)

    pos = first_pos - HALF + iota((1, extent), 1)
    visual = (pos >= 0) & (pos < VIS)
    seventh_pos = seventh(pos)
    x_row = jnp.where(visual, (pos - 7 * seventh_pos) * 142 + 71, window(x_own))
    c_row = jnp.where(visual, 64 + seventh_pos, window(line_own))
    lane = iota((1, HALF), 1)
    x_vis = (lane - 7 * seventh(lane)) * 142 + 71
    c_vis = 64 + seventh(lane)
    for i in range(blocks):
        cut = slice(ROWS * i, ROWS * i + 3 * HALF)
        kx_ref[i : i + 1, :] = jnp.concatenate([x_vis, x_row[:, cut]], axis=1).astype(F32)
        kc_ref[i : i + 1, :] = jnp.concatenate([c_vis, c_row[:, cut]], axis=1).astype(F32)


def key_positions(first_pos, i, shape):
    lane = iota(shape, 1)
    return jnp.where(
        lane < HALF,
        jnp.where(lane < VIS, lane, -1),
        first_pos + ROWS * i - 2 * HALF + lane,
    )


def allowed(first_pos, i, length):
    shape = (ROWS, KEYS)
    lane = iota(shape, 1)
    key = key_positions(first_pos, i, shape)
    query = first_pos + ROWS * i + iota(shape, 0)
    near = (key >= VIS) & (query >= VIS) & (jnp.abs(query - key) <= HALF)
    return (key >= 0) & (key < VIS + length) & ((lane < HALF) | near)


def rel_buckets(first_pos, i):
    shape = (ROWS, KEYS)
    key = key_positions(first_pos, i, shape)
    query = first_pos + ROWS * i + iota(shape, 0)
    return bucket((key - query).astype(F32), REL_BUCKETS, REL_REACH)


def class_y(index):
    return jnp.where(index < 64, 15 * index, 142 * (index - 64) + 71).astype(F32)


def lookup(table_row, index):
    shape = index.shape
    row = jnp.broadcast_to(table_row, (shape[0], 128))
    cuts = [
        jnp.take_along_axis(row, index[:, s : s + 128], axis=1) for s in range(0, shape[1], 128)
    ]
    return cuts[0] if len(cuts) == 1 else jnp.concatenate(cuts, axis=1)


def head_split(tile):
    low = iota(tile.shape, 1) < 64
    zero = jnp.zeros_like(tile)
    return jnp.concatenate([jnp.where(low, tile, zero), jnp.where(low, zero, tile)], axis=0)


def head_join(stack):
    rows = stack.shape[0] // 2
    low = iota((rows, stack.shape[1]), 1) < 64
    return jnp.where(low, stack[:rows], stack[rows:])


def key_tile(kv_ref, i, column):
    return jnp.concatenate(
        [
            kv_ref[0, 0:HALF, column : column + 128],
            kv_ref[0, pl.ds(pl.multiple_of(HALF + ROWS * i, ROWS), 3 * HALF), column : column + 128],
        ],
        axis=0,
    )


def attention_kernel(
    band_ref, len_ref, hid_ref, got_ref, x_ref, line_ref, w_ref, vec_ref, table_ref,
    ctx_ref, p_ref, q_ref, kv_ref, ext_ref,
    kx_ref, kc_ref, rb_ref, yb_ref, ctx_s, tab_ref,
):
    page = pl.program_id(0)
    band = band_ref[0]
    rows = hid_ref.shape[1]
    blocks = q_ref.shape[1] // ROWS
    first_pos = band * rows

    @pl.when(page == 0)
    def _():
        start = 0
        for slot, count in enumerate((REL_BUCKETS, XY_BUCKETS, XY_BUCKETS)):
            eye = jnp.where(iota((count, 128), 0) == iota((count, 128), 1), 1.0, 0.0).astype(BF16)
            turned = dot(table_ref[start : start + count, :], eye, TN)
            if slot == 1:
                turned = jnp.where(iota((HEADS, 128), 1) == HIDE, MASKED, turned)
            tab_ref[:HEADS, 128 * slot : 128 * slot + 128] = turned
            start += count
        for i in range(blocks):
            index = rel_buckets(first_pos, i).astype(I32)
            for h in range(HEADS):
                part = slice(ROWS * h, ROWS * h + ROWS)
                if i == 0:
                    rb_ref[i, part, :] = lookup(tab_ref[h : h + 1, 0:128], index)
                else:
                    rb_ref[i, part, :128] = lookup(tab_ref[h : h + 1, 0:128], index[:, :128])
                    rb_ref[i, part, 128:] = rb_ref[0, part, 128:]
        square = (CLASSES, CLASSES)
        gap = class_y(iota(square, 1)) - class_y(iota(square, 0))
        index = jnp.minimum(bucket(gap, XY_BUCKETS, XY_REACH), 63.0).astype(I32)
        for h in range(HEADS):
            yb_ref[:, CLASSES * h : CLASSES * h + CLASSES] = lookup(
                tab_ref[h : h + 1, 256:384], index
            ).astype(BF16)

    own = pl.ds(page, 1)
    stage_geometry(first_pos, band, x_ref[own, :], line_ref[own, :], kx_ref, kc_ref, blocks)
    ext_ref[0, :HALF] = jnp.where(band == 0, hid_ref[0, :HALF], got_ref[0, :HALF])
    ext_ref[0, HALF : 2 * HALF] = got_ref[0, HALF:]
    ext_ref[0, 2 * HALF :] = hid_ref[0]
    q_ref[0, 0:rows] = (
        (dot(hid_ref[0], w_ref[:, :WIDTH]) + vec_ref[Q_B : Q_B + 1, :].astype(F32)).astype(BF16).astype(F32)
        * 0.125
    ).astype(BF16)
    q_ref[0, rows:] = jnp.zeros((q_ref.shape[1] - rows, WIDTH), BF16)
    kv_ref[0, : 2 * HALF + rows, :WIDTH] = dot(ext_ref[0], w_ref[:, WIDTH : 2 * WIDTH]).astype(BF16)
    kv_ref[0, : 2 * HALF + rows, WIDTH:] = (
        dot(ext_ref[0], w_ref[:, 2 * WIDTH :]) + vec_ref[V_B : V_B + 1, :].astype(F32)
    ).astype(BF16)
    kv_ref[0, 2 * HALF + rows : 3 * HALF + rows] = kv_ref[0, HALF : 2 * HALF]
    tail = kv_ref.shape[1] - (3 * HALF + rows)
    kv_ref[0, 3 * HALF + rows :] = jnp.zeros((tail, 2 * WIDTH), BF16)

    def block(i, _):
        start = pl.multiple_of(ROWS * i, ROWS)
        kx = kx_ref[pl.ds(i, 1), :]
        kc = kc_ref[pl.ds(i, 1), :]
        gap = kx - column_of(kx[:, 2 * HALF : 3 * HALF])
        index = jnp.where(
            allowed(first_pos, i, len_ref[page]), bucket(gap, XY_BUCKETS, XY_REACH), float(HIDE)
        ).astype(I32)
        pick_q = jnp.where(
            iota((ROWS, CLASSES), 1).astype(F32) == column_of(kc[:, 2 * HALF : 3 * HALF]), 1.0, 0.0
        ).astype(BF16)
        pick_k = jnp.where(
            iota((KEYS, CLASSES), 1).astype(F32) == column_of(kc), 1.0, 0.0
        ).astype(BF16)
        pairs = range(HEADS // 2)
        scores = []
        for j in pairs:
            column = 128 * j
            queries = head_split(q_ref[0, pl.ds(start, ROWS), column : column + 128])
            picked = dot(pick_q, yb_ref[:, 2 * column : 2 * column + 256]).astype(BF16)
            picked = jnp.concatenate([picked[:, :128], picked[:, 128:]], axis=0)
            scores.append(
                dot(
                    jnp.concatenate([queries, picked], axis=1),
                    jnp.concatenate([key_tile(kv_ref, i, column), pick_k], axis=1),
                    NT,
                )
            )
        weights = []
        for j in pairs:
            x_bias = jnp.concatenate(
                [lookup(tab_ref[2 * j + e : 2 * j + e + 1, 128:256], index) for e in (0, 1)], axis=0
            )
            biased = scores[j] + rb_ref[i, 128 * j : 128 * j + 128, :] + x_bias
            peak = jnp.max(biased, axis=1, keepdims=True)
            raised = jnp.exp(biased - peak)
            weights.append(raised.astype(BF16))
        ones = jnp.ones((KEYS, 128), BF16)
        joint = [
            dot(weights[j], jnp.concatenate([key_tile(kv_ref, i, WIDTH + 128 * j), ones], axis=1))
            for j in pairs
        ]
        contexts = []
        for j in pairs:
            share = 1.0 / joint[j][:, 128:]
            contexts.append(joint[j][:, :128] * share)
            share = jnp.concatenate([share, share], axis=1)
            weights[j] = (weights[j].astype(F32) * share).astype(BF16)
        for j in pairs:
            p_ref[0, i, 128 * j : 128 * j + 128, :] = weights[j]
        ctx_s[pl.ds(start, ROWS), :] = jnp.concatenate(
            [head_join(c).astype(BF16) for c in contexts], axis=1
        )
        return 0

    lax.fori_loop(0, blocks, block, 0, unroll=blocks)
    ctx_ref[0] = ctx_s[:rows]


def page_block(*shape):
    return pl.BlockSpec((1,) + shape, lambda p, *_: (p,) + (0,) * len(shape))


def whole(*shape):
    return pl.BlockSpec(shape, lambda *_: (0,) * len(shape))


def attention_forward(
    band, lengths, hidden, got, x_coord, line_ids, qkv_w, vectors, tables
):
    pages, rows, width = hidden.shape
    blocks = -(-rows // ROWS)
    padded = blocks * ROWS
    ext = padded + 3 * HALF
    shape = jax.ShapeDtypeStruct
    return pl.pallas_call(
        attention_kernel,
        out_shape=(
            pltpu.HBM((pages, rows, width), BF16),
            pltpu.HBM((pages, blocks, HEADS * ROWS, KEYS), BF16),
            pltpu.HBM((pages, padded, width), BF16),
            pltpu.HBM((pages, ext, 2 * width), BF16),
            pltpu.HBM((pages, rows + 2 * HALF, width), BF16),
        ),
        grid_spec=pltpu.PrefetchScalarGridSpec(
            num_scalar_prefetch=2,
            grid=(pages,),
            in_specs=[
                page_block(rows, width),
                page_block(2 * HALF, width),
                whole(*x_coord.shape),
                whole(*line_ids.shape),
                whole(width, 3 * width),
                whole(*vectors.shape),
                whole(*tables.shape),
            ],
            out_specs=[
                page_block(rows, width),
                page_block(blocks, HEADS * ROWS, KEYS),
                page_block(padded, width),
                page_block(ext, 2 * width),
                page_block(rows + 2 * HALF, width),
            ],
            scratch_shapes=[
                pltpu.VMEM((8, KEYS), F32),
                pltpu.VMEM((8, KEYS), F32),
                pltpu.VMEM((blocks, HEADS * ROWS, KEYS), F32),
                pltpu.VMEM((CLASSES, HEADS * CLASSES), BF16),
                pltpu.VMEM((padded, width), BF16),
                pltpu.VMEM((16, 384), F32),
            ],
        ),
        compiler_params=pltpu.CompilerParams(vmem_limit_bytes=56 << 20),
        cost_estimate=pl.CostEstimate(
            flops=2 * pages * (rows + 2 * HALF) * width * 3 * width
            + 8 * pages * padded * HEADS * KEYS * 128,
            bytes_accessed=30 << 20,
            transcendentals=pages * padded * HEADS * KEYS,
        ),
        name="attention_forward",
    )(
        band, lengths, *far_away(hidden), got, x_coord, line_ids, *far_away(qkv_w), vectors, tables,
    )


def layer_norm(total):
    centred = total - jnp.mean(total, axis=1, keepdims=True)
    inverse = lax.rsqrt(jnp.mean(centred * centred, axis=1, keepdims=True) + EPSILON)
    return centred * inverse, inverse


def norm_back(grad, normed, inverse, gain):
    scaled = grad * gain
    return inverse * (
        scaled
        - jnp.mean(scaled, axis=1, keepdims=True)
        - normed * jnp.mean(scaled * normed, axis=1, keepdims=True)
    )


def gelu_parts(inner):
    size = jnp.abs(inner)
    falling = jnp.exp(inner * inner * -0.5)
    t = 1.0 / (1.0 + (0.3275911 * math.sqrt(0.5)) * size)
    poly = 1.061405429 * t - 1.453152027
    poly = poly * t + 1.421413741
    poly = poly * t - 0.284496736
    poly = poly * t + 0.254829592
    tail = (0.5 * poly) * (t * falling)
    share = jnp.where(inner >= 0.0, 1.0 - tail, tail)
    return inner * share, share + inner * falling * (2.0 * math.pi) ** (-0.5)


def column_sum(values):
    return jnp.sum(values, axis=0, keepdims=True)


def accumulate(ref, row, value):
    first = pl.program_id(0) == 0

    @pl.when(first)
    def _():
        ref[row : row + 1, :] = value

    @pl.when(jnp.logical_not(first))
    def _():
        ref[row : row + 1, :] = ref[row : row + 1, :] + value


def fixed(*shape):
    return pl.BlockSpec(shape, lambda *_: (0,) * len(shape), pipeline_mode=pl.Buffered(1))


def resident():
    return pl.BlockSpec(memory_space=pltpu.VMEM)


FORWARD_CUT = 768
CUT = 768
BLOCKS = 6


def ffn_forward_kernel(
    ctx_ref, hid_ref, cot_ref, vec_ref, bin_ref, wo_ref, w1_ref, w2_ref,
    out_ref, first_ref, norm_ref, inv_ref, act_ref, slope_ref, dh_ref, ds_ref, sums_ref,
    second_s,
):
    step = pl.program_id(0)

    def vector(row):
        return vec_ref[row : row + 1, :].astype(F32)

    @pl.when(step == 0)
    def _():
        attended = dot(ctx_ref[...], wo_ref[...]) + vector(OUT_B)
        normed, inverse = layer_norm(hid_ref[...].astype(F32) + attended)
        first = (normed * vector(LN1_G) + vector(LN1_B)).astype(BF16)
        first_ref[...] = first
        norm_ref[...] = normed
        inv_ref[...] = jnp.broadcast_to(inverse, inv_ref.shape)
        second_s[...] = first.astype(F32) + vector(FFN_OUT_B)

    size = first_ref.shape[0] // BLOCKS
    parts = [slice(size * r, size * r + size) for r in range(BLOCKS)]
    w1, w2 = w1_ref[...], w2_ref[...]
    offset = bin_ref[...].astype(F32)

    def inner_of(r):
        return dot(first_ref[parts[r], :], w1) + offset

    def feed(r, act):
        second_s[parts[r], :] = second_s[parts[r], :] + dot(act, w2)

    ahead, behind = inner_of(0), None
    for r in range(BLOCKS):
        inner = ahead
        if r + 1 < BLOCKS:
            ahead = inner_of(r + 1)
        act, slope = gelu_parts(inner)
        act = act.astype(BF16)
        act_ref[parts[r], :] = act
        slope_ref[parts[r], :] = slope.astype(BF16)
        if r > 0:
            feed(r - 1, behind)
        behind = act
    feed(BLOCKS - 1, behind)

    @pl.when(step == pl.num_programs(0) - 1)
    def _():
        normed2, inverse2 = layer_norm(second_s[...])
        out_ref[...] = (normed2 * vector(LN2_G) + vector(LN2_B)).astype(BF16)
        grad = cot_ref[...].astype(F32)
        back = norm_back(grad, normed2, inverse2, vector(LN2_G))
        low = back.astype(BF16)
        dh_ref[...] = back
        ds_ref[...] = low
        sums_ref[0:1, :] = column_sum(grad * normed2)
        sums_ref[1:2, :] = column_sum(grad)
        sums_ref[2:3, :] = column_sum(low.astype(F32))


def ffn_forward(context, hidden, cotangent, vectors, ffn_in_b, out_w, ffn_in_w, ffn_out_w):
    tokens, width = context.shape
    shape = jax.ShapeDtypeStruct
    rows = fixed(tokens, width)
    step = FORWARD_CUT
    wide = pl.BlockSpec((tokens, step), lambda i: (0, i))
    return pl.pallas_call(
        ffn_forward_kernel,
        out_shape=(
            pltpu.HBM((tokens, width), BF16),
            shape((tokens, width), BF16),
            shape((tokens, width), F32),
            shape((tokens, 128), F32),
            pltpu.HBM((tokens, FF), BF16),
            pltpu.HBM((tokens, FF), BF16),
            shape((tokens, width), F32),
            shape((tokens, width), BF16),
            shape((8, width), F32),
        ),
        grid=(FF // step,),
        in_specs=[
            rows, rows, rows,
            whole(*vectors.shape),
            pl.BlockSpec((1, step), lambda i: (0, i)),
            fixed(width, width),
            pl.BlockSpec((width, step), lambda i: (0, i)),
            pl.BlockSpec((step, width), lambda i: (i, 0)),
        ],
        out_specs=[
            rows, resident(), resident(), resident(),
            wide, wide, resident(), resident(),
            whole(8, width),
        ],
        scratch_shapes=[pltpu.VMEM((tokens, width), F32)],
        compiler_params=pltpu.CompilerParams(vmem_limit_bytes=36 << 20),
        cost_estimate=pl.CostEstimate(
            flops=2 * tokens * width * (2 * FF + width),
            bytes_accessed=40 << 20,
            transcendentals=tokens * FF,
        ),
        name="ffn_forward",
    )(
        *far_away(context, hidden, cotangent), vectors, ffn_in_b,
        *far_away(out_w, ffn_in_w, ffn_out_w),
    )


def ffn_parts(owner, ds_ref, first_ref, act_ref, slope_ref, w1_ref, w2_ref, parts_ref, bsum_ref):
    step = pl.program_id(0)
    chunks, size, _ = parts_ref.shape
    orders = split_orders(chunks, True)
    low = ds_ref[...]
    grad = dot(low, w2_ref[...], NT)
    inner = (grad * slope_ref[...].astype(F32)).astype(BF16)
    out_part = dot(act_ref[...], low, TN).astype(BF16)
    in_part = dot(inner, first_ref[...], TN).astype(BF16)
    bsum_ref[...] = column_sum(inner.astype(F32))
    for c in range(CUT // size):
        chunk = step * (CUT // size) + c
        spot = jnp.where(owner == 0, place(chunk, orders[0]), place(chunk, orders[1]))
        part = slice(size * c, size * c + size)
        parts_ref[spot] = jnp.concatenate([in_part[part], out_part[part]], axis=1)
    return dot(inner, w1_ref[...], NT)


def ffn_back_far_kernel(
    band_ref, ds_ref, first_ref, act_ref, slope_ref, w1_ref, w2_ref, dh_ref,
    parts_ref, bsum_ref, total_ref,
):
    added = ffn_parts(
        1 - band_ref[0], ds_ref, first_ref, act_ref, slope_ref, w1_ref, w2_ref, parts_ref, bsum_ref
    )

    @pl.when(pl.program_id(0) == 0)
    def _():
        total_ref[...] = dh_ref[...] + added

    @pl.when(pl.program_id(0) > 0)
    def _():
        total_ref[...] = total_ref[...] + added


def ffn_back_own_kernel(
    band_ref, ds_ref, first_ref, act_ref, slope_ref, w1_ref, w2_ref, part_ref, norm_ref, inv_ref,
    vec_ref, wo_ref,
    parts_ref, bsum_ref, dh1_ref, da_ref, dc_ref, sums_ref,
    total_s,
):
    added = ffn_parts(
        band_ref[0], ds_ref, first_ref, act_ref, slope_ref, w1_ref, w2_ref, parts_ref, bsum_ref
    )

    @pl.when(pl.program_id(0) == 0)
    def _():
        total_s[...] = part_ref[...] + added

    @pl.when(pl.program_id(0) > 0)
    def _():
        total_s[...] = total_s[...] + added

    @pl.when(pl.program_id(0) == pl.num_programs(0) - 1)
    def _():
        total = total_s[...]
        normed = norm_ref[...]
        gain = vec_ref[LN1_G : LN1_G + 1, :].astype(F32)
        back = norm_back(total, normed, inv_ref[:, 0:1], gain)
        low = back.astype(BF16)
        dh1_ref[...] = back
        da_ref[...] = low
        dc_ref[...] = dot(low, wo_ref[...], NT).astype(BF16)
        sums_ref[0:1, :] = column_sum(total * normed)
        sums_ref[1:2, :] = column_sum(total)
        sums_ref[2:3, :] = column_sum(low.astype(F32))


def ffn_back_call(own, band, second_low, first, act, slope, ffn_in_w, ffn_out_w, extra, chunks):
    tokens, width = second_low.shape
    half = FF // 2
    steps = half // CUT
    shape = jax.ShapeDtypeStruct
    rows = fixed(tokens, width)

    def at(i, b):
        return (b[0] if own else 1 - b[0]) * steps + i

    in_specs = [
        resident(), resident(),
        pl.BlockSpec((tokens, CUT), lambda i, b: (0, at(i, b))),
        pl.BlockSpec((tokens, CUT), lambda i, b: (0, at(i, b))),
        pl.BlockSpec((width, CUT), lambda i, b: (0, at(i, b))),
        pl.BlockSpec((CUT, width), lambda i, b: (at(i, b), 0)),
    ] + ([resident()] * 3 + [fixed(*e.shape) for e in extra[3:]] if own else [resident()])
    out_shape = [
        pltpu.HBM((chunks // 2, FF // chunks, 2 * width), BF16),
        shape((1, half), F32),
    ]
    out_specs = [
        fixed(chunks // 2, FF // chunks, 2 * width),
        pl.BlockSpec((1, CUT), lambda i, b: (0, i)),
    ]
    if own:
        out_shape += [
            pltpu.HBM((tokens, width), F32), pltpu.HBM((tokens, width), BF16),
            pltpu.HBM((tokens, width), BF16), shape((8, width), F32),
        ]
        out_specs += [rows, rows, rows, whole(8, width)]
    else:
        out_shape += [shape((tokens, width), F32)]
        out_specs += [resident()]
    return pl.pallas_call(
        ffn_back_own_kernel if own else ffn_back_far_kernel,
        out_shape=out_shape,
        grid_spec=pltpu.PrefetchScalarGridSpec(
            num_scalar_prefetch=1,
            grid=(steps,),
            in_specs=in_specs,
            out_specs=out_specs,
            scratch_shapes=[pltpu.VMEM((tokens, width), F32)] if own else [],
        ),
        compiler_params=pltpu.CompilerParams(vmem_limit_bytes=34 << 20),
        cost_estimate=pl.CostEstimate(
            flops=8 * tokens * width * half, bytes_accessed=30 << 20, transcendentals=0
        ),
        name="ffn_back_own" if own else "ffn_back_far",
    )(
        band, second_low, first, *far_away(act, slope, ffn_in_w, ffn_out_w),
        *(extra[:-1] + tuple(far_away(extra[-1])) if own else extra),
    )


def attention_back_kernel(
    p_ref, q_ref, kv_ref, dc_ref,
    dm_ref, ds_ref,
    dkv_ref, dc_s, dq_s,
):
    rows = dc_ref.shape[1]
    blocks = q_ref.shape[1] // ROWS
    dkv_ref[...] = jnp.zeros_like(dkv_ref)
    dc_s[:rows] = dc_ref[0]
    dc_s[rows:] = jnp.zeros((dc_s.shape[0] - rows, WIDTH), BF16)
    def block(i, _):
        start = pl.multiple_of(ROWS * i, ROWS)
        window = pl.ds(pl.multiple_of(HALF + ROWS * i, ROWS), 3 * HALF)
        pairs = range(HEADS // 2)
        grads = []
        for j in pairs:
            column = 128 * j
            grads.append(head_split(dc_s[pl.ds(start, ROWS), column : column + 128]))
        dprobs = [dot(grads[j], key_tile(kv_ref, i, WIDTH + 128 * j), NT) for j in pairs]
        for j in pairs:
            dv = dot(p_ref[0, i, 128 * j : 128 * j + 128, :], grads[j], TN)
            column = WIDTH + 128 * j
            cut = slice(column, column + 128)
            dkv_ref[0:HALF, cut] = dkv_ref[0:HALF, cut] + dv[:HALF]
            dkv_ref[window, cut] = dkv_ref[window, cut] + dv[HALF:]
        lows = []
        for j in pairs:
            probs = p_ref[0, i, 128 * j : 128 * j + 128, :].astype(F32)
            grad = probs * (
                dprobs[j] - jnp.sum(probs * dprobs[j], axis=1, keepdims=True)
            )
            lows.append(grad.astype(BF16))
        dq = [head_join(dot(lows[j], key_tile(kv_ref, i, 128 * j))) for j in pairs]
        dq_s[pl.ds(start, ROWS), :] = (jnp.concatenate(dq, axis=1) * 0.125).astype(BF16)
        for j in pairs:
            cut = slice(128 * j, 128 * j + 128)
            dk = dot(lows[j], head_split(q_ref[0, pl.ds(start, ROWS), cut]), TN)
            dkv_ref[0:HALF, cut] = dkv_ref[0:HALF, cut] + dk[:HALF]
            dkv_ref[window, cut] = dkv_ref[window, cut] + dk[HALF:]

        for j in pairs:
            ds_ref[0, i, 128 * j : 128 * j + 128, :] = lows[j]
        return 0

    lax.fori_loop(0, blocks, block, 0, unroll=blocks)
    dm_ref[0, : 2 * HALF, :WIDTH] = jnp.zeros((2 * HALF, WIDTH), BF16)
    dm_ref[0, 2 * HALF :, :WIDTH] = dq_s[:rows]
    dm_ref[0, :HALF, WIDTH:] = dkv_ref[:HALF].astype(BF16)
    dm_ref[0, HALF : 2 * HALF, WIDTH:] = (
        dkv_ref[HALF : 2 * HALF] + dkv_ref[2 * HALF + rows : 3 * HALF + rows]
    ).astype(BF16)
    dm_ref[0, 2 * HALF :, WIDTH:] = dkv_ref[2 * HALF : 2 * HALF + rows].astype(BF16)


def attention_backward(probs, queries, pairs, grad_context):
    pages, rows, width = grad_context.shape
    padded = queries.shape[1]
    blocks = padded // ROWS
    ext = pairs.shape[1]
    shape = jax.ShapeDtypeStruct
    return pl.pallas_call(
        attention_back_kernel,
        out_shape=(
            pltpu.HBM((pages, rows + 2 * HALF, 3 * width), BF16),
            pltpu.HBM(probs.shape, BF16),
        ),
        grid=(pages,),
        in_specs=[
            page_block(blocks, HEADS * ROWS, KEYS),
            page_block(padded, width),
            page_block(ext, 2 * width),
            page_block(rows, width),
        ],
        out_specs=[page_block(rows + 2 * HALF, 3 * width), page_block(blocks, HEADS * ROWS, KEYS)],
        scratch_shapes=[
            pltpu.VMEM((ext, 2 * width), F32),
            pltpu.VMEM((padded, width), BF16),
            pltpu.VMEM((padded, width), BF16),
        ],
        compiler_params=pltpu.CompilerParams(vmem_limit_bytes=56 << 20),
        cost_estimate=pl.CostEstimate(
            flops=10 * pages * padded * HEADS * KEYS * 128, bytes_accessed=30 << 20, transcendentals=0
        ),
        name="attention_backward",
    )(*far_away(probs, queries, pairs, grad_context))


def table_kernel(
    blocks, start, band_ref, ds_ref, x_ref, line_ref, tab_ref, kx_ref, kc_ref, left_ref, right_ref,
    index_ref,
):
    step = pl.program_id(0)
    band = band_ref[0]
    page = (start + step) // blocks
    i = (start + step) % blocks
    first_pos = band * (x_ref.shape[-1] // 2)

    @pl.when((step == 0) | (i == 0))
    def _():
        own = pl.ds(page, 1)
        stage_geometry(first_pos, band, x_ref[own, :], line_ref[own, :], kx_ref, kc_ref, blocks)

    slots = iota((REL_BUCKETS + 2 * XY_BUCKETS, KEYS), 0).astype(F32).astype(BF16)
    one = jnp.ones((), BF16)
    zero = jnp.zeros((), BF16)

    left_ref[...] = ds_ref[0, :, :128].astype(F32)
    right_ref[...] = ds_ref[0, :, 128:].astype(F32)
    kx = kx_ref[pl.ds(i, 1), :]
    ky = class_y(kc_ref[pl.ds(i, 1), :].astype(I32))
    index_ref[0:ROWS] = bucket(kx - column_of(kx[:, 2 * HALF : 3 * HALF]), XY_BUCKETS, XY_REACH)
    index_ref[ROWS : 2 * ROWS] = 64.0 + bucket(
        ky - column_of(ky[:, 2 * HALF : 3 * HALF]), XY_BUCKETS, XY_REACH
    )
    index_ref[2 * ROWS : 3 * ROWS] = 128.0 + rel_buckets(first_pos, i)

    def table_row(q, acc):
        own = jnp.concatenate(
            [
                jnp.broadcast_to(index_ref[pl.ds(q, 1), :], (XY_BUCKETS, KEYS)),
                jnp.broadcast_to(index_ref[pl.ds(ROWS + q, 1), :], (XY_BUCKETS, KEYS)),
                jnp.broadcast_to(index_ref[pl.ds(2 * ROWS + q, 1), :], (REL_BUCKETS, KEYS)),
            ],
            axis=0,
        ).astype(BF16)
        heads = jnp.concatenate(
            [
                left_ref[pl.ds(q, HEADS, stride=ROWS), :],
                right_ref[pl.ds(q, HEADS, stride=ROWS), :],
            ],
            axis=1,
        ).astype(BF16)
        return acc + dot(heads, jnp.where(slots == own, one, zero), NT)

    table_sum = lax.fori_loop(
        0, ROWS, table_row, jnp.zeros(tab_ref.shape, F32), unroll=ROWS
    )

    @pl.when(step == 0)
    def _():
        tab_ref[...] = table_sum

    @pl.when(step > 0)
    def _():
        tab_ref[...] = tab_ref[...] + table_sum


def table_sums(band, start, count, grad_scores, x_coord, line_ids):
    pages, blocks, height, keys = grad_scores.shape
    buckets = REL_BUCKETS + 2 * XY_BUCKETS
    return pl.pallas_call(
        functools.partial(table_kernel, blocks, start),
        out_shape=jax.ShapeDtypeStruct((HEADS, buckets), F32),
        grid_spec=pltpu.PrefetchScalarGridSpec(
            num_scalar_prefetch=1,
            grid=(count,),
            in_specs=[
                pl.BlockSpec((1, height, keys), lambda i, *_: (start + i, 0, 0)),
                whole(*x_coord.shape),
                whole(*line_ids.shape),
            ],
            out_specs=whole(HEADS, buckets),
            scratch_shapes=[
                pltpu.VMEM((8, KEYS), F32),
                pltpu.VMEM((8, KEYS), F32),
                pltpu.VMEM((height, 128), F32),
                pltpu.VMEM((height, 128), F32),
                pltpu.VMEM((3 * ROWS, KEYS), F32),
            ],
        ),
        compiler_params=pltpu.CompilerParams(vmem_limit_bytes=40 << 20),
        cost_estimate=BRIEF,
        name="table_sums",
    )(band, *far_away(grad_scores.reshape(pages * blocks, height, keys)), x_coord, line_ids)


def hidden_back_kernel(dm_ref, dh_ref, w_ref, *refs):
    own_ref, far_ref = refs[-2:]
    own_ref[0] = dh_ref[0] + dot(dm_ref[0, 2 * HALF :], w_ref[...], NT)
    far_ref[0] = dot(dm_ref[0, : 2 * HALF, WIDTH:], w_ref[:, WIDTH:], NT).astype(BF16)


def hidden_backward(page, outs, grad_mixed, grad_total, qkv_w):
    pages, rows, width = grad_total.shape

    def one(*shape):
        return pl.BlockSpec((1,) + shape, lambda i: (page, 0, 0))

    return pl.pallas_call(
        hidden_back_kernel,
        out_shape=(
            pltpu.HBM((pages, rows, width), F32),
            pltpu.HBM((pages, 2 * HALF, width), BF16),
        ),
        grid=(1,),
        in_specs=[
            one(rows + 2 * HALF, 3 * width),
            one(rows, width),
            whole(width, 3 * width),
        ]
        + [pl.BlockSpec(memory_space=pl.ANY)] * len(outs),
        out_specs=[one(rows, width), one(2 * HALF, width)],
        input_output_aliases={3 + i: i for i in range(len(outs))},
        compiler_params=pltpu.CompilerParams(vmem_limit_bytes=60 << 20),
        cost_estimate=BRIEF,
        name="hidden_backward",
    )(*far_away(grad_mixed, grad_total, qkv_w), *outs)


def edge_kernel(band_ref, grad_ref, far_ref, got_ref, out_ref):
    band = band_ref[0]
    side = pl.program_id(0)
    edge = HALF // 2
    for s in range(4):

        @pl.when(side == s)
        def _():
            part = slice(edge * (s % 2), edge * (s % 2) + edge)
            rim = slice(HALF + part.start, HALF + part.stop)
            if s < 2:
                own = far_ref[:, part].astype(F32) + got_ref[:, part].astype(F32)
                added = jnp.where(band == 0, own, got_ref[:, rim].astype(F32))
            else:
                added = jnp.where(band == 0, got_ref[:, rim].astype(F32), 0.0)
            out_ref[...] = grad_ref[...] + added


def edge_add(band, grad, far, got):
    pages, rows, width = grad.shape
    half = HALF // 2
    last = rows // half - 2

    def edge(s, *_):
        return (0, jnp.where(s < 2, s, last + s - 2), 0)

    return pl.pallas_call(
        edge_kernel,
        out_shape=jax.ShapeDtypeStruct(grad.shape, F32),
        grid_spec=pltpu.PrefetchScalarGridSpec(
            num_scalar_prefetch=1,
            grid=(4,),
            in_specs=[
                pl.BlockSpec((pages, half, width), edge),
                whole(*far.shape),
                whole(*got.shape),
            ],
            out_specs=pl.BlockSpec((pages, half, width), edge),
        ),
        input_output_aliases={1: 0},
        cost_estimate=BRIEF,
        name="edge_add",
    )(band, grad, far, got)


def split_orders(count, mixed=False):
    total = count.bit_length() - 1
    side = total // 3
    x, y, z = (range(side), range(side, 2 * side), range(2 * side, total))
    if mixed:
        return [*x, *z[:-1], *y, z[-1]], [*y, *z[:-1], *x, z[-1]]
    return [*x, *y, *z], [*y, *x, *z]


def place(chunk, order):
    spot = 0
    for level, bit in enumerate(order):
        spot = spot + (((chunk >> bit) & 1) << (len(order) - 1 - level))
    return spot


def product_halves(band, tokens_ext, grad_mixed, context, grad_attn):
    tokens, height = tokens_ext.shape
    width = grad_mixed.shape[1]
    step = height // 2

    def kernel(band_ref, l_ref, r_ref, l2_ref, r2_ref, send_ref, keep_ref, sums_ref):
        def write(ref):
            ref[:, :width] = dot(l_ref[...], r_ref[...], TN).astype(BF16)
            ref[:, width:] = dot(l2_ref[...], r2_ref[...], TN).astype(BF16)

        @pl.when(pl.program_id(0) == 0)
        def _():
            write(send_ref)
            sums_ref[...] = dot(jnp.ones((tokens, 8), BF16), r_ref[...], TN)

        pl.when(pl.program_id(0) == 1)(lambda: write(keep_ref))

    def at(i, b):
        return (0, jnp.where(i == 0, 1 - b[0], b[0]))

    out = pltpu.HBM((step, width + height), BF16)
    return pl.pallas_call(
        kernel,
        out_shape=(out, out, jax.ShapeDtypeStruct((8, width), F32)),
        grid_spec=pltpu.PrefetchScalarGridSpec(
            num_scalar_prefetch=1,
            grid=(2,),
            in_specs=[
                pl.BlockSpec((tokens, step), at),
                fixed(*grad_mixed.shape),
                pl.BlockSpec((context.shape[0], step), at),
                fixed(*grad_attn.shape),
            ],
            out_specs=[
                fixed(step, width + height), fixed(step, width + height), fixed(8, width)
            ],
        ),
        compiler_params=pltpu.CompilerParams(vmem_limit_bytes=60 << 20),
        cost_estimate=pl.CostEstimate(
            flops=2 * tokens * height * (width + height), bytes_accessed=16 << 20, transcendentals=0
        ),
        name="product_halves",
    )(band, *far_away(tokens_ext, grad_mixed, context, grad_attn))


def swap_bands(block):
    return lax.ppermute(block, "band", [(0, 1), (1, 0)])


def swap_pages(block, level, orders):
    count = lax.axis_size("page")
    route = [
        (b * count + p, b * count + (p ^ (1 << orders[b][level])))
        for b in range(2)
        for p in range(count)
    ]
    return lax.ppermute(block, ("band", "page"), route)


def sides(orders):
    band, page = lax.axis_index("band"), lax.axis_index("page")
    return [
        jnp.where(band == 0, (page >> first) & 1, (page >> second) & 1)
        for first, second in zip(*orders)
    ]


def widen(band, block, own, outs, shapes):
    half, width = shapes[0][0] // 2, block.shape[1]
    steps = 4
    step = half // steps
    edges = [sum(shape[1] for shape in shapes[:i]) for i in range(len(shapes) + 1)]

    def kernel(band_ref, block_ref, *refs):
        for out, start, stop in zip(refs[-len(shapes) :], edges, edges[1:]):
            out[...] = block_ref[:, start:stop].astype(F32)

    def at(i, b):
        return ((b[0] if own else 1 - b[0]) * steps + i, 0)

    return pl.pallas_call(
        kernel,
        out_shape=[pltpu.HBM(shape, F32) for shape in shapes],
        grid_spec=pltpu.PrefetchScalarGridSpec(
            num_scalar_prefetch=1,
            grid=(steps,),
            in_specs=[pl.BlockSpec((step, width), lambda i, *_: (i, 0))]
            + [pl.BlockSpec(memory_space=pl.ANY)] * len(outs),
            out_specs=[pl.BlockSpec((step, shape[1]), at) for shape in shapes],
        ),
        input_output_aliases={2 + i: i for i in range(len(outs))},
        compiler_params=pltpu.CompilerParams(vmem_limit_bytes=40 << 20),
        cost_estimate=BRIEF,
        name="widen",
    )(band, block, *outs)


class Order:
    def __init__(self):
        self.mark = None

    def __call__(self, part, *args):
        if self.mark is not None:
            leaves, tree = jax.tree.flatten(args)
            leaves = lax.optimization_barrier((*leaves, self.mark))[:-1]
            args = jax.tree.unflatten(tree, leaves)
        out = part(*args)
        self.mark = jax.tree.leaves(out)[0]
        return out

    def late(self, block):
        return lax.optimization_barrier((block, self.mark))[0]


def halving_plan(size, orders):
    starts, spots = [], [[0, 0]]
    for side in sides(orders):
        size = size // 2
        starts.append([at + (1 - side) * size for at in spots[-1]])
        spots.append([at + side * size for at in spots[-1]] + [0])
    return starts, spots


class Halving:
    def __init__(self, order, send, keep, orders, plan):
        self.order = order
        self.orders = orders
        self.starts, self.spots, self.sides = plan
        self.level = 0
        self.held = [keep]
        self.size = keep.shape[0]
        self.flight = swap_bands(send)

    def land(self):
        self.held.append(self.flight)
        self.flight = None

    def total(self, size):
        def add(spots, *held):
            parts = [
                lax.dynamic_slice_in_dim(block, at, size, 0, allow_negative_indices=False)
                for block, at in zip(held, spots)
            ]
            return sum([part.astype(F32) for part in parts[1:]], parts[0].astype(F32))

        return add

    def step(self):
        self.gather()
        self.send(self.sent)

    def gather(self):
        self.land()
        self.size //= 2
        add = self.total(self.size)
        self.sent = self.order(
            lambda *a: add(*a).astype(BF16), self.starts[self.level], *self.held
        )

    def send(self, sent):
        self.flight = swap_pages(sent, self.level, self.orders)
        self.level += 1

    def send_late(self):
        self.send(self.order.late(self.sent))

    def finish(self, wrap):
        self.land()
        add = self.total(self.size)
        return self.order(lambda *a: wrap(add(*a)), self.spots[self.level], *self.held)

    def meet(self):
        self.land()
        add = self.total(self.size)
        mine = self.order(lambda *a: add(*a).astype(BF16), self.spots[self.level], *self.held)
        self.flight = swap_pages(mine, self.level, self.orders)
        self.mine = mine

    def met(self):
        self.mine = self.order(
            lambda a, b: (a.astype(F32) + b.astype(F32)).astype(BF16), self.mine, self.flight
        )
        self.rider = None
        self.level -= 1
        self.flight = swap_pages(self.mine, self.level, self.orders)

    def after(self, other):
        self.mine, other.flight = lax.optimization_barrier((self.mine, other.flight))

    def grow(self, rider=None):
        size = self.mine.shape[0]
        if rider is None and self.rider is None:
            self.mine = self.order(join, self.mine, self.flight, self.sides[self.level])
            sent = self.mine
        else:
            first = rider is not None

            def both(mine, got, rider, side):
                if not first:
                    rider = rider + rider_of(got[size:])
                return with_rider(join(mine, got[:size], side), rider)

            sent, self.mine, self.rider = self.order(
                both, self.mine, self.flight, rider if first else self.rider,
                self.sides[self.level],
            )
        self.level -= 1
        self.flight = (
            swap_pages(sent, self.level, self.orders) if self.level >= 0 else swap_bands(sent)
        )

    def last_rider(self):
        size = self.mine.shape[0]
        return self.order(
            lambda got, rider: rider + rider_of(got[size:]), self.flight, self.rider
        )


def with_rider(block, rider):
    high = lax.reduce_precision(rider, 8, 7)
    low = (rider - high).astype(BF16)
    return jnp.concatenate([block, high.astype(BF16), low], axis=0), block, rider


def rider_of(rows):
    half = rows.shape[0] // 2
    return rows[:half].astype(F32) + rows[half:].astype(F32)


def join(mine, other, side):
    return jnp.where(
        side == 0,
        jnp.concatenate([mine, other], axis=0),
        jnp.concatenate([other, mine], axis=0),
    )


def flat(block):
    return block.reshape(-1, block.shape[-1])


def local(
    hidden, cotangent, page_lengths, x_coord, line_ids, qkv_w, q_bias, v_bias,
    rel_table, x_table, y_table, out_w, out_b, ln1_gain, ln1_bias,
    ffn_in_w, ffn_in_b, ffn_out_w, ffn_out_b, ln2_gain, ln2_bias,
):
    pages, rows, width = hidden.shape
    band = lax.axis_index("band")
    chunks = 2 * lax.axis_size("page")
    band_arr = band.reshape(1).astype(I32)
    own_edge = jnp.where(band == 0, hidden[:, rows - HALF :], hidden[:, :HALF])
    got = swap_bands(jnp.concatenate([hidden[:, :HALF], own_edge], axis=1))
    half = chunks // 2
    ffn_orders, attn_orders = split_orders(half, True), split_orders(half)
    plans = [
        (*halving_plan(size, orders), sides(orders))
        for size, orders in ((half, ffn_orders), (width // 2, attn_orders))
    ]
    got, plans = lax.optimization_barrier((got, plans))
    ffn_plan, attn_plan = plans
    vectors = jnp.concatenate(
        [out_b, ln1_gain, ln1_bias, ffn_out_b, ln2_gain, ln2_bias, q_bias, v_bias]
    ).reshape(8, width)
    tables = jnp.concatenate([rel_table, x_table, y_table], axis=0)
    context, probs, queries, pairs, extended = attention_forward(
        band_arr, page_lengths, hidden, got, x_coord, line_ids, qkv_w, vectors, tables
    )
    output, first, normed, inverse, act, slope, grad_total2, second_low, sums2 = ffn_forward(
        flat(context), flat(hidden), flat(cotangent), vectors,
        ffn_in_b.reshape(1, FF), out_w, ffn_in_w, ffn_out_w,
    )
    order = Order()
    send, bsum_far, part = order(
        lambda *a: ffn_back_call(False, band_arr, *a, chunks),
        second_low, first, act, slope, ffn_in_w, ffn_out_w, (grad_total2,),
    )
    keep, bsum_own, grad_total1, attn_low, grad_context, sums1 = order(
        lambda *a: ffn_back_call(True, band_arr, *a, chunks),
        second_low, first, act, slope, ffn_in_w, ffn_out_w,
        (part, normed, inverse, vectors, out_w),
    )
    ffn = Halving(order, send, keep, ffn_orders, ffn_plan)
    ffn.step()
    grad_mixed, grad_scores = order(
        attention_backward, probs, queries, pairs, grad_context.reshape(pages, rows, width)
    )
    send, keep, mixed_sums = order(
        product_halves, band_arr, flat(extended), flat(grad_mixed), flat(context), attn_low
    )
    attn = Halving(order, send, keep, attn_orders, attn_plan)
    ffn.step()
    attn.step()
    total = grad_scores.shape[0] * grad_scores.shape[1]
    marks = [0, total // 3, total // 3 + 2, 2 * total // 3, total]

    def tables_of(piece):
        start, stop = marks[piece : piece + 2]
        return order(
            lambda *a: table_sums(band_arr, start, stop - start, *a),
            grad_scores, x_coord, line_ids,
        )

    tables = [tables_of(0)]
    attn.step()
    tables.append(tables_of(1))
    attn.step()
    while ffn.level < len(ffn.sides) - 1:
        ffn.step()
    tables.append(tables_of(2))
    inner_sums = order(
        lambda own, far: jnp.where(
            band == 0,
            jnp.concatenate([own, far], axis=1),
            jnp.concatenate([far, own], axis=1),
        ),
        bsum_own, bsum_far,
    )
    attn.meet()
    tables.append(tables_of(3))
    rider = order(
        lambda m, a, b, c, *t: jnp.pad(
            jnp.concatenate(
                [
                    m[0].reshape(3, width), a[:3], b[:3], c.reshape(FF // width, width),
                    jnp.pad(sum(t[1:], t[0]), ((0, 3), (0, width - t[0].shape[1]))),
                ],
                axis=0,
            ).reshape(7, 4 * width),
            ((0, 1), (0, 0)),
        ),
        mixed_sums, sums1, sums2, inner_sums, *tables,
    )
    levels = len(attn.sides)
    flat_levels = 2 * (levels // 3)
    got = swap_pages(rider, levels - 1, attn.orders)
    attn.met()
    ffn.gather()
    grads = ()

    def hidden_of(page):
        return order(
            lambda outs, *a: hidden_backward(page, outs, *a),
            grads, grad_mixed, grad_total1.reshape(pages, rows, width), qkv_w,
        )

    for level in reversed(range(flat_levels, levels - 1)):
        rider = order(lambda a, b: a + b, rider, got)
        got = swap_pages(rider, level, attn.orders)
    grads = hidden_of(0)
    rider = order(lambda a, b: a + b, rider, got)
    while attn.level > flat_levels:
        attn.grow()
    attn.grow(rider)
    ffn.send_late()
    grads = hidden_of(1)
    while attn.level > 0:
        attn.grow()
    for page in range(2, pages):
        grads = hidden_of(page)
    grad_hidden, far = grads
    far_got = swap_bands(far)
    attn.after(ffn)
    attn.grow()
    ffn_in_share, ffn_out_share = ffn.finish(
        lambda total: (total[0, :, :width].T, total[0, :, width:])
    )
    shapes = ((width, 3 * width), (width, width))
    halves = order(lambda mine: widen(band_arr, mine, True, (), shapes), attn.mine)
    grad_hidden = order(edge_add, band_arr, grad_hidden, far, far_got)
    small = attn.last_rider()
    grad_qkv, grad_out = order(
        lambda other, *outs: widen(band_arr, other, False, outs, shapes), attn.flight, *halves
    )

    def outs_of(small):
        small = small.reshape(-1, width)
        tables = small[13 : 13 + HEADS]
        return (
            small[0], small[2], tables[:, 128:160].T, tables[:, :64].T, tables[:, 64:128].T,
            small[5], small[3], small[4], small[9:13].reshape(FF), small[8], small[6], small[7],
        )

    small_outs = order(outs_of, small)
    (
        grad_q_bias, grad_v_bias, grad_rel, grad_x, grad_y, grad_out_b, grad_ln1_gain,
        grad_ln1_bias, grad_ffn_in_b, grad_ffn_out_b, grad_ln2_gain, grad_ln2_bias,
    ) = small_outs
    return (
        output.reshape(hidden.shape),
        grad_hidden,
        grad_qkv,
        grad_q_bias,
        grad_v_bias,
        grad_rel,
        grad_x,
        grad_y,
        grad_out,
        grad_out_b,
        grad_ln1_gain,
        grad_ln1_bias,
        ffn_in_share,
        grad_ffn_in_b,
        ffn_out_share,
        grad_ffn_out_b,
        grad_ln2_gain,
        grad_ln2_bias,
    )


def solution(mesh):
    in_specs = (
        P("page", "band", None),
        P("page", "band", None),
        P("page"),
        P("page", None),
        P("page", None),
        P(),
        P(),
        P(),
        P(),
        P(),
        P(),
        P(),
        P(),
        P(),
        P(),
        P(),
        P(),
        P(),
        P(),
        P(),
        P(),
    )
    out_specs = (
        P("page", "band", None),
        P("page", "band", None),
        P(),
        P(),
        P(),
        P(),
        P(),
        P(),
        P(),
        P(),
        P(),
        P(),
        P(None, ("band", "page")),
        P(),
        P(("band", "page"), None),
        P(),
        P(),
        P(),
    )
    return jax.shard_map(local, mesh=mesh, in_specs=in_specs, out_specs=out_specs, check_vma=False)
```

```python
import functools
import math

import jax
import jax.numpy as jnp
import numpy as np
from jax import lax
from jax.experimental import pallas as pl
from jax.experimental.pallas import tpu as pltpu
from jax.sharding import PartitionSpec as P

F32 = jnp.float32
BF16 = jnp.bfloat16
I32 = jnp.int32

HEADS = 12
WIDTH = 768
FF = 3072
REL_BUCKETS = 32
REL_REACH = 128
XY_BUCKETS = 64
XY_REACH = 256
VIS = 49
HALF = 64
ROWS = 64
KEYS = 256
CLASSES = 128
HIDE = 127
EPSILON = 1e-05
MASKED = -1e30
OUT_B, LN1_G, LN1_B, FFN_OUT_B, LN2_G, LN2_B, Q_B, V_B = range(8)
BRIEF = pl.CostEstimate(flops=1, bytes_accessed=1, transcendentals=0)
NT = (((1,), (1,)), ((), ()))
TN = (((0,), (0,)), ((), ()))
NN = (((1,), (0,)), ((), ()))


def far_away(*arrays):
    return [pltpu.with_memory_space_constraint(a, pltpu.HBM) for a in arrays]


def dot(a, b, dims=NN):
    return lax.dot_general(a, b, dims, preferred_element_type=F32)


def bucket_edges(buckets, reach):
    exact = buckets // 4
    spread = buckets // 2 - exact
    return [
        int(np.ceil(exact * (reach / exact) ** (level / spread) - 1e-09))
        for level in range(1, spread)
    ]


def bucket(offsets, buckets, reach):
    distance = jnp.abs(offsets)
    result = jnp.minimum(distance, float(buckets // 4))
    for edge in bucket_edges(buckets, reach):
        result = result + jnp.where(distance >= float(edge), 1.0, 0.0)
    return result + jnp.where(offsets > 0.0, float(buckets // 2), 0.0)


def iota(shape, axis):
    return lax.broadcasted_iota(I32, shape, axis)


def seventh(index):
    return lax.shift_right_logical(index * 37, 8)


def column_of(row):
    size = row.shape[1]
    shape = (size, size)
    spread = jnp.broadcast_to(row, shape)
    return jnp.sum(jnp.where(iota(shape, 0) == iota(shape, 1), spread, 0.0), axis=1, keepdims=True)


def stage_geometry(first_pos, band, x_own, line_own, kx_ref, kc_ref, blocks):
    extent = ROWS * blocks + 2 * HALF
    seq = x_own.shape[-1]
    half_seq = seq // 2

    def window(row):
        left = jnp.concatenate([jnp.zeros((1, HALF), I32), row[:, : extent - HALF]], axis=1)
        start = half_seq - HALF
        right = jnp.concatenate(
            [row[:, start:], jnp.zeros((1, extent - (seq - start)), I32)], axis=1
        )
        return jnp.where(band == 0, left, right)

    pos = first_pos - HALF + iota((1, extent), 1)
    visual = (pos >= 0) & (pos < VIS)
    seventh_pos = seventh(pos)
    x_row = jnp.where(visual, (pos - 7 * seventh_pos) * 142 + 71, window(x_own))
    c_row = jnp.where(visual, 64 + seventh_pos, window(line_own))
    lane = iota((1, HALF), 1)
    x_vis = (lane - 7 * seventh(lane)) * 142 + 71
    c_vis = 64 + seventh(lane)
    for i in range(blocks):
        cut = slice(ROWS * i, ROWS * i + 3 * HALF)
        kx_ref[i : i + 1, :] = jnp.concatenate([x_vis, x_row[:, cut]], axis=1).astype(F32)
        kc_ref[i : i + 1, :] = jnp.concatenate([c_vis, c_row[:, cut]], axis=1).astype(F32)


def key_positions(first_pos, i, shape):
    lane = iota(shape, 1)
    return jnp.where(
        lane < HALF,
        jnp.where(lane < VIS, lane, -1),
        first_pos + ROWS * i - 2 * HALF + lane,
    )


def allowed(first_pos, i, length):
    shape = (ROWS, KEYS)
    lane = iota(shape, 1)
    key = key_positions(first_pos, i, shape)
    query = first_pos + ROWS * i + iota(shape, 0)
    near = (key >= VIS) & (query >= VIS) & (jnp.abs(query - key) <= HALF)
    return (key >= 0) & (key < VIS + length) & ((lane < HALF) | near)


def rel_buckets(first_pos, i):
    shape = (ROWS, KEYS)
    key = key_positions(first_pos, i, shape)
    query = first_pos + ROWS * i + iota(shape, 0)
    return bucket((key - query).astype(F32), REL_BUCKETS, REL_REACH)


def class_y(index):
    return jnp.where(index < 64, 15 * index, 142 * (index - 64) + 71).astype(F32)


def lookup(table_row, index):
    shape = index.shape
    row = jnp.broadcast_to(table_row, (shape[0], 128))
    cuts = [
        jnp.take_along_axis(row, index[:, s : s + 128], axis=1) for s in range(0, shape[1], 128)
    ]
    return cuts[0] if len(cuts) == 1 else jnp.concatenate(cuts, axis=1)


def head_split(tile):
    low = iota(tile.shape, 1) < 64
    zero = jnp.zeros_like(tile)
    return jnp.concatenate([jnp.where(low, tile, zero), jnp.where(low, zero, tile)], axis=0)


def head_join(stack):
    rows = stack.shape[0] // 2
    low = iota((rows, stack.shape[1]), 1) < 64
    return jnp.where(low, stack[:rows], stack[rows:])


def key_tile(kv_ref, i, column):
    return jnp.concatenate(
        [
            kv_ref[0, 0:HALF, column : column + 128],
            kv_ref[0, pl.ds(pl.multiple_of(HALF + ROWS * i, ROWS), 3 * HALF), column : column + 128],
        ],
        axis=0,
    )


def attention_kernel(
    band_ref, len_ref, hid_ref, got_ref, x_ref, line_ref, w_ref, vec_ref, table_ref,
    ctx_ref, p_ref, q_ref, kv_ref, ext_ref,
    kx_ref, kc_ref, rb_ref, yb_ref, ctx_s, tab_ref,
):
    page = pl.program_id(0)
    band = band_ref[0]
    rows = hid_ref.shape[1]
    blocks = q_ref.shape[1] // ROWS
    first_pos = band * rows

    @pl.when(page == 0)
    def _():
        start = 0
        for slot, count in enumerate((REL_BUCKETS, XY_BUCKETS, XY_BUCKETS)):
            eye = jnp.where(iota((count, 128), 0) == iota((count, 128), 1), 1.0, 0.0).astype(BF16)
            turned = dot(table_ref[start : start + count, :], eye, TN)
            if slot == 1:
                turned = jnp.where(iota((HEADS, 128), 1) == HIDE, MASKED, turned)
            tab_ref[:HEADS, 128 * slot : 128 * slot + 128] = turned
            start += count
        for i in range(blocks):
            index = rel_buckets(first_pos, i).astype(I32)
            for h in range(HEADS):
                part = slice(ROWS * h, ROWS * h + ROWS)
                if i == 0:
                    rb_ref[i, part, :] = lookup(tab_ref[h : h + 1, 0:128], index)
                else:
                    rb_ref[i, part, :128] = lookup(tab_ref[h : h + 1, 0:128], index[:, :128])
                    rb_ref[i, part, 128:] = rb_ref[0, part, 128:]
        square = (CLASSES, CLASSES)
        gap = class_y(iota(square, 1)) - class_y(iota(square, 0))
        index = jnp.minimum(bucket(gap, XY_BUCKETS, XY_REACH), 63.0).astype(I32)
        for h in range(HEADS):
            yb_ref[:, CLASSES * h : CLASSES * h + CLASSES] = lookup(
                tab_ref[h : h + 1, 256:384], index
            ).astype(BF16)

    own = pl.ds(page, 1)
    stage_geometry(first_pos, band, x_ref[own, :], line_ref[own, :], kx_ref, kc_ref, blocks)
    ext_ref[0, :HALF] = jnp.where(band == 0, hid_ref[0, :HALF], got_ref[0, :HALF])
    ext_ref[0, HALF : 2 * HALF] = got_ref[0, HALF:]
    ext_ref[0, 2 * HALF :] = hid_ref[0]
    q_ref[0, 0:rows] = (
        (dot(hid_ref[0], w_ref[:, :WIDTH]) + vec_ref[Q_B : Q_B + 1, :].astype(F32)).astype(BF16).astype(F32)
        * 0.125
    ).astype(BF16)
    q_ref[0, rows:] = jnp.zeros((q_ref.shape[1] - rows, WIDTH), BF16)
    kv_ref[0, : 2 * HALF + rows, :WIDTH] = dot(ext_ref[0], w_ref[:, WIDTH : 2 * WIDTH]).astype(BF16)
    kv_ref[0, : 2 * HALF + rows, WIDTH:] = (
        dot(ext_ref[0], w_ref[:, 2 * WIDTH :]) + vec_ref[V_B : V_B + 1, :].astype(F32)
    ).astype(BF16)
    kv_ref[0, 2 * HALF + rows : 3 * HALF + rows] = kv_ref[0, HALF : 2 * HALF]
    tail = kv_ref.shape[1] - (3 * HALF + rows)
    kv_ref[0, 3 * HALF + rows :] = jnp.zeros((tail, 2 * WIDTH), BF16)

    def block(i, _):
        start = pl.multiple_of(ROWS * i, ROWS)
        kx = kx_ref[pl.ds(i, 1), :]
        kc = kc_ref[pl.ds(i, 1), :]
        gap = kx - column_of(kx[:, 2 * HALF : 3 * HALF])
        index = jnp.where(
            allowed(first_pos, i, len_ref[page]), bucket(gap, XY_BUCKETS, XY_REACH), float(HIDE)
        ).astype(I32)
        pick_q = jnp.where(
            iota((ROWS, CLASSES), 1).astype(F32) == column_of(kc[:, 2 * HALF : 3 * HALF]), 1.0, 0.0
        ).astype(BF16)
        pick_k = jnp.where(
            iota((KEYS, CLASSES), 1).astype(F32) == column_of(kc), 1.0, 0.0
        ).astype(BF16)
        pairs = range(HEADS // 2)
        scores = []
        for j in pairs:
            column = 128 * j
            queries = head_split(q_ref[0, pl.ds(start, ROWS), column : column + 128])
            picked = dot(pick_q, yb_ref[:, 2 * column : 2 * column + 256]).astype(BF16)
            picked = jnp.concatenate([picked[:, :128], picked[:, 128:]], axis=0)
            scores.append(
                dot(
                    jnp.concatenate([queries, picked], axis=1),
                    jnp.concatenate([key_tile(kv_ref, i, column), pick_k], axis=1),
                    NT,
                )
            )
        weights = []
        for j in pairs:
            x_bias = jnp.concatenate(
                [lookup(tab_ref[2 * j + e : 2 * j + e + 1, 128:256], index) for e in (0, 1)], axis=0
            )
            biased = scores[j] + rb_ref[i, 128 * j : 128 * j + 128, :] + x_bias
            peak = jnp.max(biased, axis=1, keepdims=True)
            raised = jnp.exp(biased - peak)
            weights.append(raised.astype(BF16))
        ones = jnp.ones((KEYS, 128), BF16)
        joint = [
            dot(weights[j], jnp.concatenate([key_tile(kv_ref, i, WIDTH + 128 * j), ones], axis=1))
            for j in pairs
        ]
        contexts = []
        for j in pairs:
            share = 1.0 / joint[j][:, 128:]
            contexts.append(joint[j][:, :128] * share)
            share = jnp.concatenate([share, share], axis=1)
            weights[j] = (weights[j].astype(F32) * share).astype(BF16)
        for j in pairs:
            p_ref[0, i, 128 * j : 128 * j + 128, :] = weights[j]
        ctx_s[pl.ds(start, ROWS), :] = jnp.concatenate(
            [head_join(c).astype(BF16) for c in contexts], axis=1
        )
        return 0

    lax.fori_loop(0, blocks, block, 0, unroll=blocks)
    ctx_ref[0] = ctx_s[:rows]


def page_block(*shape):
    return pl.BlockSpec((1,) + shape, lambda p, *_: (p,) + (0,) * len(shape))


def whole(*shape):
    return pl.BlockSpec(shape, lambda *_: (0,) * len(shape))


def attention_forward(
    band, lengths, hidden, got, x_coord, line_ids, qkv_w, vectors, tables
):
    pages, rows, width = hidden.shape
    blocks = -(-rows // ROWS)
    padded = blocks * ROWS
    ext = padded + 3 * HALF
    shape = jax.ShapeDtypeStruct
    return pl.pallas_call(
        attention_kernel,
        out_shape=(
            pltpu.HBM((pages, rows, width), BF16),
            pltpu.HBM((pages, blocks, HEADS * ROWS, KEYS), BF16),
            pltpu.HBM((pages, padded, width), BF16),
            pltpu.HBM((pages, ext, 2 * width), BF16),
            pltpu.HBM((pages, rows + 2 * HALF, width), BF16),
        ),
        grid_spec=pltpu.PrefetchScalarGridSpec(
            num_scalar_prefetch=2,
            grid=(pages,),
            in_specs=[
                page_block(rows, width),
                page_block(2 * HALF, width),
                whole(*x_coord.shape),
                whole(*line_ids.shape),
                whole(width, 3 * width),
                whole(*vectors.shape),
                whole(*tables.shape),
            ],
            out_specs=[
                page_block(rows, width),
                page_block(blocks, HEADS * ROWS, KEYS),
                page_block(padded, width),
                page_block(ext, 2 * width),
                page_block(rows + 2 * HALF, width),
            ],
            scratch_shapes=[
                pltpu.VMEM((8, KEYS), F32),
                pltpu.VMEM((8, KEYS), F32),
                pltpu.VMEM((blocks, HEADS * ROWS, KEYS), F32),
                pltpu.VMEM((CLASSES, HEADS * CLASSES), BF16),
                pltpu.VMEM((padded, width), BF16),
                pltpu.VMEM((16, 384), F32),
            ],
        ),
        compiler_params=pltpu.CompilerParams(vmem_limit_bytes=44 << 20),
        cost_estimate=pl.CostEstimate(
            flops=2 * pages * (rows + 2 * HALF) * width * 3 * width
            + 8 * pages * padded * HEADS * KEYS * 128,
            bytes_accessed=30 << 20,
            transcendentals=pages * padded * HEADS * KEYS,
        ),
        name="attention_forward",
    )(
        band, lengths, *far_away(hidden), got, x_coord, line_ids, *far_away(qkv_w), vectors, tables,
    )


def layer_norm(total):
    centred = total - jnp.mean(total, axis=1, keepdims=True)
    inverse = lax.rsqrt(jnp.mean(centred * centred, axis=1, keepdims=True) + EPSILON)
    return centred * inverse, inverse


def norm_back(grad, normed, inverse, gain):
    scaled = grad * gain
    return inverse * (
        scaled
        - jnp.mean(scaled, axis=1, keepdims=True)
        - normed * jnp.mean(scaled * normed, axis=1, keepdims=True)
    )


def gelu_parts(inner):
    size = jnp.abs(inner)
    falling = jnp.exp(inner * inner * -0.5)
    t = 1.0 / (1.0 + (0.3275911 * math.sqrt(0.5)) * size)
    poly = 1.061405429 * t - 1.453152027
    poly = poly * t + 1.421413741
    poly = poly * t - 0.284496736
    poly = poly * t + 0.254829592
    tail = (0.5 * poly) * (t * falling)
    share = jnp.where(inner >= 0.0, 1.0 - tail, tail)
    return inner * share, share + inner * falling * (2.0 * math.pi) ** (-0.5)


def column_sum(values):
    return jnp.sum(values, axis=0, keepdims=True)


def accumulate(ref, row, value):
    first = pl.program_id(0) == 0

    @pl.when(first)
    def _():
        ref[row : row + 1, :] = value

    @pl.when(jnp.logical_not(first))
    def _():
        ref[row : row + 1, :] = ref[row : row + 1, :] + value


def fixed(*shape):
    return pl.BlockSpec(shape, lambda *_: (0,) * len(shape), pipeline_mode=pl.Buffered(1))


def resident():
    return pl.BlockSpec(memory_space=pltpu.VMEM)


FORWARD_CUT = 768
CUT = 768
BLOCKS = 6


def ffn_forward_kernel(
    ctx_ref, hid_ref, cot_ref, vec_ref, bin_ref, wo_ref, w1_ref, w2_ref,
    out_ref, first_ref, norm_ref, inv_ref, act_ref, slope_ref, dh_ref, ds_ref, sums_ref,
    second_s,
):
    step = pl.program_id(0)

    def vector(row):
        return vec_ref[row : row + 1, :].astype(F32)

    @pl.when(step == 0)
    def _():
        attended = dot(ctx_ref[...], wo_ref[...]) + vector(OUT_B)
        normed, inverse = layer_norm(hid_ref[...].astype(F32) + attended)
        first = (normed * vector(LN1_G) + vector(LN1_B)).astype(BF16)
        first_ref[...] = first
        norm_ref[...] = normed
        inv_ref[...] = jnp.broadcast_to(inverse, inv_ref.shape)
        second_s[...] = first.astype(F32) + vector(FFN_OUT_B)

    size = first_ref.shape[0] // BLOCKS
    parts = [slice(size * r, size * r + size) for r in range(BLOCKS)]
    w1, w2 = w1_ref[...], w2_ref[...]
    offset = bin_ref[...].astype(F32)

    def inner_of(r):
        return dot(first_ref[parts[r], :], w1) + offset

    def feed(r, act):
        second_s[parts[r], :] = second_s[parts[r], :] + dot(act, w2)

    ahead, behind = inner_of(0), None
    for r in range(BLOCKS):
        inner = ahead
        if r + 1 < BLOCKS:
            ahead = inner_of(r + 1)
        act, slope = gelu_parts(inner)
        act = act.astype(BF16)
        act_ref[parts[r], :] = act
        slope_ref[parts[r], :] = slope.astype(BF16)
        if r > 0:
            feed(r - 1, behind)
        behind = act
    feed(BLOCKS - 1, behind)

    @pl.when(step == pl.num_programs(0) - 1)
    def _():
        normed2, inverse2 = layer_norm(second_s[...])
        out_ref[...] = (normed2 * vector(LN2_G) + vector(LN2_B)).astype(BF16)
        grad = cot_ref[...].astype(F32)
        back = norm_back(grad, normed2, inverse2, vector(LN2_G))
        low = back.astype(BF16)
        dh_ref[...] = back
        ds_ref[...] = low
        sums_ref[0:1, :] = column_sum(grad * normed2)
        sums_ref[1:2, :] = column_sum(grad)
        sums_ref[2:3, :] = column_sum(low.astype(F32))


def ffn_forward(context, hidden, cotangent, vectors, ffn_in_b, out_w, ffn_in_w, ffn_out_w):
    tokens, width = context.shape
    shape = jax.ShapeDtypeStruct
    rows = fixed(tokens, width)
    step = FORWARD_CUT
    wide = pl.BlockSpec((tokens, step), lambda i: (0, i))
    return pl.pallas_call(
        ffn_forward_kernel,
        out_shape=(
            pltpu.HBM((tokens, width), BF16),
            shape((tokens, width), BF16),
            shape((tokens, width), F32),
            shape((tokens, 128), F32),
            pltpu.HBM((tokens, FF), BF16),
            pltpu.HBM((tokens, FF), BF16),
            shape((tokens, width), F32),
            shape((tokens, width), BF16),
            shape((8, width), F32),
        ),
        grid=(FF // step,),
        in_specs=[
            rows, rows, rows,
            whole(*vectors.shape),
            pl.BlockSpec((1, step), lambda i: (0, i)),
            fixed(width, width),
            pl.BlockSpec((width, step), lambda i: (0, i)),
            pl.BlockSpec((step, width), lambda i: (i, 0)),
        ],
        out_specs=[
            rows, resident(), resident(), resident(),
            wide, wide, resident(), resident(),
            whole(8, width),
        ],
        scratch_shapes=[pltpu.VMEM((tokens, width), F32)],
        compiler_params=pltpu.CompilerParams(vmem_limit_bytes=36 << 20),
        cost_estimate=pl.CostEstimate(
            flops=2 * tokens * width * (2 * FF + width),
            bytes_accessed=40 << 20,
            transcendentals=tokens * FF,
        ),
        name="ffn_forward",
    )(
        *far_away(context, hidden, cotangent), vectors, ffn_in_b,
        *far_away(out_w, ffn_in_w, ffn_out_w),
    )


def ffn_parts(owner, ds_ref, first_ref, act_ref, slope_ref, w1_ref, w2_ref, parts_ref, bsum_ref):
    step = pl.program_id(0)
    chunks, size, _ = parts_ref.shape
    orders = split_orders(chunks, True)
    low = ds_ref[...]
    grad = dot(low, w2_ref[...], NT)
    inner = (grad * slope_ref[...].astype(F32)).astype(BF16)
    out_part = dot(act_ref[...], low, TN).astype(BF16)
    in_part = dot(inner, first_ref[...], TN).astype(BF16)
    bsum_ref[...] = column_sum(inner.astype(F32))
    for c in range(CUT // size):
        chunk = step * (CUT // size) + c
        spot = jnp.where(owner == 0, place(chunk, orders[0]), place(chunk, orders[1]))
        part = slice(size * c, size * c + size)
        parts_ref[spot] = jnp.concatenate([in_part[part], out_part[part]], axis=1)
    return dot(inner, w1_ref[...], NT)


def ffn_back_far_kernel(
    band_ref, ds_ref, first_ref, act_ref, slope_ref, w1_ref, w2_ref, dh_ref,
    parts_ref, bsum_ref, total_ref,
):
    added = ffn_parts(
        1 - band_ref[0], ds_ref, first_ref, act_ref, slope_ref, w1_ref, w2_ref, parts_ref, bsum_ref
    )

    @pl.when(pl.program_id(0) == 0)
    def _():
        total_ref[...] = dh_ref[...] + added

    @pl.when(pl.program_id(0) > 0)
    def _():
        total_ref[...] = total_ref[...] + added


def ffn_back_own_kernel(
    band_ref, ds_ref, first_ref, act_ref, slope_ref, w1_ref, w2_ref, part_ref, norm_ref, inv_ref,
    vec_ref, wo_ref,
    parts_ref, bsum_ref, dh1_ref, da_ref, dc_ref, sums_ref,
    total_s,
):
    added = ffn_parts(
        band_ref[0], ds_ref, first_ref, act_ref, slope_ref, w1_ref, w2_ref, parts_ref, bsum_ref
    )

    @pl.when(pl.program_id(0) == 0)
    def _():
        total_s[...] = part_ref[...] + added

    @pl.when(pl.program_id(0) > 0)
    def _():
        total_s[...] = total_s[...] + added

    @pl.when(pl.program_id(0) == pl.num_programs(0) - 1)
    def _():
        total = total_s[...]
        normed = norm_ref[...]
        gain = vec_ref[LN1_G : LN1_G + 1, :].astype(F32)
        back = norm_back(total, normed, inv_ref[:, 0:1], gain)
        low = back.astype(BF16)
        dh1_ref[...] = back
        da_ref[...] = low
        dc_ref[...] = dot(low, wo_ref[...], NT).astype(BF16)
        sums_ref[0:1, :] = column_sum(total * normed)
        sums_ref[1:2, :] = column_sum(total)
        sums_ref[2:3, :] = column_sum(low.astype(F32))


def ffn_back_call(own, band, second_low, first, act, slope, ffn_in_w, ffn_out_w, extra, chunks):
    tokens, width = second_low.shape
    half = FF // 2
    steps = half // CUT
    shape = jax.ShapeDtypeStruct
    rows = fixed(tokens, width)

    def at(i, b):
        return (b[0] if own else 1 - b[0]) * steps + i

    in_specs = [
        resident(), resident(),
        pl.BlockSpec((tokens, CUT), lambda i, b: (0, at(i, b))),
        pl.BlockSpec((tokens, CUT), lambda i, b: (0, at(i, b))),
        pl.BlockSpec((width, CUT), lambda i, b: (0, at(i, b))),
        pl.BlockSpec((CUT, width), lambda i, b: (at(i, b), 0)),
    ] + ([resident()] * 3 + [fixed(*e.shape) for e in extra[3:]] if own else [resident()])
    out_shape = [
        pltpu.HBM((chunks // 2, FF // chunks, 2 * width), BF16),
        shape((1, half), F32),
    ]
    out_specs = [
        fixed(chunks // 2, FF // chunks, 2 * width),
        pl.BlockSpec((1, CUT), lambda i, b: (0, i)),
    ]
    if own:
        out_shape += [
            pltpu.HBM((tokens, width), F32), pltpu.HBM((tokens, width), BF16),
            pltpu.HBM((tokens, width), BF16), shape((8, width), F32),
        ]
        out_specs += [rows, rows, rows, whole(8, width)]
    else:
        out_shape += [shape((tokens, width), F32)]
        out_specs += [resident()]
    return pl.pallas_call(
        ffn_back_own_kernel if own else ffn_back_far_kernel,
        out_shape=out_shape,
        grid_spec=pltpu.PrefetchScalarGridSpec(
            num_scalar_prefetch=1,
            grid=(steps,),
            in_specs=in_specs,
            out_specs=out_specs,
            scratch_shapes=[pltpu.VMEM((tokens, width), F32)] if own else [],
        ),
        compiler_params=pltpu.CompilerParams(vmem_limit_bytes=34 << 20),
        cost_estimate=pl.CostEstimate(
            flops=8 * tokens * width * half, bytes_accessed=30 << 20, transcendentals=0
        ),
        name="ffn_back_own" if own else "ffn_back_far",
    )(
        band, second_low, first, *far_away(act, slope, ffn_in_w, ffn_out_w),
        *(extra[:-1] + tuple(far_away(extra[-1])) if own else extra),
    )


def attention_back_kernel(
    p_ref, q_ref, kv_ref, dc_ref,
    dm_ref, ds_ref,
    dkv_ref, dc_s, dq_s,
):
    rows = dc_ref.shape[1]
    blocks = q_ref.shape[1] // ROWS
    dkv_ref[...] = jnp.zeros_like(dkv_ref)
    dc_s[:rows] = dc_ref[0]
    dc_s[rows:] = jnp.zeros((dc_s.shape[0] - rows, WIDTH), BF16)
    def block(i, _):
        start = pl.multiple_of(ROWS * i, ROWS)
        window = pl.ds(pl.multiple_of(HALF + ROWS * i, ROWS), 3 * HALF)
        pairs = range(HEADS // 2)
        grads = []
        for j in pairs:
            column = 128 * j
            grads.append(head_split(dc_s[pl.ds(start, ROWS), column : column + 128]))
        dprobs = [dot(grads[j], key_tile(kv_ref, i, WIDTH + 128 * j), NT) for j in pairs]
        for j in pairs:
            dv = dot(p_ref[0, i, 128 * j : 128 * j + 128, :], grads[j], TN)
            column = WIDTH + 128 * j
            cut = slice(column, column + 128)
            dkv_ref[0:HALF, cut] = dkv_ref[0:HALF, cut] + dv[:HALF]
            dkv_ref[window, cut] = dkv_ref[window, cut] + dv[HALF:]
        lows = []
        for j in pairs:
            probs = p_ref[0, i, 128 * j : 128 * j + 128, :].astype(F32)
            grad = probs * (
                dprobs[j] - jnp.sum(probs * dprobs[j], axis=1, keepdims=True)
            )
            lows.append(grad.astype(BF16))
        dq = [head_join(dot(lows[j], key_tile(kv_ref, i, 128 * j))) for j in pairs]
        dq_s[pl.ds(start, ROWS), :] = (jnp.concatenate(dq, axis=1) * 0.125).astype(BF16)
        for j in pairs:
            cut = slice(128 * j, 128 * j + 128)
            dk = dot(lows[j], head_split(q_ref[0, pl.ds(start, ROWS), cut]), TN)
            dkv_ref[0:HALF, cut] = dkv_ref[0:HALF, cut] + dk[:HALF]
            dkv_ref[window, cut] = dkv_ref[window, cut] + dk[HALF:]

        for j in pairs:
            ds_ref[0, i, 128 * j : 128 * j + 128, :] = lows[j]
        return 0

    lax.fori_loop(0, blocks, block, 0, unroll=blocks)
    dm_ref[0, : 2 * HALF, :WIDTH] = jnp.zeros((2 * HALF, WIDTH), BF16)
    dm_ref[0, 2 * HALF :, :WIDTH] = dq_s[:rows]
    dm_ref[0, :HALF, WIDTH:] = dkv_ref[:HALF].astype(BF16)
    dm_ref[0, HALF : 2 * HALF, WIDTH:] = (
        dkv_ref[HALF : 2 * HALF] + dkv_ref[2 * HALF + rows : 3 * HALF + rows]
    ).astype(BF16)
    dm_ref[0, 2 * HALF :, WIDTH:] = dkv_ref[2 * HALF : 2 * HALF + rows].astype(BF16)


def attention_backward(probs, queries, pairs, grad_context):
    pages, rows, width = grad_context.shape
    padded = queries.shape[1]
    blocks = padded // ROWS
    ext = pairs.shape[1]
    shape = jax.ShapeDtypeStruct
    return pl.pallas_call(
        attention_back_kernel,
        out_shape=(
            pltpu.HBM((pages, rows + 2 * HALF, 3 * width), BF16),
            pltpu.HBM(probs.shape, BF16),
        ),
        grid=(pages,),
        in_specs=[
            page_block(blocks, HEADS * ROWS, KEYS),
            page_block(padded, width),
            page_block(ext, 2 * width),
            page_block(rows, width),
        ],
        out_specs=[page_block(rows + 2 * HALF, 3 * width), page_block(blocks, HEADS * ROWS, KEYS)],
        scratch_shapes=[
            pltpu.VMEM((ext, 2 * width), F32),
            pltpu.VMEM((padded, width), BF16),
            pltpu.VMEM((padded, width), BF16),
        ],
        compiler_params=pltpu.CompilerParams(vmem_limit_bytes=56 << 20),
        cost_estimate=pl.CostEstimate(
            flops=10 * pages * padded * HEADS * KEYS * 128, bytes_accessed=30 << 20, transcendentals=0
        ),
        name="attention_backward",
    )(*far_away(probs, queries, pairs, grad_context))


def table_kernel(
    blocks, start, band_ref, ds_ref, x_ref, line_ref, tab_ref, kx_ref, kc_ref, left_ref, right_ref,
    index_ref,
):
    step = pl.program_id(0)
    band = band_ref[0]
    page = (start + step) // blocks
    i = (start + step) % blocks
    first_pos = band * (x_ref.shape[-1] // 2)

    @pl.when((step == 0) | (i == 0))
    def _():
        own = pl.ds(page, 1)
        stage_geometry(first_pos, band, x_ref[own, :], line_ref[own, :], kx_ref, kc_ref, blocks)

    slots = iota((REL_BUCKETS + 2 * XY_BUCKETS, KEYS), 0).astype(F32).astype(BF16)
    one = jnp.ones((), BF16)
    zero = jnp.zeros((), BF16)

    left_ref[...] = ds_ref[0, :, :128].astype(F32)
    right_ref[...] = ds_ref[0, :, 128:].astype(F32)
    kx = kx_ref[pl.ds(i, 1), :]
    ky = class_y(kc_ref[pl.ds(i, 1), :].astype(I32))
    index_ref[0:ROWS] = bucket(kx - column_of(kx[:, 2 * HALF : 3 * HALF]), XY_BUCKETS, XY_REACH)
    index_ref[ROWS : 2 * ROWS] = 64.0 + bucket(
        ky - column_of(ky[:, 2 * HALF : 3 * HALF]), XY_BUCKETS, XY_REACH
    )
    index_ref[2 * ROWS : 3 * ROWS] = 128.0 + rel_buckets(first_pos, i)

    def table_row(q, acc):
        own = jnp.concatenate(
            [
                jnp.broadcast_to(index_ref[pl.ds(q, 1), :], (XY_BUCKETS, KEYS)),
                jnp.broadcast_to(index_ref[pl.ds(ROWS + q, 1), :], (XY_BUCKETS, KEYS)),
                jnp.broadcast_to(index_ref[pl.ds(2 * ROWS + q, 1), :], (REL_BUCKETS, KEYS)),
            ],
            axis=0,
        ).astype(BF16)
        heads = jnp.concatenate(
            [
                left_ref[pl.ds(q, HEADS, stride=ROWS), :],
                right_ref[pl.ds(q, HEADS, stride=ROWS), :],
            ],
            axis=1,
        ).astype(BF16)
        return acc + dot(heads, jnp.where(slots == own, one, zero), NT)

    table_sum = lax.fori_loop(
        0, ROWS, table_row, jnp.zeros(tab_ref.shape, F32), unroll=ROWS
    )

    @pl.when(step == 0)
    def _():
        tab_ref[...] = table_sum

    @pl.when(step > 0)
    def _():
        tab_ref[...] = tab_ref[...] + table_sum


def table_sums(band, start, count, grad_scores, x_coord, line_ids):
    pages, blocks, height, keys = grad_scores.shape
    buckets = REL_BUCKETS + 2 * XY_BUCKETS
    return pl.pallas_call(
        functools.partial(table_kernel, blocks, start),
        out_shape=jax.ShapeDtypeStruct((HEADS, buckets), F32),
        grid_spec=pltpu.PrefetchScalarGridSpec(
            num_scalar_prefetch=1,
            grid=(count,),
            in_specs=[
                pl.BlockSpec((1, height, keys), lambda i, *_: (start + i, 0, 0)),
                whole(*x_coord.shape),
                whole(*line_ids.shape),
            ],
            out_specs=whole(HEADS, buckets),
            scratch_shapes=[
                pltpu.VMEM((8, KEYS), F32),
                pltpu.VMEM((8, KEYS), F32),
                pltpu.VMEM((height, 128), F32),
                pltpu.VMEM((height, 128), F32),
                pltpu.VMEM((3 * ROWS, KEYS), F32),
            ],
        ),
        compiler_params=pltpu.CompilerParams(vmem_limit_bytes=40 << 20),
        cost_estimate=BRIEF,
        name="table_sums",
    )(band, *far_away(grad_scores.reshape(pages * blocks, height, keys)), x_coord, line_ids)


def hidden_back_kernel(dm_ref, dh_ref, w_ref, *refs):
    own_ref, far_ref = refs[-2:]
    own_ref[0] = dh_ref[0] + dot(dm_ref[0, 2 * HALF :], w_ref[...], NT)
    far_ref[0] = dot(dm_ref[0, : 2 * HALF, WIDTH:], w_ref[:, WIDTH:], NT).astype(BF16)


def hidden_backward(page, count, outs, grad_mixed, grad_total, qkv_w):
    pages, rows, width = grad_total.shape

    def one(*shape):
        return pl.BlockSpec((1,) + shape, lambda i: (page + i, 0, 0))

    return pl.pallas_call(
        hidden_back_kernel,
        out_shape=(
            pltpu.HBM((pages, rows, width), F32),
            pltpu.HBM((pages, 2 * HALF, width), BF16),
        ),
        grid=(count,),
        in_specs=[
            one(rows + 2 * HALF, 3 * width),
            one(rows, width),
            whole(width, 3 * width),
        ]
        + [pl.BlockSpec(memory_space=pl.ANY)] * len(outs),
        out_specs=[one(rows, width), one(2 * HALF, width)],
        input_output_aliases={3 + i: i for i in range(len(outs))},
        compiler_params=pltpu.CompilerParams(vmem_limit_bytes=60 << 20),
        cost_estimate=BRIEF,
        name="hidden_backward",
    )(*far_away(grad_mixed, grad_total, qkv_w), *outs)


def edge_kernel(band_ref, grad_ref, far_ref, got_ref, out_ref):
    band = band_ref[0]
    side = pl.program_id(0)
    edge = HALF // 2
    for s in range(4):

        @pl.when(side == s)
        def _():
            part = slice(edge * (s % 2), edge * (s % 2) + edge)
            rim = slice(HALF + part.start, HALF + part.stop)
            if s < 2:
                own = far_ref[:, part].astype(F32) + got_ref[:, part].astype(F32)
                added = jnp.where(band == 0, own, got_ref[:, rim].astype(F32))
            else:
                added = jnp.where(band == 0, got_ref[:, rim].astype(F32), 0.0)
            out_ref[...] = grad_ref[...] + added


def edge_add(band, grad, far, got):
    pages, rows, width = grad.shape
    half = HALF // 2
    last = rows // half - 2

    def edge(s, *_):
        return (0, jnp.where(s < 2, s, last + s - 2), 0)

    return pl.pallas_call(
        edge_kernel,
        out_shape=jax.ShapeDtypeStruct(grad.shape, F32),
        grid_spec=pltpu.PrefetchScalarGridSpec(
            num_scalar_prefetch=1,
            grid=(4,),
            in_specs=[
                pl.BlockSpec((pages, half, width), edge),
                whole(*far.shape),
                whole(*got.shape),
            ],
            out_specs=pl.BlockSpec((pages, half, width), edge),
        ),
        input_output_aliases={1: 0},
        cost_estimate=BRIEF,
        name="edge_add",
    )(band, grad, far, got)


def split_orders(count, mixed=False):
    total = count.bit_length() - 1
    side = total // 3
    x, y, z = (range(side), range(side, 2 * side), range(2 * side, total))
    if mixed:
        return [*x, *z[:-1], *y, z[-1]], [*y, *z[:-1], *x, z[-1]]
    return [*x, *y, *z], [*y, *x, *z]


def place(chunk, order):
    spot = 0
    for level, bit in enumerate(order):
        spot = spot + (((chunk >> bit) & 1) << (len(order) - 1 - level))
    return spot


def product_halves(band, tokens_ext, grad_mixed, context, grad_attn):
    tokens, height = tokens_ext.shape
    width = grad_mixed.shape[1]
    step = height // 2

    def kernel(band_ref, l_ref, r_ref, l2_ref, r2_ref, send_ref, keep_ref, sums_ref):
        def write(ref):
            ref[:, :width] = dot(l_ref[...], r_ref[...], TN).astype(BF16)
            ref[:, width:] = dot(l2_ref[...], r2_ref[...], TN).astype(BF16)

        @pl.when(pl.program_id(0) == 0)
        def _():
            write(send_ref)
            sums_ref[...] = dot(jnp.ones((tokens, 8), BF16), r_ref[...], TN)

        pl.when(pl.program_id(0) == 1)(lambda: write(keep_ref))

    def at(i, b):
        return (0, jnp.where(i == 0, 1 - b[0], b[0]))

    out = pltpu.HBM((step, width + height), BF16)
    return pl.pallas_call(
        kernel,
        out_shape=(out, out, jax.ShapeDtypeStruct((8, width), F32)),
        grid_spec=pltpu.PrefetchScalarGridSpec(
            num_scalar_prefetch=1,
            grid=(2,),
            in_specs=[
                pl.BlockSpec((tokens, step), at),
                fixed(*grad_mixed.shape),
                pl.BlockSpec((context.shape[0], step), at),
                fixed(*grad_attn.shape),
            ],
            out_specs=[
                fixed(step, width + height), fixed(step, width + height), fixed(8, width)
            ],
        ),
        compiler_params=pltpu.CompilerParams(vmem_limit_bytes=60 << 20),
        cost_estimate=pl.CostEstimate(
            flops=2 * tokens * height * (width + height), bytes_accessed=16 << 20, transcendentals=0
        ),
        name="product_halves",
    )(band, *far_away(tokens_ext, grad_mixed, context, grad_attn))


def swap_bands(block):
    return lax.ppermute(block, "band", [(0, 1), (1, 0)])


def swap_pages(block, level, orders):
    count = lax.axis_size("page")
    route = [
        (b * count + p, b * count + (p ^ (1 << orders[b][level])))
        for b in range(2)
        for p in range(count)
    ]
    return lax.ppermute(block, ("band", "page"), route)


def sides(orders):
    band, page = lax.axis_index("band"), lax.axis_index("page")
    return [
        jnp.where(band == 0, (page >> first) & 1, (page >> second) & 1)
        for first, second in zip(*orders)
    ]


def widen(band, block, own, outs, shapes):
    half, width = shapes[0][0] // 2, block.shape[1]
    steps = 4
    step = half // steps
    edges = [sum(shape[1] for shape in shapes[:i]) for i in range(len(shapes) + 1)]

    def kernel(band_ref, block_ref, *refs):
        for out, start, stop in zip(refs[-len(shapes) :], edges, edges[1:]):
            out[...] = block_ref[:, start:stop].astype(F32)

    def at(i, b):
        return ((b[0] if own else 1 - b[0]) * steps + i, 0)

    return pl.pallas_call(
        kernel,
        out_shape=[pltpu.HBM(shape, F32) for shape in shapes],
        grid_spec=pltpu.PrefetchScalarGridSpec(
            num_scalar_prefetch=1,
            grid=(steps,),
            in_specs=[pl.BlockSpec((step, width), lambda i, *_: (i, 0))]
            + [pl.BlockSpec(memory_space=pl.ANY)] * len(outs),
            out_specs=[pl.BlockSpec((step, shape[1]), at) for shape in shapes],
        ),
        input_output_aliases={2 + i: i for i in range(len(outs))},
        compiler_params=pltpu.CompilerParams(vmem_limit_bytes=40 << 20),
        cost_estimate=BRIEF,
        name="widen",
    )(band, block, *outs)


class Order:
    def __init__(self):
        self.mark = None

    def __call__(self, part, *args):
        if self.mark is not None:
            leaves, tree = jax.tree.flatten(args)
            leaves = lax.optimization_barrier((*leaves, self.mark))[:-1]
            args = jax.tree.unflatten(tree, leaves)
        out = part(*args)
        self.mark = jax.tree.leaves(out)[0]
        return out

    def late(self, block):
        return lax.optimization_barrier((block, self.mark))[0]


def halving_plan(size, orders):
    starts, spots = [], [[0, 0]]
    for side in sides(orders):
        size = size // 2
        starts.append([at + (1 - side) * size for at in spots[-1]])
        spots.append([at + side * size for at in spots[-1]] + [0])
    return starts, spots


class Halving:
    def __init__(self, order, send, keep, orders, plan):
        self.order = order
        self.orders = orders
        self.starts, self.spots, self.sides = plan
        self.level = 0
        self.held = [keep]
        self.size = keep.shape[0]
        self.flight = swap_bands(send)

    def land(self):
        self.held.append(self.flight)
        self.flight = None

    def total(self, size):
        def add(spots, *held):
            parts = [
                lax.dynamic_slice_in_dim(block, at, size, 0, allow_negative_indices=False)
                for block, at in zip(held, spots)
            ]
            return sum([part.astype(F32) for part in parts[1:]], parts[0].astype(F32))

        return add

    def step(self):
        self.gather()
        self.send(self.sent)

    def gather(self):
        self.land()
        self.size //= 2
        add = self.total(self.size)
        self.sent = self.order(
            lambda *a: add(*a).astype(BF16), self.starts[self.level], *self.held
        )

    def send(self, sent):
        self.flight = swap_pages(sent, self.level, self.orders)
        self.level += 1

    def send_late(self):
        self.send(self.order.late(self.sent))

    def finish(self, wrap):
        self.land()
        add = self.total(self.size)
        return self.order(lambda *a: wrap(add(*a)), self.spots[self.level], *self.held)

    def meet(self):
        self.land()
        add = self.total(self.size)
        mine = self.order(lambda *a: add(*a).astype(BF16), self.spots[self.level], *self.held)
        self.flight = swap_pages(mine, self.level, self.orders)
        self.mine = mine

    def met(self):
        self.mine = self.order(
            lambda a, b: (a.astype(F32) + b.astype(F32)).astype(BF16), self.mine, self.flight
        )
        self.rider = None
        self.level -= 1
        self.flight = swap_pages(self.mine, self.level, self.orders)

    def after(self, other):
        self.mine, other.flight = lax.optimization_barrier((self.mine, other.flight))

    def grow(self, rider=None):
        size = self.mine.shape[0]
        if self.level == 0:
            self.mine, self.rider = self.order(
                lambda mine, got, rider, side: (
                    join(mine, got[:size], side), rider + rider_of(got[size:])
                ),
                self.mine, self.flight, self.rider, self.sides[0],
            )
            self.level -= 1
            self.flight = swap_bands(self.mine)
            self.rider_flight = swap_bands(self.rider)
            return
        if rider is None and self.rider is None:
            self.mine = self.order(join, self.mine, self.flight, self.sides[self.level])
            sent = self.mine
        else:
            first = rider is not None

            def both(mine, got, rider, side):
                if not first:
                    rider = rider + rider_of(got[size:])
                return with_rider(join(mine, got[:size], side), rider)

            sent, self.mine, self.rider = self.order(
                both, self.mine, self.flight, rider if first else self.rider,
                self.sides[self.level],
            )
        self.level -= 1
        self.flight = swap_pages(sent, self.level, self.orders)

    def last_rider(self):
        return self.order(lambda a, b: a + b, self.rider, self.rider_flight)


def with_rider(block, rider):
    high = lax.reduce_precision(rider, 8, 7)
    low = (rider - high).astype(BF16)
    return jnp.concatenate([block, high.astype(BF16), low], axis=0), block, rider


def rider_of(rows):
    half = rows.shape[0] // 2
    return rows[:half].astype(F32) + rows[half:].astype(F32)


def join(mine, other, side):
    return jnp.where(
        side == 0,
        jnp.concatenate([mine, other], axis=0),
        jnp.concatenate([other, mine], axis=0),
    )


def flat(block):
    return block.reshape(-1, block.shape[-1])


def local(
    hidden, cotangent, page_lengths, x_coord, line_ids, qkv_w, q_bias, v_bias,
    rel_table, x_table, y_table, out_w, out_b, ln1_gain, ln1_bias,
    ffn_in_w, ffn_in_b, ffn_out_w, ffn_out_b, ln2_gain, ln2_bias,
):
    pages, rows, width = hidden.shape
    band = lax.axis_index("band")
    chunks = 2 * lax.axis_size("page")
    band_arr = band.reshape(1).astype(I32)
    own_edge = jnp.where(band == 0, hidden[:, rows - HALF :], hidden[:, :HALF])
    got = swap_bands(jnp.concatenate([hidden[:, :HALF], own_edge], axis=1))
    half = chunks // 2
    ffn_orders, attn_orders = split_orders(half, True), split_orders(half)
    plans = [
        (*halving_plan(size, orders), sides(orders))
        for size, orders in ((half, ffn_orders), (width // 2, attn_orders))
    ]
    got, plans = lax.optimization_barrier((got, plans))
    ffn_plan, attn_plan = plans
    vectors = jnp.concatenate(
        [out_b, ln1_gain, ln1_bias, ffn_out_b, ln2_gain, ln2_bias, q_bias, v_bias]
    ).reshape(8, width)
    tables = jnp.concatenate([rel_table, x_table, y_table], axis=0)
    context, probs, queries, pairs, extended = attention_forward(
        band_arr, page_lengths, hidden, got, x_coord, line_ids, qkv_w, vectors, tables
    )
    output, first, normed, inverse, act, slope, grad_total2, second_low, sums2 = ffn_forward(
        flat(context), flat(hidden), flat(cotangent), vectors,
        ffn_in_b.reshape(1, FF), out_w, ffn_in_w, ffn_out_w,
    )
    order = Order()
    send, bsum_far, part = order(
        lambda *a: ffn_back_call(False, band_arr, *a, chunks),
        second_low, first, act, slope, ffn_in_w, ffn_out_w, (grad_total2,),
    )
    keep, bsum_own, grad_total1, attn_low, grad_context, sums1 = order(
        lambda *a: ffn_back_call(True, band_arr, *a, chunks),
        second_low, first, act, slope, ffn_in_w, ffn_out_w,
        (part, normed, inverse, vectors, out_w),
    )
    ffn = Halving(order, send, keep, ffn_orders, ffn_plan)
    ffn.step()
    grad_mixed, grad_scores = order(
        attention_backward, probs, queries, pairs, grad_context.reshape(pages, rows, width)
    )
    send, keep, mixed_sums = order(
        product_halves, band_arr, flat(extended), flat(grad_mixed), flat(context), attn_low
    )
    attn = Halving(order, send, keep, attn_orders, attn_plan)
    ffn.step()
    attn.step()
    total = grad_scores.shape[0] * grad_scores.shape[1]
    marks = [0, total // 3, total // 3 + 2, 2 * total // 3, total]

    def tables_of(piece):
        start, stop = marks[piece : piece + 2]
        return order(
            lambda *a: table_sums(band_arr, start, stop - start, *a),
            grad_scores, x_coord, line_ids,
        )

    tables = [tables_of(0)]
    attn.step()
    tables.append(tables_of(1))
    attn.step()
    while ffn.level < len(ffn.sides) - 1:
        ffn.step()
    tables.append(tables_of(2))
    inner_sums = order(
        lambda own, far: jnp.where(
            band == 0,
            jnp.concatenate([own, far], axis=1),
            jnp.concatenate([far, own], axis=1),
        ),
        bsum_own, bsum_far,
    )
    attn.meet()
    tables.append(tables_of(3))
    rider = order(
        lambda m, a, b, c, *t: jnp.pad(
            jnp.concatenate(
                [
                    m[0].reshape(3, width), a[:3], b[:3], c.reshape(FF // width, width),
                    jnp.pad(sum(t[1:], t[0]), ((0, 3), (0, width - t[0].shape[1]))),
                ],
                axis=0,
            ).reshape(7, 4 * width),
            ((0, 1), (0, 0)),
        ),
        mixed_sums, sums1, sums2, inner_sums, *tables,
    )
    levels = len(attn.sides)
    flat_levels = 2 * (levels // 3)
    got = swap_pages(rider, levels - 1, attn.orders)
    attn.met()
    ffn.gather()
    grads = ()

    def hidden_of(page, count):
        return order(
            lambda outs, *a: hidden_backward(page, count, outs, *a),
            grads, grad_mixed, grad_total1.reshape(pages, rows, width), qkv_w,
        )

    for level in reversed(range(flat_levels, levels - 1)):
        rider = order(lambda a, b: a + b, rider, got)
        got = swap_pages(rider, level, attn.orders)
    rider = order(lambda a, b: a + b, rider, got)
    while attn.level > flat_levels:
        attn.grow()
    attn.grow(rider)
    ffn.send_late()
    grads = hidden_of(0, 1)
    while attn.level > 0:
        attn.grow()
    grads = hidden_of(1, pages - 1)
    grad_hidden, far = grads
    far_got = swap_bands(far)
    attn.after(ffn)
    attn.grow()
    ffn_in_share, ffn_out_share = ffn.finish(
        lambda total: (total[0, :, :width].T, total[0, :, width:])
    )
    shapes = ((width, 3 * width), (width, width))
    halves = order(lambda mine: widen(band_arr, mine, True, (), shapes), attn.mine)
    grad_hidden = order(edge_add, band_arr, grad_hidden, far, far_got)
    small = attn.last_rider()
    grad_qkv, grad_out = order(
        lambda other, *outs: widen(band_arr, other, False, outs, shapes), attn.flight, *halves
    )

    def outs_of(small):
        small = small.reshape(-1, width)
        tables = small[13 : 13 + HEADS]
        return (
            small[0], small[2], tables[:, 128:160].T, tables[:, :64].T, tables[:, 64:128].T,
            small[5], small[3], small[4], small[9:13].reshape(FF), small[8], small[6], small[7],
        )

    small_outs = order(outs_of, small)
    (
        grad_q_bias, grad_v_bias, grad_rel, grad_x, grad_y, grad_out_b, grad_ln1_gain,
        grad_ln1_bias, grad_ffn_in_b, grad_ffn_out_b, grad_ln2_gain, grad_ln2_bias,
    ) = small_outs
    return (
        output.reshape(hidden.shape),
        grad_hidden,
        grad_qkv,
        grad_q_bias,
        grad_v_bias,
        grad_rel,
        grad_x,
        grad_y,
        grad_out,
        grad_out_b,
        grad_ln1_gain,
        grad_ln1_bias,
        ffn_in_share,
        grad_ffn_in_b,
        ffn_out_share,
        grad_ffn_out_b,
        grad_ln2_gain,
        grad_ln2_bias,
    )


def solution(mesh):
    in_specs = (
        P("page", "band", None),
        P("page", "band", None),
        P("page"),
        P("page", None),
        P("page", None),
        P(),
        P(),
        P(),
        P(),
        P(),
        P(),
        P(),
        P(),
        P(),
        P(),
        P(),
        P(),
        P(),
        P(),
        P(),
        P(),
    )
    out_specs = (
        P("page", "band", None),
        P("page", "band", None),
        P(),
        P(),
        P(),
        P(),
        P(),
        P(),
        P(),
        P(),
        P(),
        P(),
        P(None, ("band", "page")),
        P(),
        P(("band", "page"), None),
        P(),
        P(),
        P(),
    )
    return jax.shard_map(local, mesh=mesh, in_specs=in_specs, out_specs=out_specs, check_vma=False)
```

```python
import functools
import math

import jax
import jax.numpy as jnp
import numpy as np
from jax import lax
from jax.experimental import pallas as pl
from jax.experimental.pallas import tpu as pltpu
from jax.sharding import PartitionSpec as P

F32 = jnp.float32
BF16 = jnp.bfloat16
I32 = jnp.int32

HEADS = 12
WIDTH = 768
FF = 3072
REL_BUCKETS = 32
REL_REACH = 128
XY_BUCKETS = 64
XY_REACH = 256
VIS = 49
HALF = 64
ROWS = 64
KEYS = 256
CLASSES = 128
HIDE = 127
EPSILON = 1e-05
MASKED = -1e30
OUT_B, LN1_G, LN1_B, FFN_OUT_B, LN2_G, LN2_B, Q_B, V_B = range(8)
BRIEF = pl.CostEstimate(flops=1, bytes_accessed=1, transcendentals=0)
NT = (((1,), (1,)), ((), ()))
TN = (((0,), (0,)), ((), ()))
NN = (((1,), (0,)), ((), ()))


def far_away(*arrays):
    return [pltpu.with_memory_space_constraint(a, pltpu.HBM) for a in arrays]


def dot(a, b, dims=NN):
    return lax.dot_general(a, b, dims, preferred_element_type=F32)


def bucket_edges(buckets, reach):
    exact = buckets // 4
    spread = buckets // 2 - exact
    return [
        int(np.ceil(exact * (reach / exact) ** (level / spread) - 1e-09))
        for level in range(1, spread)
    ]


def bucket(offsets, buckets, reach):
    distance = jnp.abs(offsets)
    result = jnp.minimum(distance, float(buckets // 4))
    for edge in bucket_edges(buckets, reach):
        result = result + jnp.where(distance >= float(edge), 1.0, 0.0)
    return result + jnp.where(offsets > 0.0, float(buckets // 2), 0.0)


def iota(shape, axis):
    return lax.broadcasted_iota(I32, shape, axis)


def seventh(index):
    return lax.shift_right_logical(index * 37, 8)


def column_of(row):
    size = row.shape[1]
    shape = (size, size)
    spread = jnp.broadcast_to(row, shape)
    return jnp.sum(jnp.where(iota(shape, 0) == iota(shape, 1), spread, 0.0), axis=1, keepdims=True)


def stage_geometry(first_pos, band, x_own, line_own, kx_ref, kc_ref, blocks):
    extent = ROWS * blocks + 2 * HALF
    seq = x_own.shape[-1]
    half_seq = seq // 2

    def window(row):
        left = jnp.concatenate([jnp.zeros((1, HALF), I32), row[:, : extent - HALF]], axis=1)
        start = half_seq - HALF
        right = jnp.concatenate(
            [row[:, start:], jnp.zeros((1, extent - (seq - start)), I32)], axis=1
        )
        return jnp.where(band == 0, left, right)

    pos = first_pos - HALF + iota((1, extent), 1)
    visual = (pos >= 0) & (pos < VIS)
    seventh_pos = seventh(pos)
    x_row = jnp.where(visual, (pos - 7 * seventh_pos) * 142 + 71, window(x_own))
    c_row = jnp.where(visual, 64 + seventh_pos, window(line_own))
    lane = iota((1, HALF), 1)
    x_vis = (lane - 7 * seventh(lane)) * 142 + 71
    c_vis = 64 + seventh(lane)
    for i in range(blocks):
        cut = slice(ROWS * i, ROWS * i + 3 * HALF)
        kx_ref[i : i + 1, :] = jnp.concatenate([x_vis, x_row[:, cut]], axis=1).astype(F32)
        kc_ref[i : i + 1, :] = jnp.concatenate([c_vis, c_row[:, cut]], axis=1).astype(F32)


def key_positions(first_pos, i, shape):
    lane = iota(shape, 1)
    return jnp.where(
        lane < HALF,
        jnp.where(lane < VIS, lane, -1),
        first_pos + ROWS * i - 2 * HALF + lane,
    )


def allowed(first_pos, i, length):
    shape = (ROWS, KEYS)
    lane = iota(shape, 1)
    key = key_positions(first_pos, i, shape)
    query = first_pos + ROWS * i + iota(shape, 0)
    near = (key >= VIS) & (query >= VIS) & (jnp.abs(query - key) <= HALF)
    return (key >= 0) & (key < VIS + length) & ((lane < HALF) | near)


def rel_buckets(first_pos, i):
    shape = (ROWS, KEYS)
    key = key_positions(first_pos, i, shape)
    query = first_pos + ROWS * i + iota(shape, 0)
    return bucket((key - query).astype(F32), REL_BUCKETS, REL_REACH)


def class_y(index):
    return jnp.where(index < 64, 15 * index, 142 * (index - 64) + 71).astype(F32)


def lookup(table_row, index):
    shape = index.shape
    row = jnp.broadcast_to(table_row, (shape[0], 128))
    cuts = [
        jnp.take_along_axis(row, index[:, s : s + 128], axis=1) for s in range(0, shape[1], 128)
    ]
    return cuts[0] if len(cuts) == 1 else jnp.concatenate(cuts, axis=1)


def head_split(tile):
    low = iota(tile.shape, 1) < 64
    zero = jnp.zeros_like(tile)
    return jnp.concatenate([jnp.where(low, tile, zero), jnp.where(low, zero, tile)], axis=0)


def head_join(stack):
    rows = stack.shape[0] // 2
    low = iota((rows, stack.shape[1]), 1) < 64
    return jnp.where(low, stack[:rows], stack[rows:])


def key_tile(kv_ref, i, column):
    return jnp.concatenate(
        [
            kv_ref[0, 0:HALF, column : column + 128],
            kv_ref[0, pl.ds(pl.multiple_of(HALF + ROWS * i, ROWS), 3 * HALF), column : column + 128],
        ],
        axis=0,
    )


def attention_kernel(
    band_ref, len_ref, hid_ref, got_ref, x_ref, line_ref, w_ref, vec_ref, table_ref,
    ctx_ref, p_ref, q_ref, kv_ref, ext_ref,
    kx_ref, kc_ref, rb_ref, yb_ref, ctx_s, tab_ref,
):
    page = pl.program_id(0)
    band = band_ref[0]
    rows = hid_ref.shape[1]
    blocks = q_ref.shape[1] // ROWS
    first_pos = band * rows

    @pl.when(page == 0)
    def _():
        start = 0
        for slot, count in enumerate((REL_BUCKETS, XY_BUCKETS, XY_BUCKETS)):
            eye = jnp.where(iota((count, 128), 0) == iota((count, 128), 1), 1.0, 0.0).astype(BF16)
            turned = dot(table_ref[start : start + count, :], eye, TN)
            if slot == 1:
                turned = jnp.where(iota((HEADS, 128), 1) == HIDE, MASKED, turned)
            tab_ref[:HEADS, 128 * slot : 128 * slot + 128] = turned
            start += count
        for i in range(blocks):
            index = rel_buckets(first_pos, i).astype(I32)
            for h in range(HEADS):
                part = slice(ROWS * h, ROWS * h + ROWS)
                if i == 0:
                    rb_ref[i, part, :] = lookup(tab_ref[h : h + 1, 0:128], index)
                else:
                    rb_ref[i, part, :128] = lookup(tab_ref[h : h + 1, 0:128], index[:, :128])
                    rb_ref[i, part, 128:] = rb_ref[0, part, 128:]
        square = (CLASSES, CLASSES)
        gap = class_y(iota(square, 1)) - class_y(iota(square, 0))
        index = jnp.minimum(bucket(gap, XY_BUCKETS, XY_REACH), 63.0).astype(I32)
        for h in range(HEADS):
            yb_ref[:, CLASSES * h : CLASSES * h + CLASSES] = lookup(
                tab_ref[h : h + 1, 256:384], index
            ).astype(BF16)

    own = pl.ds(page, 1)
    stage_geometry(first_pos, band, x_ref[own, :], line_ref[own, :], kx_ref, kc_ref, blocks)
    ext_ref[0, :HALF] = jnp.where(band == 0, hid_ref[0, :HALF], got_ref[0, :HALF])
    ext_ref[0, HALF : 2 * HALF] = got_ref[0, HALF:]
    ext_ref[0, 2 * HALF :] = hid_ref[0]
    q_ref[0, 0:rows] = (
        (dot(hid_ref[0], w_ref[:, :WIDTH]) + vec_ref[Q_B : Q_B + 1, :].astype(F32)).astype(BF16).astype(F32)
        * 0.125
    ).astype(BF16)
    q_ref[0, rows:] = jnp.zeros((q_ref.shape[1] - rows, WIDTH), BF16)
    kv_ref[0, : 2 * HALF + rows, :WIDTH] = dot(ext_ref[0], w_ref[:, WIDTH : 2 * WIDTH]).astype(BF16)
    kv_ref[0, : 2 * HALF + rows, WIDTH:] = (
        dot(ext_ref[0], w_ref[:, 2 * WIDTH :]) + vec_ref[V_B : V_B + 1, :].astype(F32)
    ).astype(BF16)
    kv_ref[0, 2 * HALF + rows : 3 * HALF + rows] = kv_ref[0, HALF : 2 * HALF]
    tail = kv_ref.shape[1] - (3 * HALF + rows)
    kv_ref[0, 3 * HALF + rows :] = jnp.zeros((tail, 2 * WIDTH), BF16)

    def block(i, _):
        start = pl.multiple_of(ROWS * i, ROWS)
        kx = kx_ref[pl.ds(i, 1), :]
        kc = kc_ref[pl.ds(i, 1), :]
        gap = kx - column_of(kx[:, 2 * HALF : 3 * HALF])
        index = jnp.where(
            allowed(first_pos, i, len_ref[page]), bucket(gap, XY_BUCKETS, XY_REACH), float(HIDE)
        ).astype(I32)
        pick_q = jnp.where(
            iota((ROWS, CLASSES), 1).astype(F32) == column_of(kc[:, 2 * HALF : 3 * HALF]), 1.0, 0.0
        ).astype(BF16)
        pick_k = jnp.where(
            iota((KEYS, CLASSES), 1).astype(F32) == column_of(kc), 1.0, 0.0
        ).astype(BF16)
        pairs = range(HEADS // 2)
        scores = []
        for j in pairs:
            column = 128 * j
            queries = head_split(q_ref[0, pl.ds(start, ROWS), column : column + 128])
            picked = dot(pick_q, yb_ref[:, 2 * column : 2 * column + 256]).astype(BF16)
            picked = jnp.concatenate([picked[:, :128], picked[:, 128:]], axis=0)
            scores.append(
                dot(
                    jnp.concatenate([queries, picked], axis=1),
                    jnp.concatenate([key_tile(kv_ref, i, column), pick_k], axis=1),
                    NT,
                )
            )
        weights = []
        for j in pairs:
            x_bias = jnp.concatenate(
                [lookup(tab_ref[2 * j + e : 2 * j + e + 1, 128:256], index) for e in (0, 1)], axis=0
            )
            biased = scores[j] + rb_ref[i, 128 * j : 128 * j + 128, :] + x_bias
            peak = jnp.max(biased, axis=1, keepdims=True)
            raised = jnp.exp(biased - peak)
            weights.append(raised.astype(BF16))
        ones = jnp.ones((KEYS, 128), BF16)
        joint = [
            dot(weights[j], jnp.concatenate([key_tile(kv_ref, i, WIDTH + 128 * j), ones], axis=1))
            for j in pairs
        ]
        contexts = []
        for j in pairs:
            share = 1.0 / joint[j][:, 128:]
            contexts.append(joint[j][:, :128] * share)
            share = jnp.concatenate([share, share], axis=1)
            weights[j] = (weights[j].astype(F32) * share).astype(BF16)
        for j in pairs:
            p_ref[0, i, 128 * j : 128 * j + 128, :] = weights[j]
        ctx_s[pl.ds(start, ROWS), :] = jnp.concatenate(
            [head_join(c).astype(BF16) for c in contexts], axis=1
        )
        return 0

    lax.fori_loop(0, blocks, block, 0, unroll=blocks)
    ctx_ref[0] = ctx_s[:rows]


def page_block(*shape):
    return pl.BlockSpec((1,) + shape, lambda p, *_: (p,) + (0,) * len(shape))


def whole(*shape):
    return pl.BlockSpec(shape, lambda *_: (0,) * len(shape))


def attention_forward(
    band, lengths, hidden, got, x_coord, line_ids, qkv_w, vectors, tables
):
    pages, rows, width = hidden.shape
    blocks = -(-rows // ROWS)
    padded = blocks * ROWS
    ext = padded + 3 * HALF
    shape = jax.ShapeDtypeStruct
    return pl.pallas_call(
        attention_kernel,
        out_shape=(
            pltpu.HBM((pages, rows, width), BF16),
            pltpu.HBM((pages, blocks, HEADS * ROWS, KEYS), BF16),
            pltpu.HBM((pages, padded, width), BF16),
            pltpu.HBM((pages, ext, 2 * width), BF16),
            pltpu.HBM((pages, rows + 2 * HALF, width), BF16),
        ),
        grid_spec=pltpu.PrefetchScalarGridSpec(
            num_scalar_prefetch=2,
            grid=(pages,),
            in_specs=[
                page_block(rows, width),
                page_block(2 * HALF, width),
                whole(*x_coord.shape),
                whole(*line_ids.shape),
                whole(width, 3 * width),
                whole(*vectors.shape),
                whole(*tables.shape),
            ],
            out_specs=[
                page_block(rows, width),
                page_block(blocks, HEADS * ROWS, KEYS),
                page_block(padded, width),
                page_block(ext, 2 * width),
                page_block(rows + 2 * HALF, width),
            ],
            scratch_shapes=[
                pltpu.VMEM((8, KEYS), F32),
                pltpu.VMEM((8, KEYS), F32),
                pltpu.VMEM((blocks, HEADS * ROWS, KEYS), F32),
                pltpu.VMEM((CLASSES, HEADS * CLASSES), BF16),
                pltpu.VMEM((padded, width), BF16),
                pltpu.VMEM((16, 384), F32),
            ],
        ),
        compiler_params=pltpu.CompilerParams(vmem_limit_bytes=44 << 20),
        cost_estimate=pl.CostEstimate(
            flops=2 * pages * (rows + 2 * HALF) * width * 3 * width
            + 8 * pages * padded * HEADS * KEYS * 128,
            bytes_accessed=30 << 20,
            transcendentals=pages * padded * HEADS * KEYS,
        ),
        name="attention_forward",
    )(
        band, lengths, *far_away(hidden), got, x_coord, line_ids, *far_away(qkv_w), vectors, tables,
    )


def layer_norm(total):
    centred = total - jnp.mean(total, axis=1, keepdims=True)
    inverse = lax.rsqrt(jnp.mean(centred * centred, axis=1, keepdims=True) + EPSILON)
    return centred * inverse, inverse


def norm_back(grad, normed, inverse, gain):
    scaled = grad * gain
    return inverse * (
        scaled
        - jnp.mean(scaled, axis=1, keepdims=True)
        - normed * jnp.mean(scaled * normed, axis=1, keepdims=True)
    )


def gelu_parts(inner):
    size = jnp.abs(inner)
    falling = jnp.exp(inner * inner * -0.5)
    t = 1.0 / (1.0 + (0.3275911 * math.sqrt(0.5)) * size)
    poly = 1.061405429 * t - 1.453152027
    poly = poly * t + 1.421413741
    poly = poly * t - 0.284496736
    poly = poly * t + 0.254829592
    tail = (0.5 * poly) * (t * falling)
    share = jnp.where(inner >= 0.0, 1.0 - tail, tail)
    return inner * share, share + inner * falling * (2.0 * math.pi) ** (-0.5)


def column_sum(values):
    return jnp.sum(values, axis=0, keepdims=True)


def accumulate(ref, row, value):
    first = pl.program_id(0) == 0

    @pl.when(first)
    def _():
        ref[row : row + 1, :] = value

    @pl.when(jnp.logical_not(first))
    def _():
        ref[row : row + 1, :] = ref[row : row + 1, :] + value


def fixed(*shape):
    return pl.BlockSpec(shape, lambda *_: (0,) * len(shape), pipeline_mode=pl.Buffered(1))


def resident():
    return pl.BlockSpec(memory_space=pltpu.VMEM)


FORWARD_CUT = 768
CUT = 768
BLOCKS = 6


def ffn_forward_kernel(
    ctx_ref, hid_ref, cot_ref, vec_ref, bin_ref, wo_ref, w1_ref, w2_ref,
    out_ref, first_ref, norm_ref, inv_ref, act_ref, slope_ref, dh_ref, ds_ref, sums_ref,
    second_s,
):
    step = pl.program_id(0)

    def vector(row):
        return vec_ref[row : row + 1, :].astype(F32)

    @pl.when(step == 0)
    def _():
        attended = dot(ctx_ref[...], wo_ref[...]) + vector(OUT_B)
        normed, inverse = layer_norm(hid_ref[...].astype(F32) + attended)
        first = (normed * vector(LN1_G) + vector(LN1_B)).astype(BF16)
        first_ref[...] = first
        norm_ref[...] = normed
        inv_ref[...] = jnp.broadcast_to(inverse, inv_ref.shape)
        second_s[...] = first.astype(F32) + vector(FFN_OUT_B)

    size = first_ref.shape[0] // BLOCKS
    parts = [slice(size * r, size * r + size) for r in range(BLOCKS)]
    w1, w2 = w1_ref[...], w2_ref[...]
    offset = bin_ref[...].astype(F32)

    def inner_of(r):
        return dot(first_ref[parts[r], :], w1) + offset

    def feed(r, act):
        second_s[parts[r], :] = second_s[parts[r], :] + dot(act, w2)

    ahead, behind = inner_of(0), None
    for r in range(BLOCKS):
        inner = ahead
        if r + 1 < BLOCKS:
            ahead = inner_of(r + 1)
        act, slope = gelu_parts(inner)
        act = act.astype(BF16)
        act_ref[parts[r], :] = act
        slope_ref[parts[r], :] = slope.astype(BF16)
        if r > 0:
            feed(r - 1, behind)
        behind = act
    feed(BLOCKS - 1, behind)

    @pl.when(step == pl.num_programs(0) - 1)
    def _():
        normed2, inverse2 = layer_norm(second_s[...])
        out_ref[...] = (normed2 * vector(LN2_G) + vector(LN2_B)).astype(BF16)
        grad = cot_ref[...].astype(F32)
        back = norm_back(grad, normed2, inverse2, vector(LN2_G))
        low = back.astype(BF16)
        dh_ref[...] = back
        ds_ref[...] = low
        sums_ref[0:1, :] = column_sum(grad * normed2)
        sums_ref[1:2, :] = column_sum(grad)
        sums_ref[2:3, :] = column_sum(low.astype(F32))


def ffn_forward(context, hidden, cotangent, vectors, ffn_in_b, out_w, ffn_in_w, ffn_out_w):
    tokens, width = context.shape
    shape = jax.ShapeDtypeStruct
    rows = fixed(tokens, width)
    step = FORWARD_CUT
    wide = pl.BlockSpec((tokens, step), lambda i: (0, i))
    return pl.pallas_call(
        ffn_forward_kernel,
        out_shape=(
            pltpu.HBM((tokens, width), BF16),
            shape((tokens, width), BF16),
            shape((tokens, width), F32),
            shape((tokens, 128), F32),
            pltpu.HBM((tokens, FF), BF16),
            pltpu.HBM((tokens, FF), BF16),
            shape((tokens, width), F32),
            shape((tokens, width), BF16),
            shape((8, width), F32),
        ),
        grid=(FF // step,),
        in_specs=[
            rows, rows, rows,
            whole(*vectors.shape),
            pl.BlockSpec((1, step), lambda i: (0, i)),
            fixed(width, width),
            pl.BlockSpec((width, step), lambda i: (0, i)),
            pl.BlockSpec((step, width), lambda i: (i, 0)),
        ],
        out_specs=[
            rows, resident(), resident(), resident(),
            wide, wide, resident(), resident(),
            whole(8, width),
        ],
        scratch_shapes=[pltpu.VMEM((tokens, width), F32)],
        compiler_params=pltpu.CompilerParams(vmem_limit_bytes=36 << 20),
        cost_estimate=pl.CostEstimate(
            flops=2 * tokens * width * (2 * FF + width),
            bytes_accessed=40 << 20,
            transcendentals=tokens * FF,
        ),
        name="ffn_forward",
    )(
        *far_away(context, hidden, cotangent), vectors, ffn_in_b,
        *far_away(out_w, ffn_in_w, ffn_out_w),
    )


def ffn_parts(owner, ds_ref, first_ref, act_ref, slope_ref, w1_ref, w2_ref, parts_ref, bsum_ref):
    step = pl.program_id(0)
    chunks, size, _ = parts_ref.shape
    orders = split_orders(chunks, True)
    low = ds_ref[...]
    grad = dot(low, w2_ref[...], NT)
    out_part = dot(act_ref[...], low, TN).astype(BF16)
    inner = (grad * slope_ref[...].astype(F32)).astype(BF16)
    added = dot(inner, w1_ref[...], NT)
    bsum_ref[...] = column_sum(inner.astype(F32))
    in_part = dot(inner, first_ref[...], TN).astype(BF16)
    for c in range(CUT // size):
        chunk = step * (CUT // size) + c
        spot = jnp.where(owner == 0, place(chunk, orders[0]), place(chunk, orders[1]))
        part = slice(size * c, size * c + size)
        parts_ref[spot] = jnp.concatenate([in_part[part], out_part[part]], axis=1)
    return added


def ffn_back_far_kernel(
    band_ref, ds_ref, first_ref, act_ref, slope_ref, w1_ref, w2_ref, dh_ref,
    parts_ref, bsum_ref, total_ref,
):
    added = ffn_parts(
        1 - band_ref[0], ds_ref, first_ref, act_ref, slope_ref, w1_ref, w2_ref, parts_ref, bsum_ref
    )

    @pl.when(pl.program_id(0) == 0)
    def _():
        total_ref[...] = dh_ref[...] + added

    @pl.when(pl.program_id(0) > 0)
    def _():
        total_ref[...] = total_ref[...] + added


def ffn_back_own_kernel(
    band_ref, ds_ref, first_ref, act_ref, slope_ref, w1_ref, w2_ref, part_ref, norm_ref, inv_ref,
    vec_ref, wo_ref,
    parts_ref, bsum_ref, dh1_ref, da_ref, dc_ref, sums_ref,
    total_s,
):
    added = ffn_parts(
        band_ref[0], ds_ref, first_ref, act_ref, slope_ref, w1_ref, w2_ref, parts_ref, bsum_ref
    )

    @pl.when(pl.program_id(0) == 0)
    def _():
        total_s[...] = part_ref[...] + added

    @pl.when(pl.program_id(0) > 0)
    def _():
        total_s[...] = total_s[...] + added

    @pl.when(pl.program_id(0) == pl.num_programs(0) - 1)
    def _():
        total = total_s[...]
        normed = norm_ref[...]
        gain = vec_ref[LN1_G : LN1_G + 1, :].astype(F32)
        back = norm_back(total, normed, inv_ref[:, 0:1], gain)
        low = back.astype(BF16)
        dh1_ref[...] = back
        da_ref[...] = low
        dc_ref[...] = dot(low, wo_ref[...], NT).astype(BF16)
        sums_ref[0:1, :] = column_sum(total * normed)
        sums_ref[1:2, :] = column_sum(total)
        sums_ref[2:3, :] = column_sum(low.astype(F32))


def ffn_back_call(own, band, second_low, first, act, slope, ffn_in_w, ffn_out_w, extra, chunks):
    tokens, width = second_low.shape
    half = FF // 2
    steps = half // CUT
    shape = jax.ShapeDtypeStruct
    rows = fixed(tokens, width)

    def at(i, b):
        return (b[0] if own else 1 - b[0]) * steps + i

    in_specs = [
        resident(), resident(),
        pl.BlockSpec((tokens, CUT), lambda i, b: (0, at(i, b))),
        pl.BlockSpec((tokens, CUT), lambda i, b: (0, at(i, b))),
        pl.BlockSpec((width, CUT), lambda i, b: (0, at(i, b))),
        pl.BlockSpec((CUT, width), lambda i, b: (at(i, b), 0)),
    ] + ([resident()] * 3 + [fixed(*e.shape) for e in extra[3:]] if own else [resident()])
    out_shape = [
        pltpu.HBM((chunks // 2, FF // chunks, 2 * width), BF16),
        shape((1, half), F32),
    ]
    out_specs = [
        fixed(chunks // 2, FF // chunks, 2 * width),
        pl.BlockSpec((1, CUT), lambda i, b: (0, i)),
    ]
    if own:
        out_shape += [
            pltpu.HBM((tokens, width), F32), pltpu.HBM((tokens, width), BF16),
            pltpu.HBM((tokens, width), BF16), shape((8, width), F32),
        ]
        out_specs += [rows, rows, rows, whole(8, width)]
    else:
        out_shape += [shape((tokens, width), F32)]
        out_specs += [resident()]
    return pl.pallas_call(
        ffn_back_own_kernel if own else ffn_back_far_kernel,
        out_shape=out_shape,
        grid_spec=pltpu.PrefetchScalarGridSpec(
            num_scalar_prefetch=1,
            grid=(steps,),
            in_specs=in_specs,
            out_specs=out_specs,
            scratch_shapes=[pltpu.VMEM((tokens, width), F32)] if own else [],
        ),
        compiler_params=pltpu.CompilerParams(vmem_limit_bytes=34 << 20),
        cost_estimate=pl.CostEstimate(
            flops=8 * tokens * width * half, bytes_accessed=30 << 20, transcendentals=0
        ),
        name="ffn_back_own" if own else "ffn_back_far",
    )(
        band, second_low, first, *far_away(act, slope, ffn_in_w, ffn_out_w),
        *(extra[:-1] + tuple(far_away(extra[-1])) if own else extra),
    )


def attention_back_kernel(
    p_ref, q_ref, kv_ref, dc_ref,
    dm_ref, ds_ref,
    dkv_ref, dc_s, dq_s,
):
    rows = dc_ref.shape[1]
    blocks = q_ref.shape[1] // ROWS
    dkv_ref[...] = jnp.zeros_like(dkv_ref)
    dc_s[:rows] = dc_ref[0]
    dc_s[rows:] = jnp.zeros((dc_s.shape[0] - rows, WIDTH), BF16)
    def block(i, _):
        start = pl.multiple_of(ROWS * i, ROWS)
        window = pl.ds(pl.multiple_of(HALF + ROWS * i, ROWS), 3 * HALF)
        pairs = range(HEADS // 2)
        grads = []
        for j in pairs:
            column = 128 * j
            grads.append(head_split(dc_s[pl.ds(start, ROWS), column : column + 128]))
        dprobs = [dot(grads[j], key_tile(kv_ref, i, WIDTH + 128 * j), NT) for j in pairs]
        for j in pairs:
            dv = dot(p_ref[0, i, 128 * j : 128 * j + 128, :], grads[j], TN)
            column = WIDTH + 128 * j
            cut = slice(column, column + 128)
            dkv_ref[0:HALF, cut] = dkv_ref[0:HALF, cut] + dv[:HALF]
            dkv_ref[window, cut] = dkv_ref[window, cut] + dv[HALF:]
        lows = []
        for j in pairs:
            probs = p_ref[0, i, 128 * j : 128 * j + 128, :].astype(F32)
            grad = probs * (
                dprobs[j] - jnp.sum(probs * dprobs[j], axis=1, keepdims=True)
            )
            lows.append(grad.astype(BF16))
        dq = [head_join(dot(lows[j], key_tile(kv_ref, i, 128 * j))) for j in pairs]
        dq_s[pl.ds(start, ROWS), :] = (jnp.concatenate(dq, axis=1) * 0.125).astype(BF16)
        for j in pairs:
            cut = slice(128 * j, 128 * j + 128)
            dk = dot(lows[j], head_split(q_ref[0, pl.ds(start, ROWS), cut]), TN)
            dkv_ref[0:HALF, cut] = dkv_ref[0:HALF, cut] + dk[:HALF]
            dkv_ref[window, cut] = dkv_ref[window, cut] + dk[HALF:]

        for j in pairs:
            ds_ref[0, i, 128 * j : 128 * j + 128, :] = lows[j]
        return 0

    lax.fori_loop(0, blocks, block, 0, unroll=blocks)
    dm_ref[0, : 2 * HALF, :WIDTH] = jnp.zeros((2 * HALF, WIDTH), BF16)
    dm_ref[0, 2 * HALF :, :WIDTH] = dq_s[:rows]
    dm_ref[0, :HALF, WIDTH:] = dkv_ref[:HALF].astype(BF16)
    dm_ref[0, HALF : 2 * HALF, WIDTH:] = (
        dkv_ref[HALF : 2 * HALF] + dkv_ref[2 * HALF + rows : 3 * HALF + rows]
    ).astype(BF16)
    dm_ref[0, 2 * HALF :, WIDTH:] = dkv_ref[2 * HALF : 2 * HALF + rows].astype(BF16)


def attention_backward(probs, queries, pairs, grad_context):
    pages, rows, width = grad_context.shape
    padded = queries.shape[1]
    blocks = padded // ROWS
    ext = pairs.shape[1]
    shape = jax.ShapeDtypeStruct
    return pl.pallas_call(
        attention_back_kernel,
        out_shape=(
            pltpu.HBM((pages, rows + 2 * HALF, 3 * width), BF16),
            pltpu.HBM(probs.shape, BF16),
        ),
        grid=(pages,),
        in_specs=[
            page_block(blocks, HEADS * ROWS, KEYS),
            page_block(padded, width),
            page_block(ext, 2 * width),
            page_block(rows, width),
        ],
        out_specs=[page_block(rows + 2 * HALF, 3 * width), page_block(blocks, HEADS * ROWS, KEYS)],
        scratch_shapes=[
            pltpu.VMEM((ext, 2 * width), F32),
            pltpu.VMEM((padded, width), BF16),
            pltpu.VMEM((padded, width), BF16),
        ],
        compiler_params=pltpu.CompilerParams(vmem_limit_bytes=56 << 20),
        cost_estimate=pl.CostEstimate(
            flops=10 * pages * padded * HEADS * KEYS * 128, bytes_accessed=30 << 20, transcendentals=0
        ),
        name="attention_backward",
    )(*far_away(probs, queries, pairs, grad_context))


def table_kernel(
    blocks, start, band_ref, ds_ref, x_ref, line_ref, tab_ref, kx_ref, kc_ref, left_ref, right_ref,
    index_ref,
):
    step = pl.program_id(0)
    band = band_ref[0]
    page = (start + step) // blocks
    i = (start + step) % blocks
    first_pos = band * (x_ref.shape[-1] // 2)

    @pl.when((step == 0) | (i == 0))
    def _():
        own = pl.ds(page, 1)
        stage_geometry(first_pos, band, x_ref[own, :], line_ref[own, :], kx_ref, kc_ref, blocks)

    slots = iota((REL_BUCKETS + 2 * XY_BUCKETS, KEYS), 0).astype(F32).astype(BF16)
    one = jnp.ones((), BF16)
    zero = jnp.zeros((), BF16)

    left_ref[...] = ds_ref[0, :, :128].astype(F32)
    right_ref[...] = ds_ref[0, :, 128:].astype(F32)
    kx = kx_ref[pl.ds(i, 1), :]
    ky = class_y(kc_ref[pl.ds(i, 1), :].astype(I32))
    index_ref[0:ROWS] = bucket(kx - column_of(kx[:, 2 * HALF : 3 * HALF]), XY_BUCKETS, XY_REACH)
    index_ref[ROWS : 2 * ROWS] = 64.0 + bucket(
        ky - column_of(ky[:, 2 * HALF : 3 * HALF]), XY_BUCKETS, XY_REACH
    )
    index_ref[2 * ROWS : 3 * ROWS] = 128.0 + rel_buckets(first_pos, i)

    def table_row(q, acc):
        own = jnp.concatenate(
            [
                jnp.broadcast_to(index_ref[pl.ds(q, 1), :], (XY_BUCKETS, KEYS)),
                jnp.broadcast_to(index_ref[pl.ds(ROWS + q, 1), :], (XY_BUCKETS, KEYS)),
                jnp.broadcast_to(index_ref[pl.ds(2 * ROWS + q, 1), :], (REL_BUCKETS, KEYS)),
            ],
            axis=0,
        ).astype(BF16)
        heads = jnp.concatenate(
            [
                left_ref[pl.ds(q, HEADS, stride=ROWS), :],
                right_ref[pl.ds(q, HEADS, stride=ROWS), :],
            ],
            axis=1,
        ).astype(BF16)
        return acc + dot(heads, jnp.where(slots == own, one, zero), NT)

    table_sum = lax.fori_loop(
        0, ROWS, table_row, jnp.zeros(tab_ref.shape, F32), unroll=ROWS
    )

    @pl.when(step == 0)
    def _():
        tab_ref[...] = table_sum

    @pl.when(step > 0)
    def _():
        tab_ref[...] = tab_ref[...] + table_sum


def table_sums(band, start, count, grad_scores, x_coord, line_ids):
    pages, blocks, height, keys = grad_scores.shape
    buckets = REL_BUCKETS + 2 * XY_BUCKETS
    return pl.pallas_call(
        functools.partial(table_kernel, blocks, start),
        out_shape=jax.ShapeDtypeStruct((HEADS, buckets), F32),
        grid_spec=pltpu.PrefetchScalarGridSpec(
            num_scalar_prefetch=1,
            grid=(count,),
            in_specs=[
                pl.BlockSpec((1, height, keys), lambda i, *_: (start + i, 0, 0)),
                whole(*x_coord.shape),
                whole(*line_ids.shape),
            ],
            out_specs=whole(HEADS, buckets),
            scratch_shapes=[
                pltpu.VMEM((8, KEYS), F32),
                pltpu.VMEM((8, KEYS), F32),
                pltpu.VMEM((height, 128), F32),
                pltpu.VMEM((height, 128), F32),
                pltpu.VMEM((3 * ROWS, KEYS), F32),
            ],
        ),
        compiler_params=pltpu.CompilerParams(vmem_limit_bytes=40 << 20),
        cost_estimate=BRIEF,
        name="table_sums",
    )(band, *far_away(grad_scores.reshape(pages * blocks, height, keys)), x_coord, line_ids)


def hidden_back_kernel(dm_ref, dh_ref, w_ref, *refs):
    own_ref, far_ref = refs[-2:]
    own_ref[0] = dh_ref[0] + dot(dm_ref[0, 2 * HALF :], w_ref[...], NT)
    far_ref[0] = dot(dm_ref[0, : 2 * HALF, WIDTH:], w_ref[:, WIDTH:], NT).astype(BF16)


def hidden_backward(page, count, outs, grad_mixed, grad_total, qkv_w):
    pages, rows, width = grad_total.shape

    def one(*shape):
        return pl.BlockSpec((1,) + shape, lambda i: (page + i, 0, 0))

    return pl.pallas_call(
        hidden_back_kernel,
        out_shape=(
            pltpu.HBM((pages, rows, width), F32),
            pltpu.HBM((pages, 2 * HALF, width), BF16),
        ),
        grid=(count,),
        in_specs=[
            one(rows + 2 * HALF, 3 * width),
            one(rows, width),
            whole(width, 3 * width),
        ]
        + [pl.BlockSpec(memory_space=pl.ANY)] * len(outs),
        out_specs=[one(rows, width), one(2 * HALF, width)],
        input_output_aliases={3 + i: i for i in range(len(outs))},
        compiler_params=pltpu.CompilerParams(vmem_limit_bytes=60 << 20),
        cost_estimate=BRIEF,
        name="hidden_backward",
    )(*far_away(grad_mixed, grad_total, qkv_w), *outs)


def edge_kernel(band_ref, grad_ref, far_ref, got_ref, out_ref):
    band = band_ref[0]
    side = pl.program_id(0)
    edge = HALF // 2
    for s in range(4):

        @pl.when(side == s)
        def _():
            part = slice(edge * (s % 2), edge * (s % 2) + edge)
            rim = slice(HALF + part.start, HALF + part.stop)
            if s < 2:
                own = far_ref[:, part].astype(F32) + got_ref[:, part].astype(F32)
                added = jnp.where(band == 0, own, got_ref[:, rim].astype(F32))
            else:
                added = jnp.where(band == 0, got_ref[:, rim].astype(F32), 0.0)
            out_ref[...] = grad_ref[...] + added


def edge_add(band, grad, far, got):
    pages, rows, width = grad.shape
    half = HALF // 2
    last = rows // half - 2

    def edge(s, *_):
        return (0, jnp.where(s < 2, s, last + s - 2), 0)

    return pl.pallas_call(
        edge_kernel,
        out_shape=jax.ShapeDtypeStruct(grad.shape, F32),
        grid_spec=pltpu.PrefetchScalarGridSpec(
            num_scalar_prefetch=1,
            grid=(4,),
            in_specs=[
                pl.BlockSpec((pages, half, width), edge),
                whole(*far.shape),
                whole(*got.shape),
            ],
            out_specs=pl.BlockSpec((pages, half, width), edge),
        ),
        input_output_aliases={1: 0},
        cost_estimate=BRIEF,
        name="edge_add",
    )(band, grad, far, got)


def split_orders(count, mixed=False):
    total = count.bit_length() - 1
    side = total // 3
    x, y, z = (range(side), range(side, 2 * side), range(2 * side, total))
    if mixed:
        return [*x, *z[:-1], *y, z[-1]], [*y, *z[:-1], *x, z[-1]]
    return [*x, *y, *z], [*y, *x, *z]


def place(chunk, order):
    spot = 0
    for level, bit in enumerate(order):
        spot = spot + (((chunk >> bit) & 1) << (len(order) - 1 - level))
    return spot


def product_halves(band, tokens_ext, grad_mixed, context, grad_attn):
    tokens, height = tokens_ext.shape
    width = grad_mixed.shape[1]
    step = height // 2

    def kernel(band_ref, l_ref, r_ref, l2_ref, r2_ref, send_ref, keep_ref, sums_ref):
        def write(ref):
            ref[:, :width] = dot(l_ref[...], r_ref[...], TN).astype(BF16)
            ref[:, width:] = dot(l2_ref[...], r2_ref[...], TN).astype(BF16)

        @pl.when(pl.program_id(0) == 0)
        def _():
            write(send_ref)
            sums_ref[...] = dot(jnp.ones((tokens, 8), BF16), r_ref[...], TN)

        pl.when(pl.program_id(0) == 1)(lambda: write(keep_ref))

    def at(i, b):
        return (0, jnp.where(i == 0, 1 - b[0], b[0]))

    out = pltpu.HBM((step, width + height), BF16)
    return pl.pallas_call(
        kernel,
        out_shape=(out, out, jax.ShapeDtypeStruct((8, width), F32)),
        grid_spec=pltpu.PrefetchScalarGridSpec(
            num_scalar_prefetch=1,
            grid=(2,),
            in_specs=[
                pl.BlockSpec((tokens, step), at),
                fixed(*grad_mixed.shape),
                pl.BlockSpec((context.shape[0], step), at),
                fixed(*grad_attn.shape),
            ],
            out_specs=[
                fixed(step, width + height), fixed(step, width + height), fixed(8, width)
            ],
        ),
        compiler_params=pltpu.CompilerParams(vmem_limit_bytes=60 << 20),
        cost_estimate=pl.CostEstimate(
            flops=2 * tokens * height * (width + height), bytes_accessed=16 << 20, transcendentals=0
        ),
        name="product_halves",
    )(band, *far_away(tokens_ext, grad_mixed, context, grad_attn))


def swap_bands(block):
    return lax.ppermute(block, "band", [(0, 1), (1, 0)])


def swap_pages(block, level, orders):
    count = lax.axis_size("page")
    route = [
        (b * count + p, b * count + (p ^ (1 << orders[b][level])))
        for b in range(2)
        for p in range(count)
    ]
    return lax.ppermute(block, ("band", "page"), route)


def sides(orders):
    band, page = lax.axis_index("band"), lax.axis_index("page")
    return [
        jnp.where(band == 0, (page >> first) & 1, (page >> second) & 1)
        for first, second in zip(*orders)
    ]


def widen(band, block, own, outs, shapes):
    half, width = shapes[0][0] // 2, block.shape[1]
    steps = 4
    step = half // steps
    edges = [sum(shape[1] for shape in shapes[:i]) for i in range(len(shapes) + 1)]

    def kernel(band_ref, block_ref, *refs):
        for out, start, stop in zip(refs[-len(shapes) :], edges, edges[1:]):
            out[...] = block_ref[:, start:stop].astype(F32)

    def at(i, b):
        return ((b[0] if own else 1 - b[0]) * steps + i, 0)

    return pl.pallas_call(
        kernel,
        out_shape=[pltpu.HBM(shape, F32) for shape in shapes],
        grid_spec=pltpu.PrefetchScalarGridSpec(
            num_scalar_prefetch=1,
            grid=(steps,),
            in_specs=[pl.BlockSpec((step, width), lambda i, *_: (i, 0))]
            + [pl.BlockSpec(memory_space=pl.ANY)] * len(outs),
            out_specs=[pl.BlockSpec((step, shape[1]), at) for shape in shapes],
        ),
        input_output_aliases={2 + i: i for i in range(len(outs))},
        compiler_params=pltpu.CompilerParams(vmem_limit_bytes=40 << 20),
        cost_estimate=BRIEF,
        name="widen",
    )(band, block, *outs)


class Order:
    def __init__(self):
        self.mark = None

    def __call__(self, part, *args):
        if self.mark is not None:
            leaves, tree = jax.tree.flatten(args)
            leaves = lax.optimization_barrier((*leaves, self.mark))[:-1]
            args = jax.tree.unflatten(tree, leaves)
        out = part(*args)
        self.mark = jax.tree.leaves(out)[0]
        return out

    def late(self, block):
        return lax.optimization_barrier((block, self.mark))[0]


def halving_plan(size, orders):
    starts, spots = [], [[0, 0]]
    for side in sides(orders):
        size = size // 2
        starts.append([at + (1 - side) * size for at in spots[-1]])
        spots.append([at + side * size for at in spots[-1]] + [0])
    return starts, spots


class Halving:
    def __init__(self, order, send, keep, orders, plan):
        self.order = order
        self.orders = orders
        self.starts, self.spots, self.sides = plan
        self.level = 0
        self.held = [keep]
        self.size = keep.shape[0]
        self.flight = swap_bands(send)

    def land(self):
        self.held.append(self.flight)
        self.flight = None

    def total(self, size):
        def add(spots, *held):
            parts = [
                lax.dynamic_slice_in_dim(block, at, size, 0, allow_negative_indices=False)
                for block, at in zip(held, spots)
            ]
            return sum([part.astype(F32) for part in parts[1:]], parts[0].astype(F32))

        return add

    def step(self):
        self.gather()
        self.send(self.sent)

    def gather(self):
        self.land()
        self.size //= 2
        add = self.total(self.size)
        self.sent = self.order(
            lambda *a: add(*a).astype(BF16), self.starts[self.level], *self.held
        )

    def send(self, sent):
        self.flight = swap_pages(sent, self.level, self.orders)
        self.level += 1

    def send_late(self):
        self.send(self.order.late(self.sent))

    def finish(self, wrap):
        self.land()
        add = self.total(self.size)
        return self.order(lambda *a: wrap(add(*a)), self.spots[self.level], *self.held)

    def meet(self):
        self.land()
        add = self.total(self.size)
        mine = self.order(lambda *a: add(*a).astype(BF16), self.spots[self.level], *self.held)
        self.flight = swap_pages(mine, self.level, self.orders)
        self.mine = mine

    def met(self):
        self.mine = self.order(
            lambda a, b: (a.astype(F32) + b.astype(F32)).astype(BF16), self.mine, self.flight
        )
        self.rider = None
        self.level -= 1
        self.flight = swap_pages(self.mine, self.level, self.orders)

    def after(self, other):
        self.mine, other.flight = lax.optimization_barrier((self.mine, other.flight))

    def grow(self, rider=None):
        size = self.mine.shape[0]
        if self.level == 0:
            self.mine, self.rider = self.order(
                lambda mine, got, rider, side: (
                    join(mine, got[:size], side), rider + rider_of(got[size:])
                ),
                self.mine, self.flight, self.rider, self.sides[0],
            )
            self.level -= 1
            self.flight = swap_bands(self.mine)
            self.rider_flight = swap_bands(self.rider)
            return
        if rider is None and self.rider is None:
            self.mine = self.order(join, self.mine, self.flight, self.sides[self.level])
            sent = self.mine
        else:
            first = rider is not None

            def both(mine, got, rider, side):
                if not first:
                    rider = rider + rider_of(got[size:])
                return with_rider(join(mine, got[:size], side), rider)

            sent, self.mine, self.rider = self.order(
                both, self.mine, self.flight, rider if first else self.rider,
                self.sides[self.level],
            )
        self.level -= 1
        self.flight = swap_pages(sent, self.level, self.orders)

    def last_rider(self):
        return self.order(lambda a, b: a + b, self.rider, self.rider_flight)


def with_rider(block, rider):
    high = lax.reduce_precision(rider, 8, 7)
    low = (rider - high).astype(BF16)
    return jnp.concatenate([block, high.astype(BF16), low], axis=0), block, rider


def rider_of(rows):
    half = rows.shape[0] // 2
    return rows[:half].astype(F32) + rows[half:].astype(F32)


def join(mine, other, side):
    return jnp.where(
        side == 0,
        jnp.concatenate([mine, other], axis=0),
        jnp.concatenate([other, mine], axis=0),
    )


def flat(block):
    return block.reshape(-1, block.shape[-1])


def local(
    hidden, cotangent, page_lengths, x_coord, line_ids, qkv_w, q_bias, v_bias,
    rel_table, x_table, y_table, out_w, out_b, ln1_gain, ln1_bias,
    ffn_in_w, ffn_in_b, ffn_out_w, ffn_out_b, ln2_gain, ln2_bias,
):
    pages, rows, width = hidden.shape
    band = lax.axis_index("band")
    chunks = 2 * lax.axis_size("page")
    band_arr = band.reshape(1).astype(I32)
    own_edge = jnp.where(band == 0, hidden[:, rows - HALF :], hidden[:, :HALF])
    got = swap_bands(jnp.concatenate([hidden[:, :HALF], own_edge], axis=1))
    half = chunks // 2
    ffn_orders, attn_orders = split_orders(half, True), split_orders(half)
    plans = [
        (*halving_plan(size, orders), sides(orders))
        for size, orders in ((half, ffn_orders), (width // 2, attn_orders))
    ]
    got, plans = lax.optimization_barrier((got, plans))
    ffn_plan, attn_plan = plans
    vectors = jnp.concatenate(
        [out_b, ln1_gain, ln1_bias, ffn_out_b, ln2_gain, ln2_bias, q_bias, v_bias]
    ).reshape(8, width)
    tables = jnp.concatenate([rel_table, x_table, y_table], axis=0)
    context, probs, queries, pairs, extended = attention_forward(
        band_arr, page_lengths, hidden, got, x_coord, line_ids, qkv_w, vectors, tables
    )
    output, first, normed, inverse, act, slope, grad_total2, second_low, sums2 = ffn_forward(
        flat(context), flat(hidden), flat(cotangent), vectors,
        ffn_in_b.reshape(1, FF), out_w, ffn_in_w, ffn_out_w,
    )
    order = Order()
    send, bsum_far, part = order(
        lambda *a: ffn_back_call(False, band_arr, *a, chunks),
        second_low, first, act, slope, ffn_in_w, ffn_out_w, (grad_total2,),
    )
    keep, bsum_own, grad_total1, attn_low, grad_context, sums1 = order(
        lambda *a: ffn_back_call(True, band_arr, *a, chunks),
        second_low, first, act, slope, ffn_in_w, ffn_out_w,
        (part, normed, inverse, vectors, out_w),
    )
    ffn = Halving(order, send, keep, ffn_orders, ffn_plan)
    ffn.step()
    grad_mixed, grad_scores = order(
        attention_backward, probs, queries, pairs, grad_context.reshape(pages, rows, width)
    )
    send, keep, mixed_sums = order(
        product_halves, band_arr, flat(extended), flat(grad_mixed), flat(context), attn_low
    )
    attn = Halving(order, send, keep, attn_orders, attn_plan)
    ffn.step()
    attn.step()
    total = grad_scores.shape[0] * grad_scores.shape[1]
    marks = [0, total // 3, total // 3 + 2, 2 * total // 3, total]

    def tables_of(piece):
        start, stop = marks[piece : piece + 2]
        return order(
            lambda *a: table_sums(band_arr, start, stop - start, *a),
            grad_scores, x_coord, line_ids,
        )

    tables = [tables_of(0)]
    attn.step()
    tables.append(tables_of(1))
    attn.step()
    while ffn.level < len(ffn.sides) - 1:
        ffn.step()
    tables.append(tables_of(2))
    inner_sums = order(
        lambda own, far: jnp.where(
            band == 0,
            jnp.concatenate([own, far], axis=1),
            jnp.concatenate([far, own], axis=1),
        ),
        bsum_own, bsum_far,
    )
    attn.meet()
    tables.append(tables_of(3))
    rider = order(
        lambda m, a, b, c, *t: jnp.pad(
            jnp.concatenate(
                [
                    m[0].reshape(3, width), a[:3], b[:3], c.reshape(FF // width, width),
                    jnp.pad(sum(t[1:], t[0]), ((0, 3), (0, width - t[0].shape[1]))),
                ],
                axis=0,
            ).reshape(7, 4 * width),
            ((0, 1), (0, 0)),
        ),
        mixed_sums, sums1, sums2, inner_sums, *tables,
    )
    levels = len(attn.sides)
    flat_levels = 2 * (levels // 3)
    got = swap_pages(rider, levels - 1, attn.orders)
    attn.met()
    ffn.gather()
    grads = ()

    def hidden_of(page, count):
        return order(
            lambda outs, *a: hidden_backward(page, count, outs, *a),
            grads, grad_mixed, grad_total1.reshape(pages, rows, width), qkv_w,
        )

    for level in reversed(range(flat_levels, levels - 1)):
        rider = order(lambda a, b: a + b, rider, got)
        got = swap_pages(rider, level, attn.orders)
    rider = order(lambda a, b: a + b, rider, got)
    while attn.level > flat_levels:
        attn.grow()
    attn.grow(rider)
    ffn.send_late()
    grads = hidden_of(0, 1)
    while attn.level > 0:
        attn.grow()
    grads = hidden_of(1, pages - 1)
    grad_hidden, far = grads
    far_got = swap_bands(far)
    attn.after(ffn)
    attn.grow()
    ffn_in_share, ffn_out_share = ffn.finish(
        lambda total: (total[0, :, :width].T, total[0, :, width:])
    )
    shapes = ((width, 3 * width), (width, width))
    halves = order(lambda mine: widen(band_arr, mine, True, (), shapes), attn.mine)
    grad_hidden = order(edge_add, band_arr, grad_hidden, far, far_got)
    small = attn.last_rider()
    grad_qkv, grad_out = order(
        lambda other, *outs: widen(band_arr, other, False, outs, shapes), attn.flight, *halves
    )

    def outs_of(small):
        small = small.reshape(-1, width)
        tables = small[13 : 13 + HEADS]
        return (
            small[0], small[2], tables[:, 128:160].T, tables[:, :64].T, tables[:, 64:128].T,
            small[5], small[3], small[4], small[9:13].reshape(FF), small[8], small[6], small[7],
        )

    small_outs = order(outs_of, small)
    (
        grad_q_bias, grad_v_bias, grad_rel, grad_x, grad_y, grad_out_b, grad_ln1_gain,
        grad_ln1_bias, grad_ffn_in_b, grad_ffn_out_b, grad_ln2_gain, grad_ln2_bias,
    ) = small_outs
    return (
        output.reshape(hidden.shape),
        grad_hidden,
        grad_qkv,
        grad_q_bias,
        grad_v_bias,
        grad_rel,
        grad_x,
        grad_y,
        grad_out,
        grad_out_b,
        grad_ln1_gain,
        grad_ln1_bias,
        ffn_in_share,
        grad_ffn_in_b,
        ffn_out_share,
        grad_ffn_out_b,
        grad_ln2_gain,
        grad_ln2_bias,
    )


def solution(mesh):
    in_specs = (
        P("page", "band", None),
        P("page", "band", None),
        P("page"),
        P("page", None),
        P("page", None),
        P(),
        P(),
        P(),
        P(),
        P(),
        P(),
        P(),
        P(),
        P(),
        P(),
        P(),
        P(),
        P(),
        P(),
        P(),
        P(),
    )
    out_specs = (
        P("page", "band", None),
        P("page", "band", None),
        P(),
        P(),
        P(),
        P(),
        P(),
        P(),
        P(),
        P(),
        P(),
        P(),
        P(None, ("band", "page")),
        P(),
        P(("band", "page"), None),
        P(),
        P(),
        P(),
    )
    return jax.shard_map(local, mesh=mesh, in_specs=in_specs, out_specs=out_specs, check_vma=False)
```
